256 devices in a mesh: dp: 32 (over z, x), proto: 8 (over y, core).
Axes of the slice: x: 4, y: 4, z: 8, core: 2. Of those that a mesh axis runs over, the one named last changes fastest.
Arguments:
- centroids: bfloat16 [131072, 768], P(('dp', 'proto')), may hold values from -1 to 1
- queries: bfloat16 [4096, 768], P('dp'), may hold values from -40 to 40
- positive: int32 [4096], P('dp'), may hold values from 0 to 131071
- members: bfloat16 [32, 32, 8, 16, 768], P('dp'), may hold values from -0.29882812 to 0.29882812
- member_slot: int32 [32, 32, 8, 16], P('dp'), may hold values from 0 to 511
- block_count: int32 [32, 32, 8], P('dp'), may hold values from 0 to 16, as said below
Outputs:
- concentration: float32 [131072], P(('dp', 'proto'))
- loss: float32 [4096], P('dp')
- query_grad: bfloat16 [4096, 768], P('dp')
The draws below stay inside these ranges and needn't reach their ends.
Inputs may be any that keep to these rules, and one draw needn't show every extreme that they name: `block_count`: some block is full from every source group; the used slots come first in each block.
All inputs are finite; a program needn't handle non-finite values.
Results may differ from the reference program's by a relative error of at most 0.0056.
Values may be sent and summed in bfloat16 or wider, within the bound.
A program may use at most 128 MiB of HBM per device.

```python
import jax
import jax.numpy as jnp
from jax import lax

D = 768
CENT_DEV = 512
CAP = 16
K = 131072
QUERIES = 4096
N_DP = 32
N_PROTO = 8


def centroid_rows(key, row_ids):
    base = jax.random.fold_in(key, 11)

    def one_row(row):
        row_key = jax.random.fold_in(base, row)
        values = jax.random.normal(row_key, (D,), jnp.float32) * (1.2 / D ** 0.5)
        return jnp.clip(values, -1.0, 1.0)
    return jax.vmap(one_row)(row_ids)


def draw_centroids(key, part):
    return centroid_rows(key, jnp.arange(K, dtype=jnp.int32)).astype(jnp.bfloat16)


def draw_queries(key, part):
    values = jax.random.normal(jax.random.fold_in(key, 23), (QUERIES, D), jnp.float32)
    return jnp.clip(values, -40.0, 40.0).astype(jnp.bfloat16)


def draw_block_count(key, part):
    heat = jax.random.randint(jax.random.fold_in(key, 31), (N_DP, N_PROTO), 0, 4)
    upper = CAP // 2 * (heat + 1) + 1
    counts = jax.random.randint(jax.random.fold_in(key, 37), (N_DP, N_DP, N_PROTO), 0, upper[None, :, :])
    counts = jnp.minimum(counts, CAP)
    full_dp = jax.random.randint(jax.random.fold_in(key, 41), (), 0, N_DP)
    full_proto = jax.random.randint(jax.random.fold_in(key, 43), (), 0, N_PROTO)
    counts = counts.at[:, full_dp, full_proto].set(CAP)
    return counts.astype(jnp.int32)


def set_ends(drawn, own_key, low, largest):
    shape = drawn.shape
    place = [jax.random.randint(jax.random.fold_in(own_key, axis), (), 0, shape[axis]) for axis in range(len(shape))]
    drawn = drawn.at[tuple(place)].set(low)
    longest = shape.index(max(shape))
    place[longest] = (place[longest] + 1) % shape[longest]
    return drawn.at[tuple(place)].set(largest)


def shard_levels(own_key, extent, pieces, smallest, largest):
    def one(position, parts):
        steps = jax.random.uniform(jax.random.fold_in(jax.random.fold_in(own_key, 6), position), (parts,), jnp.float32, smallest / len(pieces), largest / len(pieces))
        return jnp.repeat(jnp.exp(steps), extent[position] // parts).reshape((-1,) + (1,) * (len(extent) - position - 1))

    factor_of = one(*pieces[0])
    for cut in pieces[1:]:
        factor_of = factor_of * one(*cut)
    return factor_of


def noise(rng, extent, deviation, bound, pieces=(), kind=jnp.bfloat16):
    loudness = shard_levels(rng, extent, pieces, -0.22, 0.18) if pieces else 1.0
    result = jax.random.normal(rng, extent, jnp.float32) * deviation * loudness
    return jnp.minimum(jnp.maximum(result, -bound), bound).astype(kind)


def setup_inputs(seed: int = 0) -> dict:
    splits = jax.random.split(jax.random.key(seed), 7)
    return {
        "centroids": draw_centroids(jax.random.fold_in(splits[6], 71), 0),
        "queries": draw_queries(jax.random.fold_in(splits[6], 71), 0),
        "positive": set_ends(jax.random.randint(splits[2], (QUERIES,), 0, K), jax.random.fold_in(splits[2], 1), 0, K - 1).astype(jnp.int32),
        "members": noise(splits[3], (N_DP, N_DP, N_PROTO, CAP, D), 0.0433, 0.29882812, ((0, 32),)),
        "member_slot": set_ends(jax.random.randint(splits[4], (N_DP, N_DP, N_PROTO, CAP), 0, CENT_DEV), jax.random.fold_in(splits[4], 1), 0, CENT_DEV - 1).astype(jnp.int32),
        "block_count": draw_block_count(jax.random.fold_in(splits[6], 71), 0),
    }


def reference(centroids, queries, positive, members, member_slot, block_count):
    owner = jnp.arange(N_DP, dtype=jnp.int32)[:, None] * N_PROTO + jnp.arange(N_PROTO, dtype=jnp.int32)[None, :]
    global_id = (owner[None, :, :, None] * CENT_DEV + member_slot).reshape(-1).astype(jnp.int32)
    valid = (jnp.arange(CAP, dtype=jnp.int32)[None, None, None, :] < block_count[..., None]).astype(jnp.float32).reshape(-1)
    member_rows = members.reshape(-1, D).astype(jnp.float32)
    picked = jnp.take(centroids, global_id, axis=0).astype(jnp.float32)
    distance = jnp.sqrt(lax.optimization_barrier(jnp.sum((member_rows - picked) ** 2, axis=1)) + 1e-06)
    total = jax.ops.segment_sum(distance * valid, global_id, num_segments=K)
    counted = jax.ops.segment_sum(valid, global_id, num_segments=K)
    concentration = (total + 1.0) / ((counted + 1.0) * jnp.log(counted + 10.0))
    inverse = 1.0 / concentration

    def block(pair):
        query_block, positive_block = pair
        scores = lax.dot_general(query_block, centroids, (((1,), (1,)), ((), ())), preferred_element_type=jnp.float32) * inverse[None, :]
        row_max = lax.optimization_barrier(jnp.max(scores, axis=1))
        row_sum = lax.optimization_barrier(jnp.sum(jnp.exp(scores - row_max[:, None]), axis=1))
        positive_hit = (jnp.arange(K, dtype=jnp.int32)[None, :] == positive_block[:, None]).astype(jnp.float32)
        target = lax.optimization_barrier(jnp.sum(scores * positive_hit, axis=1))
        loss_block = row_max + jnp.log(row_sum) - target
        probs = jnp.exp(scores - row_max[:, None]) / row_sum[:, None]
        weight = ((probs - positive_hit) * inverse[None, :]).astype(jnp.bfloat16)
        grad_block = jnp.dot(weight, centroids, preferred_element_type=jnp.float32).astype(jnp.bfloat16)
        return (loss_block, grad_block)
    losses, grads = lax.map(block, (queries.reshape(-1, 128, D), positive.reshape(-1, 128)))
    return (concentration, losses.reshape(-1), grads.reshape(-1, D))
```

```python
import functools

import jax
import jax.numpy as jnp
from jax import lax
from jax.experimental import pallas as pl
from jax.experimental.pallas import tpu as pltpu
from jax.sharding import PartitionSpec as P

MESH = pl.DeviceIdType.MESH
NX, NZ, NP = 4, 8, 8
ROWS, WIDTH, CENT = 16, 768, 512
QS = NX * NZ * ROWS
F32, BF16 = jnp.float32, jnp.bfloat16


def remote(src, dst, send, recv, device):
    return pltpu.make_async_remote_copy(
        src_ref=src, dst_ref=dst, send_sem=send, recv_sem=recv, device_id=device, device_id_type=MESH
    )


def columns_of(rows):
    n = rows.shape[0]
    wide = jnp.broadcast_to(rows, (n, ROWS, 128))
    lane = lax.broadcasted_iota(jnp.int32, (n, ROWS, 128), 2)
    sub = lax.broadcasted_iota(jnp.int32, (n, ROWS, 128), 1)
    return jnp.sum(jnp.where(lane == sub, wide, 0.0), axis=2, keepdims=True).reshape(n * ROWS, 1)


def kernel(
    cent, qry, mem, slot, pos, conc_o, loss_o, grad_o,
    call, qall, pall, mx, mall, slx, sall, invall, score, stats, sxb, szb, colr, posb,
    gsend, grx, hsend, hz, acc, fin, lfin,
    local, mx_s, mx_r, sx_s, sx_r, mz_s, mz_r, sz_s, sz_r, qz_s, qz_r, qx_s, qx_r, pz_s, pz_r, px_s, px_r,
    cy_s, cy_r, cc_s, cc_r, iv_s, iv_r, tx_s, tx_r, tz_s, tz_r, gx_s, gx_r, gz_s, gz_r, fn_s, fn_r, ln_s, ln_r,
):
    dp = lax.axis_index("dp")
    p = lax.axis_index("proto")
    z, x = dp // NX, dp % NX
    y, c = p // 2, p % 2

    def at_x(d):
        return (x + d) % NX

    def at_z(d):
        return (z + d) % NZ

    def at_p(d):
        return (p + d) % NP

    def dev_x(d):
        return {"dp": z * NX + at_x(d), "proto": p}

    def dev_z(d):
        return {"dp": at_z(d) * NX + x, "proto": p}

    def dev_p(q):
        return {"dp": dp, "proto": q}

    barrier = pltpu.get_barrier_semaphore()
    for d in range(1, NX):
        pl.semaphore_signal(barrier, inc=1, device_id=dev_x(d), device_id_type=MESH)
    for d in range(1, NZ):
        pl.semaphore_signal(barrier, inc=1, device_id=dev_z(d), device_id_type=MESH)
    for d in range(1, NP):
        pl.semaphore_signal(barrier, inc=1, device_id=dev_p(at_p(d)), device_id_type=MESH)
    pl.semaphore_wait(barrier, NX + NZ + NP - 3)

    sends = []

    def go(copy):
        copy.start()
        sends.append(copy)

    z_order = (4, 3, 5, 2, 6, 1, 7)
    half = CENT // 2
    top, bottom = pl.ds(0, half), pl.ds(half, half)
    up = ((y + 1) % 4) * 2 + c
    down = ((y + 3) % 4) * 2 + c
    far = ((y + 2) % 4) * 2 + c
    mate = y * 2 + (1 - c)

    for d in z_order:
        go(remote(qry.at[p], qall.at[x, z], qz_s.at[d - 1], qz_r.at[d - 1], dev_z(d)))
        go(remote(pos, pall.at[x, z], pz_s.at[d - 1], pz_r.at[d - 1], dev_z(d)))
    go(remote(cent.at[top], call.at[p, top], cy_s.at[0], cy_r.at[0], dev_p(up)))
    go(remote(cent.at[bottom], call.at[p, bottom], cy_s.at[3], cy_r.at[3], dev_p(down)))
    go(remote(cent.at[bottom], call.at[p, bottom], cy_s.at[1], cy_r.at[1], dev_p(up)))
    go(remote(cent.at[top], call.at[p, top], cy_s.at[2], cy_r.at[2], dev_p(down)))
    go(remote(cent, call.at[p], cc_s.at[0], cc_r.at[0], dev_p(mate)))
    for d in (2, 1, 3):
        go(remote(mem.at[:, at_x(d), p], mx.at[d - 1], mx_s.at[d - 1], mx_r.at[d - 1], dev_x(d)))
        go(remote(slot.at[:, at_x(d)], slx.at[d - 1], sx_s.at[d - 1], sx_r.at[d - 1], dev_x(d)))
    for d in z_order:
        go(remote(mem.at[at_z(d), x, p], mall.at[z, 0], mz_s.at[0, d - 1], mz_r.at[0, d - 1], dev_z(d)))
        go(remote(slot.at[at_z(d), x], sall.at[z, 0], sz_s.at[0, d - 1], sz_r.at[0, d - 1], dev_z(d)))
    own = (
        pltpu.make_async_copy(cent, call.at[p], local.at[0]),
        pltpu.make_async_copy(qry.at[p], qall.at[x, z], local.at[1]),
        pltpu.make_async_copy(mem.at[z, x, p], mall.at[z, 0], local.at[2]),
    )
    for copy in own:
        copy.start()
    pall[x, z] = pos[...]
    sall[z, 0] = slot[z, x]
    own[1].wait()

    for d in range(1, NZ):
        src = at_z(NZ - d)
        remote(qry.at[p], qall.at[x, src], qz_s.at[d - 1], qz_r.at[d - 1], dev_z(d)).wait_recv()
        remote(pos, pall.at[x, src], pz_s.at[d - 1], pz_r.at[d - 1], dev_z(d)).wait_recv()
    for d in (2, 1, 3):
        go(remote(qall.at[x], qall.at[x], qx_s.at[d - 1], qx_r.at[d - 1], dev_x(d)))
        go(remote(pall.at[x], pall.at[x], px_s.at[d - 1], px_r.at[d - 1], dev_x(d)))

    def members_on(d):
        remote(mem.at[:, x, p], mx.at[d - 1], mx_s.at[d - 1], mx_r.at[d - 1], dev_x(d)).wait_recv()
        remote(slot.at[:, x], slx.at[d - 1], sx_s.at[d - 1], sx_r.at[d - 1], dev_x(d)).wait_recv()
        for e in z_order:
            go(remote(mx.at[d - 1, at_z(e)], mall.at[z, d], mz_s.at[d, e - 1], mz_r.at[d, e - 1], dev_z(e)))
            go(remote(slx.at[d - 1, at_z(e)], sall.at[z, d], sz_s.at[d, e - 1], sz_r.at[d, e - 1], dev_z(e)))
        mall[z, d] = mx[d - 1, z]
        sall[z, d] = slx[d - 1, z]

    members_on(1)
    members_on(3)
    remote(cent.at[top], call.at[down, top], cy_s.at[0], cy_r.at[0], dev_p(up)).wait_recv()
    go(remote(call.at[down, top], call.at[down, top], cy_s.at[4], cy_r.at[4], dev_p(up)))
    remote(cent.at[bottom], call.at[up, bottom], cy_s.at[3], cy_r.at[3], dev_p(down)).wait_recv()
    go(remote(call.at[up, bottom], call.at[up, bottom], cy_s.at[5], cy_r.at[5], dev_p(down)))
    members_on(2)

    for d in range(1, NX):
        src = at_x(NX - d)
        remote(qall.at[x], qall.at[src], qx_s.at[d - 1], qx_r.at[d - 1], dev_x(d)).wait_recv()
        remote(pall.at[x], pall.at[src], px_s.at[d - 1], px_r.at[d - 1], dev_x(d)).wait_recv()
    base = (dp * (NP * CENT)).astype(F32)
    posb[...] = jnp.broadcast_to(columns_of(pall[...].reshape(NX * NZ, 1, 128)) - base, (QS, 128))

    def scores(chunk):
        def rows(i, carry):
            r = pl.ds(i * 2, 2)
            q = qall[r].reshape(2 * NZ * ROWS, WIDTH)
            score[chunk, pl.ds(i * 256, 256), :] = lax.dot_general(
                q, call[chunk], (((1,), (1,)), ((), ())), preferred_element_type=F32
            )
            return carry

        lax.fori_loop(0, 2, rows, 0)

    own[0].wait()
    scores(p)
    remote(cent, call.at[mate], cc_s.at[0], cc_r.at[0], dev_p(mate)).wait_recv()
    scores(mate)
    remote(cent.at[bottom], call.at[down, bottom], cy_s.at[1], cy_r.at[1], dev_p(up)).wait_recv()
    go(remote(call.at[down], call.at[down], cc_s.at[1], cc_r.at[1], dev_p(mate)))
    remote(cent.at[top], call.at[up, top], cy_s.at[2], cy_r.at[2], dev_p(down)).wait_recv()
    go(remote(call.at[up], call.at[up], cc_s.at[2], cc_r.at[2], dev_p(mate)))
    flip = 1 - 2 * c
    scores(down)
    scores(up)
    remote(call.at[down], call.at[down + flip], cc_s.at[1], cc_r.at[1], dev_p(mate)).wait_recv()
    scores(down + flip)
    remote(call.at[up], call.at[up + flip], cc_s.at[2], cc_r.at[2], dev_p(mate)).wait_recv()
    scores(up + flip)

    own[2].wait()
    for e in range(1, NZ):
        src = at_z(NZ - e)
        for d in range(NX):
            remote(mem.at[z, x, p], mall.at[src, d], mz_s.at[d, e - 1], mz_r.at[d, e - 1], dev_z(e)).wait_recv()
            remote(slot.at[z, x], sall.at[src, d], sz_s.at[d, e - 1], sz_r.at[d, e - 1], dev_z(e)).wait_recv()
    which = columns_of(sall[...].reshape(NX * NZ, 1, 128))
    cluster = lax.broadcasted_iota(jnp.int32, (QS, CENT), 1).astype(F32)
    hot = which == cluster
    picked = jnp.dot(hot.astype(BF16), call[p], preferred_element_type=F32)
    gap = mall[...].reshape(QS, WIDTH).astype(F32) - picked
    dist = jnp.sqrt(jnp.sum(gap * gap, axis=1, keepdims=True) + 1e-06)
    total = jnp.sum(jnp.where(hot, dist, 0.0), axis=0, keepdims=True)
    count = jnp.sum(hot.astype(F32), axis=0, keepdims=True)
    conc = (total + 1.0) / ((count + 1.0) * jnp.log(count + 10.0))
    conc_o[...] = conc
    invall[p] = 1.0 / conc
    for d in (4, 3, 5, 2, 6, 1, 7):
        go(remote(invall.at[p], invall.at[p], iv_s.at[d - 1], iv_r.at[d - 1], dev_p(at_p(d))))

    remote(call.at[down, top], call.at[far, top], cy_s.at[4], cy_r.at[4], dev_p(up)).wait_recv()
    remote(call.at[up, bottom], call.at[far, bottom], cy_s.at[5], cy_r.at[5], dev_p(down)).wait_recv()
    go(remote(call.at[far], call.at[far], cc_s.at[3], cc_r.at[3], dev_p(mate)))
    scores(far)
    remote(call.at[far], call.at[far + flip], cc_s.at[3], cc_r.at[3], dev_p(mate)).wait_recv()
    scores(far + flip)
    for d in range(1, NP):
        src = at_p(NP - d)
        remote(invall.at[p], invall.at[src], iv_s.at[d - 1], iv_r.at[d - 1], dev_p(src)).wait_recv()

    step = 16
    lane = lax.broadcasted_iota(jnp.int32, (step, 128), 1)

    def soft(i, carry):
        r = pl.ds(pl.multiple_of(i * step, step), step)
        best = None
        for k in range(NP):
            zed = score[k, r, :] * invall[k]
            score[k, r, :] = zed
            best = zed if best is None else jnp.maximum(best, zed)
        top_z = jnp.max(best, axis=1, keepdims=True)
        here = posb[r, 0:1]
        col = lax.broadcasted_iota(jnp.int32, (step, CENT), 1).astype(F32)
        added, hits = None, None
        for k in range(NP):
            zed = score[k, r, :]
            hit = jnp.where(col == here - float(k * CENT), zed, 0.0)
            e = jnp.exp(zed - top_z)
            score[k, r, :] = e
            added = e if added is None else added + e
            hits = hit if hits is None else hits + hit
        summed = jnp.sum(added, axis=1, keepdims=True)
        target = jnp.sum(hits, axis=1, keepdims=True)
        stats[r, :] = jnp.where(lane == 0, top_z, jnp.where(lane == 1, summed, target))
        return carry

    lax.fori_loop(0, QS // step, soft, 0)

    mine = stats[...].T[0:8, :]
    sxb[x] = mine

    def merged(ref, n):
        best = ref[0][0:1, :]
        for k in range(1, n):
            best = jnp.maximum(best, ref[k][0:1, :])
        added, target = None, None
        for k in range(n):
            part = ref[k][1:2, :] * jnp.exp(ref[k][0:1, :] - best)
            added = part if added is None else added + part
            target = ref[k][2:3, :] if target is None else target + ref[k][2:3, :]
        return best, added, target

    for d in (2, 1, 3):
        go(remote(sxb.at[x], sxb.at[x], tx_s.at[d - 1], tx_r.at[d - 1], dev_x(d)))
    for d in range(1, NX):
        src = at_x(NX - d)
        remote(sxb.at[x], sxb.at[src], tx_s.at[d - 1], tx_r.at[d - 1], dev_x(d)).wait_recv()
    best, added, target = merged(sxb, NX)
    szb[z] = jnp.concatenate([best, added, target, jnp.zeros((5, QS), F32)], axis=0)
    for d in z_order:
        go(remote(szb.at[z], szb.at[z], tz_s.at[d - 1], tz_r.at[d - 1], dev_z(d)))
    for d in range(1, NZ):
        src = at_z(NZ - d)
        remote(szb.at[z], szb.at[src], tz_s.at[d - 1], tz_r.at[d - 1], dev_z(d)).wait_recv()
    best, added, target = merged(szb, NZ)
    share = jnp.exp(mine[0:1, :] - best) / added
    loss = best + jnp.log(added) - target
    colr[...] = jnp.concatenate([share, loss, jnp.zeros((126, QS), F32)], axis=0).T

    def part(block):
        rows = pl.ds(pl.multiple_of(block * (NZ * ROWS), NZ * ROWS), NZ * ROWS)
        scale = colr[rows, 0:1]
        here = posb[rows, 0:1]
        col = lax.broadcasted_iota(jnp.int32, (NZ * ROWS, CENT), 1).astype(F32)
        acc[...] = jnp.zeros_like(acc)

        def add(k, carry):
            hit = (col == here - (k * CENT).astype(F32)).astype(F32)
            w = ((score[k, rows, :] * scale - hit) * invall[k]).astype(BF16)
            acc[...] += jnp.dot(w, call[k], preferred_element_type=F32)
            return carry

        lax.fori_loop(0, NP, add, 0)

    for d in (2, 1, 3):
        part(at_x(d))
        gsend[d - 1] = acc[...].astype(BF16).reshape(NZ, ROWS, WIDTH)
        go(remote(gsend.at[d - 1], grx.at[d - 1], gx_s.at[d - 1], gx_r.at[d - 1], dev_x(d)))
    part(x)
    for d in (1, 3, 2):
        remote(gsend.at[d - 1], grx.at[d - 1], gx_s.at[d - 1], gx_r.at[d - 1], dev_x(d)).wait_recv()
    summed = acc[...] + (
        grx[0].reshape(NZ * ROWS, WIDTH).astype(F32)
        + grx[1].reshape(NZ * ROWS, WIDTH).astype(F32)
        + grx[2].reshape(NZ * ROWS, WIDTH).astype(F32)
    )
    acc[...] = summed
    hsend[...] = summed.astype(BF16).reshape(NZ, ROWS, WIDTH)
    for d in z_order:
        go(remote(hsend.at[at_z(d)], hz.at[d - 1], gz_s.at[d - 1], gz_r.at[d - 1], dev_z(d)))
    grad = acc[pl.ds(pl.multiple_of(z * ROWS, ROWS), ROWS), :]
    for d in range(1, NZ):
        remote(hsend.at[z], hz.at[d - 1], gz_s.at[d - 1], gz_r.at[d - 1], dev_z(d)).wait_recv()
        grad = grad + hz[d - 1].astype(F32)

    fin[p] = grad.astype(BF16)
    lfin[p] = colr[pl.ds(pl.multiple_of((x * NZ + z) * ROWS, ROWS), ROWS), :]
    for d in (4, 3, 5, 2, 6, 1, 7):
        go(remote(fin.at[p], fin.at[p], fn_s.at[d - 1], fn_r.at[d - 1], dev_p(at_p(d))))
        go(remote(lfin.at[p], lfin.at[p], ln_s.at[d - 1], ln_r.at[d - 1], dev_p(at_p(d))))
    for d in range(1, NP):
        src = at_p(NP - d)
        remote(fin.at[p], fin.at[src], fn_s.at[d - 1], fn_r.at[d - 1], dev_p(src)).wait_recv()
        remote(lfin.at[p], lfin.at[src], ln_s.at[d - 1], ln_r.at[d - 1], dev_p(src)).wait_recv()
    grad_o[...] = fin[...].reshape(NP * ROWS, WIDTH)
    loss_o[...] = lfin[...].reshape(NP * ROWS, 128).T[1:2, :]
    for copy in sends:
        copy.wait_send()


def on_device(centroids, queries, positive, members, member_slot, block_count):
    column = lax.axis_index("proto")
    slot_mine = lax.dynamic_index_in_dim(member_slot[0], column, 1, keepdims=False)
    count_mine = lax.dynamic_index_in_dim(block_count[0], column, 1, keepdims=False)
    used = jnp.arange(ROWS, dtype=jnp.int32)[None, :] < count_mine[:, None]
    slot = jnp.where(used, slot_mine, -1).astype(F32)
    slot = jnp.pad(slot, ((0, 0), (0, 128 - ROWS))).reshape(NZ, NX, 1, 128)
    pos = lax.dynamic_slice_in_dim(positive, column * ROWS, ROWS).astype(F32)
    pos = jnp.pad(pos, (0, 128 - ROWS)).reshape(1, 128)
    vmem = pltpu.VMEM
    dma = pltpu.SemaphoreType.DMA
    sems = []
    for shape in (
        (NX - 1,), (NX - 1,), (NX, NZ - 1), (NX, NZ - 1), (NZ - 1,), (NX - 1,), (NZ - 1,), (NX - 1,),
        (6,), (4,), (NP - 1,), (NX - 1,), (NZ - 1,), (NX - 1,), (NZ - 1,), (NP - 1,), (NP - 1,),
    ):
        sems += [dma(shape), dma(shape)]
    conc, loss, grad = pl.pallas_call(
        kernel,
        out_shape=(
            jax.ShapeDtypeStruct((1, CENT), F32),
            jax.ShapeDtypeStruct((1, NP * ROWS), F32),
            jax.ShapeDtypeStruct((NP * ROWS, WIDTH), BF16),
        ),
        in_specs=[pl.BlockSpec(memory_space=pl.ANY)] * 3 + [pl.BlockSpec(memory_space=vmem)] * 2,
        out_specs=(pl.BlockSpec(memory_space=vmem),) * 3,
        scratch_shapes=[
            vmem((NP, CENT, WIDTH), BF16),
            vmem((NX, NZ, ROWS, WIDTH), BF16),
            vmem((NX, NZ, 1, 128), F32),
            vmem((NX - 1, NZ, ROWS, WIDTH), BF16),
            vmem((NZ, NX, ROWS, WIDTH), BF16),
            vmem((NX - 1, NZ, 1, 128), F32),
            vmem((NZ, NX, 1, 128), F32),
            vmem((NP, 1, CENT), F32),
            vmem((NP, QS, CENT), F32),
            vmem((QS, 128), F32),
            vmem((NX, 8, QS), F32),
            vmem((NZ, 8, QS), F32),
            vmem((QS, 128), F32),
            vmem((QS, 128), F32),
            vmem((NX - 1, NZ, ROWS, WIDTH), BF16),
            vmem((NX - 1, NZ, ROWS, WIDTH), BF16),
            vmem((NZ, ROWS, WIDTH), BF16),
            vmem((NZ - 1, ROWS, WIDTH), BF16),
            vmem((NZ * ROWS, WIDTH), F32),
            vmem((NP, ROWS, WIDTH), BF16),
            vmem((NP, ROWS, 128), F32),
            dma((3,)),
            *sems,
        ],
        compiler_params=pltpu.CompilerParams(
            collective_id=0, has_side_effects=True, vmem_limit_bytes=56 * 1024 * 1024
        ),
        name="protonce",
    )(
        centroids,
        queries.reshape(NP, ROWS, WIDTH),
        members.reshape(NZ, NX, NP, ROWS, WIDTH),
        slot,
        pos,
    )
    return conc.reshape(CENT), loss.reshape(NP * ROWS), grad


def solution(mesh):
    placed = (
        P(("dp", "proto"), None),
        P("dp", None),
        P("dp"),
        P("dp", None, None, None, None),
        P("dp", None, None, None),
        P("dp", None, None),
    )
    return jax.shard_map(
        on_device,
        mesh=mesh,
        in_specs=placed,
        out_specs=(P(("dp", "proto")), P("dp"), P("dp", None)),
        check_vma=False,
    )
```

```python
import jax
import jax.numpy as jnp
from jax import lax
from jax.experimental import pallas as pl
from jax.experimental.pallas import tpu as pltpu
from jax.sharding import PartitionSpec as P

MESH = pl.DeviceIdType.MESH
NX, NZ, NP = 4, 8, 8
ROWS, WIDTH, CENT = 16, 768, 512
QS = NX * NZ * ROWS
F32, BF16 = jnp.float32, jnp.bfloat16
LOG2E, LN2 = 1.4426950408889634, 0.6931471805599453


def remote(src, dst, send, recv, device):
    return pltpu.make_async_remote_copy(
        src_ref=src, dst_ref=dst, send_sem=send, recv_sem=recv, device_id=device, device_id_type=MESH
    )


def columns_of(rows):
    n = rows.shape[0]
    wide = jnp.broadcast_to(rows, (n, ROWS, 128))
    lane = lax.broadcasted_iota(jnp.int32, (n, ROWS, 128), 2)
    sub = lax.broadcasted_iota(jnp.int32, (n, ROWS, 128), 1)
    return jnp.sum(jnp.where(lane == sub, wide, 0.0), axis=2, keepdims=True).reshape(n * ROWS, 1)


def kernel(
    cent, qry, mem, slot_in, count_in, pos_in, conc_o, lfin, fin,
    call, qall, pall, mx, mall, slx, sall, invall, score, wgt, peak, sums, sxb, szb, colr, posb, posw,
    gsum, psum, slot, pos, tsend, trx, thz, tsum, gsend, grx, hsend, hz, acc,
    local, mx_s, mx_r, sx_s, sx_r, mz_s, mz_r, sz_s, sz_r, qz_s, qz_r, qx_s, qx_r, pz_s, pz_r, px_s, px_r,
    cy_s, cy_r, cc_s, cc_r, iv_s, iv_r, tx_s, tx_r, tz_s, tz_r, gx_s, gx_r, gz_s, gz_r, fn_s, fn_r, ln_s, ln_r,
    ux_s, ux_r, uz_s, uz_r,
):
    dp = lax.axis_index("dp")
    p = lax.axis_index("proto")
    z, x = dp // NX, dp % NX
    y, c = p // 2, p % 2

    def at_x(d):
        return (x + d) % NX

    def at_z(d):
        return (z + d) % NZ

    def at_p(d):
        return (p + d) % NP

    def dev_x(d):
        return {"dp": z * NX + at_x(d), "proto": p}

    def dev_z(d):
        return {"dp": at_z(d) * NX + x, "proto": p}

    def dev_p(q):
        return {"dp": dp, "proto": q}

    barrier = pltpu.get_barrier_semaphore()
    for d in range(1, NX):
        pl.semaphore_signal(barrier, inc=1, device_id=dev_x(d), device_id_type=MESH)
    for d in range(1, NZ):
        pl.semaphore_signal(barrier, inc=1, device_id=dev_z(d), device_id_type=MESH)
    for d in range(1, NP):
        pl.semaphore_signal(barrier, inc=1, device_id=dev_p(at_p(d)), device_id_type=MESH)

    used = lax.broadcasted_iota(jnp.int32, (ROWS, NX * NZ), 0) < count_in[pl.ds(p, 1), :]
    ids = jnp.where(used, slot_in[p], -1).astype(F32)
    ids = jnp.concatenate([ids, jnp.zeros((ROWS, 128 - NX * NZ), F32)], axis=1)
    ids = jnp.concatenate([ids, jnp.zeros((128 - ROWS, 128), F32)], axis=0).T
    for i in range(NX * NZ):
        slot[i // NX, i % NX] = ids[i : i + 1, :]
    wide = jnp.broadcast_to(pos_in[...].astype(F32), (8, 128))
    pos[...] = pltpu.roll(wide, (128 - p * ROWS) % 128, 1)[0:1, :]

    pl.semaphore_wait(barrier, NX + NZ + NP - 3)

    sends = []

    def go(copy):
        copy.start()
        sends.append(copy)

    z_order = (4, 3, 5, 2, 6, 1, 7)
    half = CENT // 2
    top, bottom = pl.ds(0, half), pl.ds(half, half)
    up = ((y + 1) % 4) * 2 + c
    down = ((y + 3) % 4) * 2 + c
    far = ((y + 2) % 4) * 2 + c
    mate = y * 2 + (1 - c)

    for d in z_order:
        go(remote(pos, pall.at[x, z], pz_s.at[d - 1], pz_r.at[d - 1], dev_z(d)))
    for d in z_order:
        go(remote(qry.at[p], qall.at[x, z], qz_s.at[d - 1], qz_r.at[d - 1], dev_z(d)))
    go(remote(cent.at[top], call.at[p, top], cy_s.at[0], cy_r.at[0], dev_p(up)))
    go(remote(cent.at[bottom], call.at[p, bottom], cy_s.at[3], cy_r.at[3], dev_p(down)))
    go(remote(cent.at[bottom], call.at[p, bottom], cy_s.at[1], cy_r.at[1], dev_p(up)))
    go(remote(cent.at[top], call.at[p, top], cy_s.at[2], cy_r.at[2], dev_p(down)))
    go(remote(cent, call.at[p], cc_s.at[0], cc_r.at[0], dev_p(mate)))
    for d in (2, 1, 3):
        go(remote(mem.at[:, at_x(d), p], mx.at[d - 1], mx_s.at[d - 1], mx_r.at[d - 1], dev_x(d)))
        go(remote(slot.at[:, at_x(d)], slx.at[d - 1], sx_s.at[d - 1], sx_r.at[d - 1], dev_x(d)))
    for d in z_order:
        go(remote(mem.at[at_z(d), x, p], mall.at[z, 0], mz_s.at[0, d - 1], mz_r.at[0, d - 1], dev_z(d)))
        go(remote(slot.at[at_z(d), x], sall.at[z, 0], sz_s.at[0, d - 1], sz_r.at[0, d - 1], dev_z(d)))
    own = (
        pltpu.make_async_copy(cent, call.at[p], local.at[0]),
        pltpu.make_async_copy(qry.at[p], qall.at[x, z], local.at[1]),
        pltpu.make_async_copy(mem.at[z, x, p], mall.at[z, 0], local.at[2]),
    )
    for copy in own:
        copy.start()
    pall[x, z] = pos[...]
    sall[z, 0] = slot[z, x]
    psum[...] = jnp.zeros_like(psum)

    for d in range(1, NZ):
        src = at_z(NZ - d)
        remote(pos, pall.at[x, src], pz_s.at[d - 1], pz_r.at[d - 1], dev_z(d)).wait_recv()
    for d in (2, 1, 3):
        go(remote(pall.at[x], pall.at[x], px_s.at[d - 1], px_r.at[d - 1], dev_x(d)))
    own[1].wait()
    for d in range(1, NZ):
        src = at_z(NZ - d)
        remote(qry.at[p], qall.at[x, src], qz_s.at[d - 1], qz_r.at[d - 1], dev_z(d)).wait_recv()
    for d in (2, 1, 3):
        go(remote(qall.at[x], qall.at[x], qx_s.at[d - 1], qx_r.at[d - 1], dev_x(d)))

    def members_on(d):
        remote(mem.at[:, x, p], mx.at[d - 1], mx_s.at[d - 1], mx_r.at[d - 1], dev_x(d)).wait_recv()
        remote(slot.at[:, x], slx.at[d - 1], sx_s.at[d - 1], sx_r.at[d - 1], dev_x(d)).wait_recv()
        for e in z_order:
            go(remote(mx.at[d - 1, at_z(e)], mall.at[z, d], mz_s.at[d, e - 1], mz_r.at[d, e - 1], dev_z(e)))
            go(remote(slx.at[d - 1, at_z(e)], sall.at[z, d], sz_s.at[d, e - 1], sz_r.at[d, e - 1], dev_z(e)))
        mall[z, d] = mx[d - 1, z]
        sall[z, d] = slx[d - 1, z]

    members_on(1)
    members_on(3)
    remote(cent.at[top], call.at[down, top], cy_s.at[0], cy_r.at[0], dev_p(up)).wait_recv()
    go(remote(call.at[down, top], call.at[down, top], cy_s.at[4], cy_r.at[4], dev_p(up)))
    remote(cent.at[bottom], call.at[up, bottom], cy_s.at[3], cy_r.at[3], dev_p(down)).wait_recv()
    go(remote(call.at[up, bottom], call.at[up, bottom], cy_s.at[5], cy_r.at[5], dev_p(down)))
    go(remote(call.at[down, top], call.at[down, top], cc_s.at[1], cc_r.at[1], dev_p(mate)))
    go(remote(call.at[up, bottom], call.at[up, bottom], cc_s.at[2], cc_r.at[2], dev_p(mate)))
    members_on(2)

    for d in range(1, NX):
        src = at_x(NX - d)
        remote(pall.at[x], pall.at[src], px_s.at[d - 1], px_r.at[d - 1], dev_x(d)).wait_recv()
    base = (dp * (NP * CENT)).astype(F32)
    posb[...] = jnp.broadcast_to(columns_of(pall[...].reshape(NX * NZ, 1, 128)) - base, (QS, 128))

    def positives(chunk):
        here = posb[:, 0:1] - (chunk * CENT).astype(F32)
        hot = lax.broadcasted_iota(jnp.int32, (QS, CENT), 1).astype(F32) == here
        psum[...] += jnp.dot(hot.astype(BF16), call[chunk], preferred_element_type=F32)

    def scores(chunk):
        def rows(i, carry):
            r = pl.ds(i * 2, 2)
            q = qall[r].reshape(2 * NZ * ROWS, WIDTH)
            score[chunk, pl.ds(i * 256, 256), :] = lax.dot_general(
                q, call[chunk], (((1,), (1,)), ((), ())), preferred_element_type=F32
            )
            return carry

        lax.fori_loop(0, 2, rows, 0)

    own[0].wait()
    positives(p)
    remote(cent, call.at[mate], cc_s.at[0], cc_r.at[0], dev_p(mate)).wait_recv()
    positives(mate)
    for d in range(1, NX):
        src = at_x(NX - d)
        remote(qall.at[x], qall.at[src], qx_s.at[d - 1], qx_r.at[d - 1], dev_x(d)).wait_recv()
    scores(p)
    scores(mate)
    remote(cent.at[bottom], call.at[down, bottom], cy_s.at[1], cy_r.at[1], dev_p(up)).wait_recv()
    go(remote(call.at[down, bottom], call.at[down, bottom], cc_s.at[3], cc_r.at[3], dev_p(mate)))
    remote(cent.at[top], call.at[up, top], cy_s.at[2], cy_r.at[2], dev_p(down)).wait_recv()
    go(remote(call.at[up, top], call.at[up, top], cc_s.at[4], cc_r.at[4], dev_p(mate)))
    flip = 1 - 2 * c
    scores(down)
    scores(up)
    remote(call.at[down, top], call.at[down + flip, top], cc_s.at[1], cc_r.at[1], dev_p(mate)).wait_recv()
    remote(call.at[down, bottom], call.at[down + flip, bottom], cc_s.at[3], cc_r.at[3], dev_p(mate)).wait_recv()
    scores(down + flip)
    remote(call.at[up, bottom], call.at[up + flip, bottom], cc_s.at[2], cc_r.at[2], dev_p(mate)).wait_recv()
    remote(call.at[up, top], call.at[up + flip, top], cc_s.at[4], cc_r.at[4], dev_p(mate)).wait_recv()
    scores(up + flip)

    own[2].wait()
    for e in range(1, NZ):
        src = at_z(NZ - e)
        for d in range(NX):
            remote(mem.at[z, x, p], mall.at[src, d], mz_s.at[d, e - 1], mz_r.at[d, e - 1], dev_z(e)).wait_recv()
            remote(slot.at[z, x], sall.at[src, d], sz_s.at[d, e - 1], sz_r.at[d, e - 1], dev_z(e)).wait_recv()
    which = columns_of(sall[...].reshape(NX * NZ, 1, 128))
    cluster = lax.broadcasted_iota(jnp.int32, (QS, CENT), 1).astype(F32)
    hot = which == cluster
    picked = jnp.dot(hot.astype(BF16), call[p], preferred_element_type=F32)
    gap = mall[...].reshape(QS, WIDTH).astype(F32) - picked
    dist = jnp.sqrt(jnp.sum(gap * gap, axis=1, keepdims=True) + 1e-06)
    total = jnp.sum(jnp.where(hot, dist, 0.0), axis=0, keepdims=True)
    count = jnp.sum(hot.astype(F32), axis=0, keepdims=True)
    conc = (total + 1.0) / ((count + 1.0) * jnp.log(count + 10.0))
    conc_o[...] = conc
    invall[p] = 1.0 / conc
    for d in (4, 3, 5, 2, 6, 1, 7):
        go(remote(invall.at[p], invall.at[p], iv_s.at[d - 1], iv_r.at[d - 1], dev_p(at_p(d))))

    positives(down)
    remote(call.at[down, top], call.at[far, top], cy_s.at[4], cy_r.at[4], dev_p(up)).wait_recv()
    go(remote(call.at[far, top], call.at[far, top], cc_s.at[5], cc_r.at[5], dev_p(mate)))
    remote(call.at[up, bottom], call.at[far, bottom], cy_s.at[5], cy_r.at[5], dev_p(down)).wait_recv()
    go(remote(call.at[far, bottom], call.at[far, bottom], cc_s.at[6], cc_r.at[6], dev_p(mate)))
    scores(far)
    remote(call.at[far, top], call.at[far + flip, top], cc_s.at[5], cc_r.at[5], dev_p(mate)).wait_recv()
    remote(call.at[far, bottom], call.at[far + flip, bottom], cc_s.at[6], cc_r.at[6], dev_p(mate)).wait_recv()
    scores(far + flip)
    for d in range(1, NP):
        src = at_p(NP - d)
        remote(invall.at[p], invall.at[src], iv_s.at[d - 1], iv_r.at[d - 1], dev_p(src)).wait_recv()

    step = 16

    def fold(v, op):
        return op(op(v[:, 0:128], v[:, 128:256]), op(v[:, 256:384], v[:, 384:512]))

    def largest(i, carry):
        r = pl.ds(pl.multiple_of(i * step, step), step)
        best = None
        for k in range(NP):
            zed = score[k, r, :] * (invall[k] * LOG2E)
            best = zed if best is None else jnp.maximum(best, zed)
        peak[r, :] = fold(best, jnp.maximum)
        return carry

    lax.fori_loop(0, QS // step, largest, 0)
    peak[...] = jnp.broadcast_to(jnp.max(peak[...], axis=1, keepdims=True), (QS, 128))

    def soft(i, carry):
        r = pl.ds(pl.multiple_of(i * step, step), step)
        most = jnp.concatenate([peak[r, :]] * 4, axis=1)
        added = None
        for k in range(NP):
            e = jnp.exp2(score[k, r, :] * (invall[k] * LOG2E) - most)
            wgt[k, r, :] = (e * invall[k]).astype(BF16)
            added = e if added is None else added + e
        sums[r, :] = fold(added, jnp.add)
        return carry

    lax.fori_loop(0, QS // step, soft, 0)

    lane = lax.broadcasted_iota(jnp.int32, (QS, 128), 1)
    mine = jnp.where(lane == 0, peak[...], jnp.sum(sums[...], axis=1, keepdims=True)).T[0:8, :]
    sxb[x] = mine

    def merged(ref, n):
        best = ref[0][0:1, :]
        for k in range(1, n):
            best = jnp.maximum(best, ref[k][0:1, :])
        added = None
        for k in range(n):
            part = ref[k][1:2, :] * jnp.exp2(ref[k][0:1, :] - best)
            added = part if added is None else added + part
        return best, added

    for d in (2, 1, 3):
        go(remote(sxb.at[x], sxb.at[x], tx_s.at[d - 1], tx_r.at[d - 1], dev_x(d)))

    def weigh(i, carry):
        r = pl.ds(pl.multiple_of(i * 256, 256), 256)
        out = None
        for k in range(NP):
            term = jnp.dot(wgt[k, r, :], call[k], preferred_element_type=F32)
            out = term if out is None else out + term
        gsum[r, :] = out
        return carry

    lax.fori_loop(0, 2, weigh, 0)

    for d in range(1, NX):
        src = at_x(NX - d)
        remote(sxb.at[x], sxb.at[src], tx_s.at[d - 1], tx_r.at[d - 1], dev_x(d)).wait_recv()
    best, added = merged(sxb, NX)
    szb[z] = jnp.concatenate([best, added, jnp.zeros((6, QS), F32)], axis=0)
    for d in z_order:
        go(remote(szb.at[z], szb.at[z], tz_s.at[d - 1], tz_r.at[d - 1], dev_z(d)))

    def hits(i, carry):
        r = pl.ds(pl.multiple_of(i * step, step), step)
        here = jnp.concatenate([posb[r, :]] * 4, axis=1)
        col = lax.broadcasted_iota(jnp.int32, (step, CENT), 1).astype(F32)
        weight, logit = None, None
        for k in range(NP):
            hit = col + float(k * CENT) == here
            a = jnp.where(hit, jnp.broadcast_to(invall[k], (step, CENT)), 0.0)
            b = jnp.where(hit, score[k, r, :], 0.0)
            weight = a if weight is None else weight + a
            logit = b if logit is None else logit + b
        posw[r, :] = fold(weight, jnp.add)
        colr[r, :] = fold(logit, jnp.add)
        return carry

    lax.fori_loop(0, QS // step, hits, 0)
    scale = jnp.sum(posw[...], axis=1, keepdims=True)
    target = jnp.sum(colr[...], axis=1, keepdims=True) * scale
    posw[...] = jnp.broadcast_to(scale, (QS, 128))
    turned = jnp.broadcast_to(target, (QS, 128)).T[0:8, :]
    for b in range(NX):
        tsend[b] = turned[:, b * 128 : (b + 1) * 128]
    positives(up)
    positives(down + flip)
    positives(up + flip)
    positives(far)
    positives(far + flip)

    for d in range(1, NZ):
        src = at_z(NZ - d)
        remote(szb.at[z], szb.at[src], tz_s.at[d - 1], tz_r.at[d - 1], dev_z(d)).wait_recv()
    best, added = merged(szb, NZ)
    share = jnp.exp2(mine[0:1, :] - best) / added
    total_log = best * LN2 + jnp.log(added)
    colr[...] = jnp.concatenate([share, total_log, jnp.zeros((126, QS), F32)], axis=0).T

    def part(block):
        rows = pl.ds(pl.multiple_of(block * (NZ * ROWS), NZ * ROWS), NZ * ROWS)
        return gsum[rows, :] * colr[rows, 0:1] - psum[rows, :] * posw[rows, 0:1]

    for d in (2, 1, 3):
        gsend[d - 1] = part(at_x(d)).astype(BF16).reshape(NZ, ROWS, WIDTH)
        go(remote(gsend.at[d - 1], grx.at[d - 1], gx_s.at[d - 1], gx_r.at[d - 1], dev_x(d)))
        go(remote(tsend.at[at_x(d)], trx.at[d - 1], ux_s.at[d - 1], ux_r.at[d - 1], dev_x(d)))
    acc[...] = part(x)
    told = tsend[x]
    for d in (1, 3, 2):
        remote(tsend.at[x], trx.at[d - 1], ux_s.at[d - 1], ux_r.at[d - 1], dev_x(d)).wait_recv()
        told = told + trx[d - 1]
    tsum[...] = told
    for d in z_order:
        go(remote(tsum, thz.at[d - 1], uz_s.at[d - 1], uz_r.at[d - 1], dev_z(d)))
    for d in (1, 3, 2):
        remote(gsend.at[d - 1], grx.at[d - 1], gx_s.at[d - 1], gx_r.at[d - 1], dev_x(d)).wait_recv()
    summed = acc[...] + (
        grx[0].reshape(NZ * ROWS, WIDTH).astype(F32)
        + grx[1].reshape(NZ * ROWS, WIDTH).astype(F32)
        + grx[2].reshape(NZ * ROWS, WIDTH).astype(F32)
    )
    acc[...] = summed
    hsend[...] = summed.astype(BF16).reshape(NZ, ROWS, WIDTH)
    for d in z_order:
        go(remote(hsend.at[at_z(d)], hz.at[d - 1], gz_s.at[d - 1], gz_r.at[d - 1], dev_z(d)))
    for d in range(1, NZ):
        remote(tsum, thz.at[d - 1], uz_s.at[d - 1], uz_r.at[d - 1], dev_z(d)).wait_recv()
        told = told + thz[d - 1]
    peak[0:128, :] = jnp.concatenate([told, jnp.zeros((120, 128), F32)], axis=0).T
    mine_rows = pl.ds(pl.multiple_of((x * NZ + z) * ROWS, ROWS), ROWS)
    z_rows = pl.ds(pl.multiple_of(z * ROWS, ROWS), ROWS)
    lfin[p] = jnp.broadcast_to(colr[mine_rows, 1:2] - peak[z_rows, 0:1], (ROWS, 128))
    for d in (4, 3, 5, 2, 6, 1, 7):
        go(remote(lfin.at[p], lfin.at[p], ln_s.at[d - 1], ln_r.at[d - 1], dev_p(at_p(d))))
    grad = acc[z_rows, :]
    for d in range(1, NZ):
        remote(hsend.at[z], hz.at[d - 1], gz_s.at[d - 1], gz_r.at[d - 1], dev_z(d)).wait_recv()
        grad = grad + hz[d - 1].astype(F32)

    fin[p] = grad.astype(BF16)
    for d in (4, 3, 5, 2, 6, 1, 7):
        go(remote(fin.at[p], fin.at[p], fn_s.at[d - 1], fn_r.at[d - 1], dev_p(at_p(d))))
    for d in range(1, NP):
        src = at_p(NP - d)
        remote(lfin.at[p], lfin.at[src], ln_s.at[d - 1], ln_r.at[d - 1], dev_p(src)).wait_recv()
        remote(fin.at[p], fin.at[src], fn_s.at[d - 1], fn_r.at[d - 1], dev_p(src)).wait_recv()
    for copy in sends:
        copy.wait_send()


def finish(conc, lfin, fin, conc_o, loss_o, grad_o):
    conc_o[...] = conc[...]
    loss_o[...] = lfin[...].reshape(NP * ROWS, 128).T[0:1, :]
    grad_o[...] = fin[...].reshape(NP * ROWS, WIDTH)


def on_device(centroids, queries, positive, members, member_slot, block_count):
    vmem = pltpu.VMEM
    dma = pltpu.SemaphoreType.DMA
    sems = []
    for shape in (
        (NX - 1,), (NX - 1,), (NX, NZ - 1), (NX, NZ - 1), (NZ - 1,), (NX - 1,), (NZ - 1,), (NX - 1,),
        (6,), (7,), (NP - 1,), (NX - 1,), (NZ - 1,), (NX - 1,), (NZ - 1,), (NP - 1,), (NP - 1,),
        (NX - 1,), (NZ - 1,),
    ):
        sems += [dma(shape), dma(shape)]
    whole = pl.BlockSpec(memory_space=vmem)
    conc, lfin, fin = pl.pallas_call(
        kernel,
        out_shape=(
            jax.ShapeDtypeStruct((1, CENT), F32),
            jax.ShapeDtypeStruct((NP, ROWS, 128), F32),
            jax.ShapeDtypeStruct((NP, ROWS, WIDTH), BF16),
        ),
        in_specs=[pl.BlockSpec(memory_space=pl.ANY)] * 3 + [whole] * 3,
        out_specs=(whole,) * 3,
        scratch_shapes=[
            vmem((NP, CENT, WIDTH), BF16),
            vmem((NX, NZ, ROWS, WIDTH), BF16),
            vmem((NX, NZ, 1, 128), F32),
            vmem((NX - 1, NZ, ROWS, WIDTH), BF16),
            vmem((NZ, NX, ROWS, WIDTH), BF16),
            vmem((NX - 1, NZ, 1, 128), F32),
            vmem((NZ, NX, 1, 128), F32),
            vmem((NP, 1, CENT), F32),
            vmem((NP, QS, CENT), F32),
            vmem((NP, QS, CENT), BF16),
            vmem((QS, 128), F32),
            vmem((QS, 128), F32),
            vmem((NX, 8, QS), F32),
            vmem((NZ, 8, QS), F32),
            vmem((QS, 128), F32),
            vmem((QS, 128), F32),
            vmem((QS, 128), F32),
            vmem((QS, WIDTH), F32),
            vmem((QS, WIDTH), F32),
            vmem((NZ, NX, 1, 128), F32),
            vmem((1, 128), F32),
            vmem((NX, 8, 128), F32),
            vmem((NX - 1, 8, 128), F32),
            vmem((NZ - 1, 8, 128), F32),
            vmem((8, 128), F32),
            vmem((NX - 1, NZ, ROWS, WIDTH), BF16),
            vmem((NX - 1, NZ, ROWS, WIDTH), BF16),
            vmem((NZ, ROWS, WIDTH), BF16),
            vmem((NZ - 1, ROWS, WIDTH), BF16),
            vmem((NZ * ROWS, WIDTH), F32),
            dma((3,)),
            *sems,
        ],
        compiler_params=pltpu.CompilerParams(
            collective_id=0, has_side_effects=True, vmem_limit_bytes=56 * 1024 * 1024
        ),
        name="protonce",
    )(
        centroids,
        queries.reshape(NP, ROWS, WIDTH),
        members.reshape(NZ, NX, NP, ROWS, WIDTH),
        member_slot.transpose(0, 2, 3, 1).reshape(NP, ROWS, NX * NZ),
        block_count.transpose(0, 2, 1).reshape(NP, NX * NZ),
        positive.reshape(1, NP * ROWS),
    )
    conc, loss, grad = pl.pallas_call(
        finish,
        out_shape=(
            jax.ShapeDtypeStruct((1, CENT), F32),
            jax.ShapeDtypeStruct((1, NP * ROWS), F32),
            jax.ShapeDtypeStruct((NP * ROWS, WIDTH), BF16),
        ),
        in_specs=[whole] * 3,
        out_specs=(whole,) * 3,
        name="finish",
    )(conc, lfin, fin)
    return conc.reshape(CENT), loss.reshape(NP * ROWS), grad


def solution(mesh):
    placed = (
        P(("dp", "proto"), None),
        P("dp", None),
        P("dp"),
        P("dp", None, None, None, None),
        P("dp", None, None, None),
        P("dp", None, None),
    )
    return jax.shard_map(
        on_device,
        mesh=mesh,
        in_specs=placed,
        out_specs=(P(("dp", "proto")), P("dp"), P("dp", None)),
        check_vma=False,
    )
```

```python
import jax
import jax.numpy as jnp
from jax import lax
from jax.experimental import pallas as pl
from jax.experimental.pallas import tpu as pltpu
from jax.sharding import PartitionSpec as P

MESH = pl.DeviceIdType.MESH
NX, NZ, NP = 4, 8, 8
ROWS, WIDTH, CENT = 16, 768, 512
QS = NX * NZ * ROWS
CA = 512
CB = WIDTH - CA
F32, BF16 = jnp.float32, jnp.bfloat16
LOG2E, LN2 = 1.4426950408889634, 0.6931471805599453


def remote(src, dst, send, recv, device):
    return pltpu.make_async_remote_copy(
        src_ref=src, dst_ref=dst, send_sem=send, recv_sem=recv, device_id=device, device_id_type=MESH
    )


def columns_of(rows):
    n = rows.shape[0]
    wide = jnp.broadcast_to(rows, (n, ROWS, 128))
    lane = lax.broadcasted_iota(jnp.int32, (n, ROWS, 128), 2)
    sub = lax.broadcasted_iota(jnp.int32, (n, ROWS, 128), 1)
    return jnp.sum(jnp.where(lane == sub, wide, 0.0), axis=2, keepdims=True).reshape(n * ROWS, 1)


def kernel(
    cent, qry, mem, slot_in, count_in, pos_in, conc_o, lfin, fin,
    call, qall, pall, mx, mall, slx, sall, invall, score, wgt, peak, sums, sxb, szb, colr, posb, posw,
    gsum, psum, slot, pos, tsend, trx, thz, tsum, ga, gra, ha, hza, acca, gb, grb, hb, hxb, accb,
    local, mx_s, mx_r, sx_s, sx_r, mz_s, mz_r, sz_s, sz_r, qz_s, qz_r, qx_s, qx_r, pz_s, pz_r, px_s, px_r,
    cy_s, cy_r, cc_s, cc_r, iv_s, iv_r, tx_s, tx_r, tz_s, tz_r, gx_s, gx_r, gz_s, gz_r, fn_s, fn_r, ln_s, ln_r,
    ux_s, ux_r, uz_s, uz_r, bz_s, bz_r, bx_s, bx_r,
):
    dp = lax.axis_index("dp")
    p = lax.axis_index("proto")
    z, x = dp // NX, dp % NX
    y, c = p // 2, p % 2

    def at_x(d):
        return (x + d) % NX

    def at_z(d):
        return (z + d) % NZ

    def at_p(d):
        return (p + d) % NP

    def dev_x(d):
        return {"dp": z * NX + at_x(d), "proto": p}

    def dev_z(d):
        return {"dp": at_z(d) * NX + x, "proto": p}

    def dev_p(q):
        return {"dp": dp, "proto": q}

    barrier = pltpu.get_barrier_semaphore()
    for d in range(1, NX):
        pl.semaphore_signal(barrier, inc=1, device_id=dev_x(d), device_id_type=MESH)
    for d in range(1, NZ):
        pl.semaphore_signal(barrier, inc=1, device_id=dev_z(d), device_id_type=MESH)
    for d in range(1, NP):
        pl.semaphore_signal(barrier, inc=1, device_id=dev_p(at_p(d)), device_id_type=MESH)

    used = lax.broadcasted_iota(jnp.int32, (ROWS, NX * NZ), 0) < count_in[pl.ds(p, 1), :]
    ids = jnp.where(used, slot_in[p], -1).astype(F32)
    ids = jnp.concatenate([ids, jnp.zeros((ROWS, 128 - NX * NZ), F32)], axis=1)
    ids = jnp.concatenate([ids, jnp.zeros((128 - ROWS, 128), F32)], axis=0).T
    for i in range(NX * NZ):
        slot[i // NX, i % NX] = ids[i : i + 1, :]
    wide = jnp.broadcast_to(pos_in[...].astype(F32), (8, 128))
    pos[...] = pltpu.roll(wide, (128 - p * ROWS) % 128, 1)[0:1, :]

    pl.semaphore_wait(barrier, NX + NZ + NP - 3)

    sends = []

    def go(copy):
        copy.start()
        sends.append(copy)

    z_order = (4, 3, 5, 2, 6, 1, 7)
    half = CENT // 2
    top, bottom = pl.ds(0, half), pl.ds(half, half)
    cut = 176
    tops = (pl.ds(0, cut), pl.ds(cut, half - cut))
    bottoms = (pl.ds(half, cut), pl.ds(half + cut, half - cut))
    up = ((y + 1) % 4) * 2 + c
    down = ((y + 3) % 4) * 2 + c
    far = ((y + 2) % 4) * 2 + c
    mate = y * 2 + (1 - c)

    for d in z_order:
        go(remote(pos, pall.at[x, z], pz_s.at[d - 1], pz_r.at[d - 1], dev_z(d)))
    for d in z_order:
        go(remote(qry.at[p], qall.at[x, z], qz_s.at[d - 1], qz_r.at[d - 1], dev_z(d)))
    go(remote(cent.at[top], call.at[p, top], cy_s.at[0], cy_r.at[0], dev_p(up)))
    go(remote(cent.at[bottom], call.at[p, bottom], cy_s.at[3], cy_r.at[3], dev_p(down)))
    go(remote(cent.at[bottom], call.at[p, bottom], cy_s.at[1], cy_r.at[1], dev_p(up)))
    go(remote(cent.at[top], call.at[p, top], cy_s.at[2], cy_r.at[2], dev_p(down)))
    go(remote(cent, call.at[p], cc_s.at[0], cc_r.at[0], dev_p(mate)))
    for d in (1, 3, 2):
        go(remote(mem.at[:, at_x(d), p], mx.at[d - 1], mx_s.at[d - 1], mx_r.at[d - 1], dev_x(d)))
        go(remote(slot.at[:, at_x(d)], slx.at[d - 1], sx_s.at[d - 1], sx_r.at[d - 1], dev_x(d)))
    for d in z_order:
        go(remote(mem.at[at_z(d), x, p], mall.at[z, 0], mz_s.at[0, d - 1], mz_r.at[0, d - 1], dev_z(d)))
        go(remote(slot.at[at_z(d), x], sall.at[z, 0], sz_s.at[0, d - 1], sz_r.at[0, d - 1], dev_z(d)))
    own = (
        pltpu.make_async_copy(cent, call.at[p], local.at[0]),
        pltpu.make_async_copy(qry.at[p], qall.at[x, z], local.at[1]),
        pltpu.make_async_copy(mem.at[z, x, p], mall.at[z, 0], local.at[2]),
    )
    for copy in own:
        copy.start()
    pall[x, z] = pos[...]
    sall[z, 0] = slot[z, x]
    psum[...] = jnp.zeros_like(psum)

    for d in range(1, NZ):
        src = at_z(NZ - d)
        remote(pos, pall.at[x, src], pz_s.at[d - 1], pz_r.at[d - 1], dev_z(d)).wait_recv()
    for d in (2, 1, 3):
        go(remote(pall.at[x], pall.at[x], px_s.at[d - 1], px_r.at[d - 1], dev_x(d)))
    own[1].wait()
    for d in range(1, NZ):
        src = at_z(NZ - d)
        remote(qry.at[p], qall.at[x, src], qz_s.at[d - 1], qz_r.at[d - 1], dev_z(d)).wait_recv()
    for d in (2, 1, 3):
        go(remote(qall.at[x], qall.at[x], qx_s.at[d - 1], qx_r.at[d - 1], dev_x(d)))

    def members_on(d):
        remote(mem.at[:, x, p], mx.at[d - 1], mx_s.at[d - 1], mx_r.at[d - 1], dev_x(d)).wait_recv()
        remote(slot.at[:, x], slx.at[d - 1], sx_s.at[d - 1], sx_r.at[d - 1], dev_x(d)).wait_recv()
        for e in z_order:
            go(remote(mx.at[d - 1, at_z(e)], mall.at[z, d], mz_s.at[d, e - 1], mz_r.at[d, e - 1], dev_z(e)))
            go(remote(slx.at[d - 1, at_z(e)], sall.at[z, d], sz_s.at[d, e - 1], sz_r.at[d, e - 1], dev_z(e)))
        mall[z, d] = mx[d - 1, z]
        sall[z, d] = slx[d - 1, z]

    members_on(1)
    members_on(3)
    remote(cent.at[top], call.at[down, top], cy_s.at[0], cy_r.at[0], dev_p(up)).wait_recv()
    for i, r in enumerate(tops):
        go(remote(call.at[down, r], call.at[down, r], cy_s.at[4 + i], cy_r.at[4 + i], dev_p(up)))
    remote(cent.at[bottom], call.at[up, bottom], cy_s.at[3], cy_r.at[3], dev_p(down)).wait_recv()
    for i, r in enumerate(bottoms):
        go(remote(call.at[up, r], call.at[up, r], cy_s.at[6 + i], cy_r.at[6 + i], dev_p(down)))
    go(remote(call.at[down, top], call.at[down, top], cc_s.at[1], cc_r.at[1], dev_p(mate)))
    go(remote(call.at[up, bottom], call.at[up, bottom], cc_s.at[2], cc_r.at[2], dev_p(mate)))
    members_on(2)

    for d in range(1, NX):
        src = at_x(NX - d)
        remote(pall.at[x], pall.at[src], px_s.at[d - 1], px_r.at[d - 1], dev_x(d)).wait_recv()
    base = (dp * (NP * CENT)).astype(F32)
    posb[...] = jnp.broadcast_to(columns_of(pall[...].reshape(NX * NZ, 1, 128)) - base, (QS, 128))

    def positives(chunk):
        here = posb[:, 0:1] - (chunk * CENT).astype(F32)
        hot = lax.broadcasted_iota(jnp.int32, (QS, CENT), 1).astype(F32) == here
        psum[...] += jnp.dot(hot.astype(BF16), call[chunk], preferred_element_type=F32).reshape(psum.shape)

    def scores(chunk):
        def rows(i, carry):
            r = pl.ds(i * 2, 2)
            q = qall[r].reshape(2 * NZ * ROWS, WIDTH)
            score[chunk, pl.ds(i * 256, 256), :] = lax.dot_general(
                q, call[chunk], (((1,), (1,)), ((), ())), preferred_element_type=F32
            )
            return carry

        lax.fori_loop(0, 2, rows, 0)

    own[0].wait()
    positives(p)
    remote(cent, call.at[mate], cc_s.at[0], cc_r.at[0], dev_p(mate)).wait_recv()
    positives(mate)
    for d in range(1, NX):
        src = at_x(NX - d)
        remote(qall.at[x], qall.at[src], qx_s.at[d - 1], qx_r.at[d - 1], dev_x(d)).wait_recv()
    scores(p)
    scores(mate)
    remote(cent.at[bottom], call.at[down, bottom], cy_s.at[1], cy_r.at[1], dev_p(up)).wait_recv()
    go(remote(call.at[down, bottom], call.at[down, bottom], cc_s.at[3], cc_r.at[3], dev_p(mate)))
    remote(cent.at[top], call.at[up, top], cy_s.at[2], cy_r.at[2], dev_p(down)).wait_recv()
    go(remote(call.at[up, top], call.at[up, top], cc_s.at[4], cc_r.at[4], dev_p(mate)))
    flip = 1 - 2 * c
    scores(down)
    scores(up)
    remote(call.at[down, top], call.at[down + flip, top], cc_s.at[1], cc_r.at[1], dev_p(mate)).wait_recv()
    remote(call.at[down, bottom], call.at[down + flip, bottom], cc_s.at[3], cc_r.at[3], dev_p(mate)).wait_recv()
    scores(down + flip)
    remote(call.at[up, bottom], call.at[up + flip, bottom], cc_s.at[2], cc_r.at[2], dev_p(mate)).wait_recv()
    remote(call.at[up, top], call.at[up + flip, top], cc_s.at[4], cc_r.at[4], dev_p(mate)).wait_recv()
    scores(up + flip)

    own[2].wait()
    for e in range(1, NZ):
        src = at_z(NZ - e)
        for d in range(NX):
            remote(mem.at[z, x, p], mall.at[src, d], mz_s.at[d, e - 1], mz_r.at[d, e - 1], dev_z(e)).wait_recv()
            remote(slot.at[z, x], sall.at[src, d], sz_s.at[d, e - 1], sz_r.at[d, e - 1], dev_z(e)).wait_recv()
    which = columns_of(sall[...].reshape(NX * NZ, 1, 128))
    cluster = lax.broadcasted_iota(jnp.int32, (QS, CENT), 1).astype(F32)
    hot = which == cluster
    picked = jnp.dot(hot.astype(BF16), call[p], preferred_element_type=F32)
    gap = mall[...].reshape(QS, WIDTH).astype(F32) - picked
    dist = jnp.sqrt(jnp.sum(gap * gap, axis=1, keepdims=True) + 1e-06)
    total = jnp.sum(jnp.where(hot, dist, 0.0), axis=0, keepdims=True)
    count = jnp.sum(hot.astype(F32), axis=0, keepdims=True)
    conc = (total + 1.0) / ((count + 1.0) * jnp.log(count + 10.0))
    conc_o[...] = conc
    invall[p] = 1.0 / conc
    for d in (4, 3, 5, 2, 6, 1, 7):
        go(remote(invall.at[p], invall.at[p], iv_s.at[d - 1], iv_r.at[d - 1], dev_p(at_p(d))))

    positives(down)
    for i in range(2):
        r = tops[i]
        remote(call.at[down, r], call.at[far, r], cy_s.at[4 + i], cy_r.at[4 + i], dev_p(up)).wait_recv()
        go(remote(call.at[far, r], call.at[far, r], cc_s.at[5 + i], cc_r.at[5 + i], dev_p(mate)))
        r = bottoms[i]
        remote(call.at[up, r], call.at[far, r], cy_s.at[6 + i], cy_r.at[6 + i], dev_p(down)).wait_recv()
        go(remote(call.at[far, r], call.at[far, r], cc_s.at[7 + i], cc_r.at[7 + i], dev_p(mate)))
    scores(far)
    for i in range(4):
        r = (tops + bottoms)[i]
        remote(call.at[far, r], call.at[far + flip, r], cc_s.at[5 + i], cc_r.at[5 + i], dev_p(mate)).wait_recv()
    scores(far + flip)
    for d in range(1, NP):
        src = at_p(NP - d)
        remote(invall.at[p], invall.at[src], iv_s.at[d - 1], iv_r.at[d - 1], dev_p(src)).wait_recv()

    step = 16

    def fold(v, op):
        return op(op(v[:, 0:128], v[:, 128:256]), op(v[:, 256:384], v[:, 384:512]))

    def largest(i, carry):
        r = pl.ds(pl.multiple_of(i * step, step), step)
        best = None
        for k in range(NP):
            zed = score[k, r, :] * (invall[k] * LOG2E)
            best = zed if best is None else jnp.maximum(best, zed)
        peak[r, :] = fold(best, jnp.maximum)
        return carry

    lax.fori_loop(0, QS // step, largest, 0)
    peak[...] = jnp.broadcast_to(jnp.max(peak[...], axis=1, keepdims=True), (QS, 128))

    def soft(i, carry):
        r = pl.ds(pl.multiple_of(i * step, step), step)
        most = jnp.concatenate([peak[r, :]] * 4, axis=1)
        added = None
        for k in range(NP):
            e = jnp.exp2(score[k, r, :] * (invall[k] * LOG2E) - most)
            wgt[k, r, :] = (e * invall[k]).astype(BF16)
            added = e if added is None else added + e
        sums[r, :] = fold(added, jnp.add)
        return carry

    lax.fori_loop(0, QS // step, soft, 0)

    lane = lax.broadcasted_iota(jnp.int32, (QS, 128), 1)
    mine = jnp.where(lane == 0, peak[...], jnp.sum(sums[...], axis=1, keepdims=True)).T[0:8, :]
    sxb[x] = mine

    def merged(ref, n):
        best = ref[0][0:1, :]
        for k in range(1, n):
            best = jnp.maximum(best, ref[k][0:1, :])
        added = None
        for k in range(n):
            part = ref[k][1:2, :] * jnp.exp2(ref[k][0:1, :] - best)
            added = part if added is None else added + part
        return best, added

    for d in (2, 1, 3):
        go(remote(sxb.at[x], sxb.at[x], tx_s.at[d - 1], tx_r.at[d - 1], dev_x(d)))

    def weigh(i, carry):
        r = pl.ds(pl.multiple_of(i * 256, 256), 256)
        out = None
        for k in range(NP):
            term = jnp.dot(wgt[k, r, :], call[k], preferred_element_type=F32)
            out = term if out is None else out + term
        gsum[pl.ds(i * 2, 2)] = out.reshape(2, NZ, ROWS, WIDTH)
        return carry

    lax.fori_loop(0, 2, weigh, 0)

    for d in range(1, NX):
        src = at_x(NX - d)
        remote(sxb.at[x], sxb.at[src], tx_s.at[d - 1], tx_r.at[d - 1], dev_x(d)).wait_recv()
    best, added = merged(sxb, NX)
    szb[z] = jnp.concatenate([best, added, jnp.zeros((6, QS), F32)], axis=0)
    for d in z_order:
        go(remote(szb.at[z], szb.at[z], tz_s.at[d - 1], tz_r.at[d - 1], dev_z(d)))

    def hits(i, carry):
        r = pl.ds(pl.multiple_of(i * step, step), step)
        here = jnp.concatenate([posb[r, :]] * 4, axis=1)
        col = lax.broadcasted_iota(jnp.int32, (step, CENT), 1).astype(F32)
        weight, logit = None, None
        for k in range(NP):
            hit = col + float(k * CENT) == here
            a = jnp.where(hit, jnp.broadcast_to(invall[k], (step, CENT)), 0.0)
            b = jnp.where(hit, score[k, r, :], 0.0)
            weight = a if weight is None else weight + a
            logit = b if logit is None else logit + b
        sums[r, :] = fold(weight, jnp.add)
        peak[r, :] = fold(logit, jnp.add)
        return carry

    lax.fori_loop(0, QS // step, hits, 0)
    scale = jnp.sum(sums[...], axis=1, keepdims=True)
    target = jnp.sum(peak[...], axis=1, keepdims=True) * scale
    posw[...] = jnp.broadcast_to(scale, (QS, 128)).reshape(posw.shape)
    turned = jnp.broadcast_to(target, (QS, 128)).T[0:8, :]
    for b in range(NX):
        tsend[b] = turned[:, b * 128 : (b + 1) * 128]
    positives(up)
    positives(down + flip)
    positives(up + flip)
    positives(far)
    positives(far + flip)

    for d in range(1, NZ):
        src = at_z(NZ - d)
        remote(szb.at[z], szb.at[src], tz_s.at[d - 1], tz_r.at[d - 1], dev_z(d)).wait_recv()
    best, added = merged(szb, NZ)
    share = jnp.exp2(mine[0:1, :] - best) / added
    total_log = best * LN2 + jnp.log(added)
    colr[...] = jnp.concatenate([share, total_log, jnp.zeros((126, QS), F32)], axis=0).T.reshape(colr.shape)

    ca, cb = pl.ds(0, CA), pl.ds(CA, CB)

    def part(at, cols):
        return gsum[at + (slice(None), cols)] * colr[at][..., 0:1] - psum[at + (slice(None), cols)] * posw[at][..., 0:1]

    def part_x(b):
        return part((b, slice(None)), ca)

    def part_z(b):
        return part((slice(None), b), cb)

    ga[1] = part_x(at_x(2)).astype(BF16)
    go(remote(ga.at[1], gra.at[1], gx_s.at[1], gx_r.at[1], dev_x(2)))
    for d in z_order[:3]:
        gb[d - 1] = part_z(at_z(d)).astype(BF16)
        go(remote(gb.at[d - 1], grb.at[d - 1], bz_s.at[d - 1], bz_r.at[d - 1], dev_z(d)))
    for d in (1, 3):
        ga[d - 1] = part_x(at_x(d)).astype(BF16)
        go(remote(ga.at[d - 1], gra.at[d - 1], gx_s.at[d - 1], gx_r.at[d - 1], dev_x(d)))
    for d in z_order[3:]:
        gb[d - 1] = part_z(at_z(d)).astype(BF16)
        go(remote(gb.at[d - 1], grb.at[d - 1], bz_s.at[d - 1], bz_r.at[d - 1], dev_z(d)))
    for d in (2, 1, 3):
        go(remote(tsend.at[at_x(d)], trx.at[d - 1], ux_s.at[d - 1], ux_r.at[d - 1], dev_x(d)))
    acca[...] = part_x(x)
    accb[...] = part_z(z)
    told = tsend[x]
    for d in (1, 3, 2):
        remote(ga.at[d - 1], gra.at[d - 1], gx_s.at[d - 1], gx_r.at[d - 1], dev_x(d)).wait_recv()
        acca[...] += gra[d - 1].astype(F32)
    ha[...] = acca[...].astype(BF16)
    for d in z_order:
        go(remote(ha.at[at_z(d)], hza.at[d - 1], gz_s.at[d - 1], gz_r.at[d - 1], dev_z(d)))
    for d in range(1, NZ):
        remote(gb.at[d - 1], grb.at[d - 1], bz_s.at[d - 1], bz_r.at[d - 1], dev_z(d)).wait_recv()
        accb[...] += grb[d - 1].astype(F32)
    hb[...] = accb[...].astype(BF16)
    for d in (2, 1, 3):
        go(remote(hb.at[at_x(d)], hxb.at[d - 1], bx_s.at[d - 1], bx_r.at[d - 1], dev_x(d)))
    for d in (1, 3, 2):
        remote(tsend.at[x], trx.at[d - 1], ux_s.at[d - 1], ux_r.at[d - 1], dev_x(d)).wait_recv()
        told = told + trx[d - 1]
    tsum[...] = told
    for d in z_order:
        go(remote(tsum, thz.at[d - 1], uz_s.at[d - 1], uz_r.at[d - 1], dev_z(d)))
    grad_b = accb[x]
    for d in (1, 3, 2):
        remote(hb.at[x], hxb.at[d - 1], bx_s.at[d - 1], bx_r.at[d - 1], dev_x(d)).wait_recv()
        grad_b = grad_b + hxb[d - 1].astype(F32)
    grad_a = acca[z]
    for d in range(1, NZ):
        remote(ha.at[z], hza.at[d - 1], gz_s.at[d - 1], gz_r.at[d - 1], dev_z(d)).wait_recv()
        grad_a = grad_a + hza[d - 1].astype(F32)

    fin[p, :, ca] = grad_a.astype(BF16)
    fin[p, :, cb] = grad_b.astype(BF16)
    for d in (4, 3, 5, 2, 6, 1, 7):
        go(remote(fin.at[p], fin.at[p], fn_s.at[d - 1], fn_r.at[d - 1], dev_p(at_p(d))))
    for d in range(1, NZ):
        remote(tsum, thz.at[d - 1], uz_s.at[d - 1], uz_r.at[d - 1], dev_z(d)).wait_recv()
        told = told + thz[d - 1]
    peak[0:128, :] = jnp.concatenate([told, jnp.zeros((120, 128), F32)], axis=0).T
    z_rows = pl.ds(pl.multiple_of(z * ROWS, ROWS), ROWS)
    lfin[p] = jnp.broadcast_to(colr[x, z][:, 1:2] - peak[z_rows, 0:1], (ROWS, 128))
    for d in (4, 3, 5, 2, 6, 1, 7):
        go(remote(lfin.at[p], lfin.at[p], ln_s.at[d - 1], ln_r.at[d - 1], dev_p(at_p(d))))
    for d in range(1, NP):
        src = at_p(NP - d)
        remote(lfin.at[p], lfin.at[src], ln_s.at[d - 1], ln_r.at[d - 1], dev_p(src)).wait_recv()
        remote(fin.at[p], fin.at[src], fn_s.at[d - 1], fn_r.at[d - 1], dev_p(src)).wait_recv()
    for copy in sends:
        copy.wait_send()


def finish(conc, lfin, fin, conc_o, loss_o, grad_o):
    conc_o[...] = conc[...]
    loss_o[...] = lfin[...].reshape(NP * ROWS, 128).T[0:1, :]
    grad_o[...] = fin[...].reshape(NP * ROWS, WIDTH)


def on_device(centroids, queries, positive, members, member_slot, block_count):
    vmem = pltpu.VMEM
    dma = pltpu.SemaphoreType.DMA
    sems = []
    for shape in (
        (NX - 1,), (NX - 1,), (NX, NZ - 1), (NX, NZ - 1), (NZ - 1,), (NX - 1,), (NZ - 1,), (NX - 1,),
        (8,), (9,), (NP - 1,), (NX - 1,), (NZ - 1,), (NX - 1,), (NZ - 1,), (NP - 1,), (NP - 1,),
        (NX - 1,), (NZ - 1,), (NZ - 1,), (NX - 1,),
    ):
        sems += [dma(shape), dma(shape)]
    whole = pl.BlockSpec(memory_space=vmem)
    conc, lfin, fin = pl.pallas_call(
        kernel,
        out_shape=(
            jax.ShapeDtypeStruct((1, CENT), F32),
            jax.ShapeDtypeStruct((NP, ROWS, 128), F32),
            jax.ShapeDtypeStruct((NP, ROWS, WIDTH), BF16),
        ),
        in_specs=[pl.BlockSpec(memory_space=pl.ANY)] * 3 + [whole] * 3,
        out_specs=(whole,) * 3,
        scratch_shapes=[
            vmem((NP, CENT, WIDTH), BF16),
            vmem((NX, NZ, ROWS, WIDTH), BF16),
            vmem((NX, NZ, 1, 128), F32),
            vmem((NX - 1, NZ, ROWS, WIDTH), BF16),
            vmem((NZ, NX, ROWS, WIDTH), BF16),
            vmem((NX - 1, NZ, 1, 128), F32),
            vmem((NZ, NX, 1, 128), F32),
            vmem((NP, 1, CENT), F32),
            vmem((NP, QS, CENT), F32),
            vmem((NP, QS, CENT), BF16),
            vmem((QS, 128), F32),
            vmem((QS, 128), F32),
            vmem((NX, 8, QS), F32),
            vmem((NZ, 8, QS), F32),
            vmem((NX, NZ, ROWS, 128), F32),
            vmem((QS, 128), F32),
            vmem((NX, NZ, ROWS, 128), F32),
            vmem((NX, NZ, ROWS, WIDTH), F32),
            vmem((NX, NZ, ROWS, WIDTH), F32),
            vmem((NZ, NX, 1, 128), F32),
            vmem((1, 128), F32),
            vmem((NX, 8, 128), F32),
            vmem((NX - 1, 8, 128), F32),
            vmem((NZ - 1, 8, 128), F32),
            vmem((8, 128), F32),
            vmem((NX - 1, NZ, ROWS, CA), BF16),
            vmem((NX - 1, NZ, ROWS, CA), BF16),
            vmem((NZ, ROWS, CA), BF16),
            vmem((NZ - 1, ROWS, CA), BF16),
            vmem((NZ, ROWS, CA), F32),
            vmem((NZ - 1, NX, ROWS, CB), BF16),
            vmem((NZ - 1, NX, ROWS, CB), BF16),
            vmem((NX, ROWS, CB), BF16),
            vmem((NX - 1, ROWS, CB), BF16),
            vmem((NX, ROWS, CB), F32),
            dma((3,)),
            *sems,
        ],
        compiler_params=pltpu.CompilerParams(
            collective_id=0, has_side_effects=True, vmem_limit_bytes=56 * 1024 * 1024
        ),
        name="protonce",
    )(
        centroids,
        queries.reshape(NP, ROWS, WIDTH),
        members.reshape(NZ, NX, NP, ROWS, WIDTH),
        member_slot.transpose(0, 2, 3, 1).reshape(NP, ROWS, NX * NZ),
        block_count.transpose(0, 2, 1).reshape(NP, NX * NZ),
        positive.reshape(1, NP * ROWS),
    )
    conc, loss, grad = pl.pallas_call(
        finish,
        out_shape=(
            jax.ShapeDtypeStruct((1, CENT), F32),
            jax.ShapeDtypeStruct((1, NP * ROWS), F32),
            jax.ShapeDtypeStruct((NP * ROWS, WIDTH), BF16),
        ),
        in_specs=[whole] * 3,
        out_specs=(whole,) * 3,
        name="finish",
    )(conc, lfin, fin)
    return conc.reshape(CENT), loss.reshape(NP * ROWS), grad


def solution(mesh):
    placed = (
        P(("dp", "proto"), None),
        P("dp", None),
        P("dp"),
        P("dp", None, None, None, None),
        P("dp", None, None, None),
        P("dp", None, None),
    )
    return jax.shard_map(
        on_device,
        mesh=mesh,
        in_specs=placed,
        out_specs=(P(("dp", "proto")), P("dp"), P("dp", None)),
        check_vma=False,
    )
```

```python
import jax
import jax.numpy as jnp
from jax import lax
from jax.experimental import pallas as pl
from jax.experimental.pallas import tpu as pltpu
from jax.sharding import PartitionSpec as P

MESH = pl.DeviceIdType.MESH
NX, NZ, NP = 4, 8, 8
ROWS, WIDTH, CENT = 16, 768, 512
QS = NX * NZ * ROWS
CA = 512
CB = WIDTH - CA
F32, BF16 = jnp.float32, jnp.bfloat16
LOG2E, LN2 = 1.4426950408889634, 0.6931471805599453


def remote(src, dst, send, recv, device):
    return pltpu.make_async_remote_copy(
        src_ref=src, dst_ref=dst, send_sem=send, recv_sem=recv, device_id=device, device_id_type=MESH
    )


def columns_of(rows):
    n = rows.shape[0]
    wide = jnp.broadcast_to(rows, (n, ROWS, 128))
    lane = lax.broadcasted_iota(jnp.int32, (n, ROWS, 128), 2)
    sub = lax.broadcasted_iota(jnp.int32, (n, ROWS, 128), 1)
    return jnp.sum(jnp.where(lane == sub, wide, 0.0), axis=2, keepdims=True).reshape(n * ROWS, 1)


def kernel(
    cent, qry, mem, slot_in, count_in, pos_in, conc_o, lfin, fin,
    call, qall, pall, mx, mall, slx, sall, invall, score, wgt, peak, sums, peakb, sumsb, tile, colr, posb, posw,
    gsum, psum, slot, pos, tsend, trx, thz, tsum, ga, gra, ha, hza, acca, gb, grb, hb, hxb, accb,
    local, mx_s, mx_r, sx_s, sx_r, mz_s, mz_r, sz_s, sz_r, qz_s, qz_r, qx_s, qx_r, pz_s, pz_r, px_s, px_r,
    cy_s, cy_r, cc_s, cc_r, iv_s, iv_r, st_s, st_r, gx_s, gx_r, gz_s, gz_r, fn_s, fn_r, ln_s, ln_r,
    ux_s, ux_r, uz_s, uz_r, bz_s, bz_r, bx_s, bx_r,
):
    dp = lax.axis_index("dp")
    p = lax.axis_index("proto")
    z, x = dp // NX, dp % NX
    y, c = p // 2, p % 2

    def at_x(d):
        return (x + d) % NX

    def at_z(d):
        return (z + d) % NZ

    def at_p(d):
        return (p + d) % NP

    def dev_x(d):
        return {"dp": z * NX + at_x(d), "proto": p}

    def dev_z(d):
        return {"dp": at_z(d) * NX + x, "proto": p}

    def dev_xz(d, e):
        return {"dp": at_z(e) * NX + at_x(d), "proto": p}

    def dev_p(q):
        return {"dp": dp, "proto": q}

    barrier = pltpu.get_barrier_semaphore()
    both = sorted(
        ((d, e) for d in range(NX) for e in range(NZ) if d + e), key=lambda v: -min(v[0], NX - v[0]) - min(v[1], NZ - v[1])
    )
    for d, e in both:
        pl.semaphore_signal(barrier, inc=1, device_id=dev_xz(d, e), device_id_type=MESH)
    for d in range(1, NP):
        pl.semaphore_signal(barrier, inc=1, device_id=dev_p(at_p(d)), device_id_type=MESH)

    used = lax.broadcasted_iota(jnp.int32, (ROWS, NX * NZ), 0) < count_in[pl.ds(p, 1), :]
    ids = jnp.where(used, slot_in[p], -1).astype(F32)
    ids = jnp.concatenate([ids, jnp.zeros((ROWS, 128 - NX * NZ), F32)], axis=1)
    ids = jnp.concatenate([ids, jnp.zeros((128 - ROWS, 128), F32)], axis=0).T
    for i in range(NX * NZ):
        slot[i // NX, i % NX] = ids[i : i + 1, :]
    wide = jnp.broadcast_to(pos_in[...].astype(F32), (8, 128))
    pos[...] = pltpu.roll(wide, (128 - p * ROWS) % 128, 1)[0:1, :]

    pl.semaphore_wait(barrier, NX * NZ + NP - 2)

    sends = []

    def go(copy):
        copy.start()
        sends.append(copy)

    z_order = (4, 3, 5, 2, 6, 1, 7)
    half = CENT // 2
    top, bottom = pl.ds(0, half), pl.ds(half, half)
    cut = 176
    tops = (pl.ds(0, cut), pl.ds(cut, half - cut))
    bottoms = (pl.ds(half, cut), pl.ds(half + cut, half - cut))
    up = ((y + 1) % 4) * 2 + c
    down = ((y + 3) % 4) * 2 + c
    far = ((y + 2) % 4) * 2 + c
    mate = y * 2 + (1 - c)

    for d in z_order:
        go(remote(pos, pall.at[x, z], pz_s.at[d - 1], pz_r.at[d - 1], dev_z(d)))
    for d in z_order:
        go(remote(qry.at[p], qall.at[x, z], qz_s.at[d - 1], qz_r.at[d - 1], dev_z(d)))
    go(remote(cent.at[top], call.at[p, top], cy_s.at[0], cy_r.at[0], dev_p(up)))
    go(remote(cent.at[bottom], call.at[p, bottom], cy_s.at[3], cy_r.at[3], dev_p(down)))
    go(remote(cent.at[bottom], call.at[p, bottom], cy_s.at[1], cy_r.at[1], dev_p(up)))
    go(remote(cent.at[top], call.at[p, top], cy_s.at[2], cy_r.at[2], dev_p(down)))
    go(remote(cent, call.at[p], cc_s.at[0], cc_r.at[0], dev_p(mate)))
    for d in (1, 3, 2):
        go(remote(mem.at[:, at_x(d), p], mx.at[d - 1], mx_s.at[d - 1], mx_r.at[d - 1], dev_x(d)))
        go(remote(slot.at[:, at_x(d)], slx.at[d - 1], sx_s.at[d - 1], sx_r.at[d - 1], dev_x(d)))
    for d in z_order:
        go(remote(mem.at[at_z(d), x, p], mall.at[z, 0], mz_s.at[0, d - 1], mz_r.at[0, d - 1], dev_z(d)))
        go(remote(slot.at[at_z(d), x], sall.at[z, 0], sz_s.at[0, d - 1], sz_r.at[0, d - 1], dev_z(d)))
    own = (
        pltpu.make_async_copy(cent, call.at[p], local.at[0]),
        pltpu.make_async_copy(qry.at[p], qall.at[x, z], local.at[1]),
        pltpu.make_async_copy(mem.at[z, x, p], mall.at[z, 0], local.at[2]),
    )
    for copy in own:
        copy.start()
    pall[x, z] = pos[...]
    sall[z, 0] = slot[z, x]
    psum[...] = jnp.zeros_like(psum)

    for d in range(1, NZ):
        src = at_z(NZ - d)
        remote(pos, pall.at[x, src], pz_s.at[d - 1], pz_r.at[d - 1], dev_z(d)).wait_recv()
    for d in (2, 1, 3):
        go(remote(pall.at[x], pall.at[x], px_s.at[d - 1], px_r.at[d - 1], dev_x(d)))
    own[1].wait()
    for d in range(1, NZ):
        src = at_z(NZ - d)
        remote(qry.at[p], qall.at[x, src], qz_s.at[d - 1], qz_r.at[d - 1], dev_z(d)).wait_recv()
    for d in (2, 1, 3):
        go(remote(qall.at[x], qall.at[x], qx_s.at[d - 1], qx_r.at[d - 1], dev_x(d)))

    def members_on(d):
        remote(mem.at[:, x, p], mx.at[d - 1], mx_s.at[d - 1], mx_r.at[d - 1], dev_x(d)).wait_recv()
        remote(slot.at[:, x], slx.at[d - 1], sx_s.at[d - 1], sx_r.at[d - 1], dev_x(d)).wait_recv()
        for e in z_order:
            go(remote(mx.at[d - 1, at_z(e)], mall.at[z, d], mz_s.at[d, e - 1], mz_r.at[d, e - 1], dev_z(e)))
            go(remote(slx.at[d - 1, at_z(e)], sall.at[z, d], sz_s.at[d, e - 1], sz_r.at[d, e - 1], dev_z(e)))
        mall[z, d] = mx[d - 1, z]
        sall[z, d] = slx[d - 1, z]

    members_on(1)
    members_on(3)
    remote(cent.at[top], call.at[down, top], cy_s.at[0], cy_r.at[0], dev_p(up)).wait_recv()
    for i, r in enumerate(tops):
        go(remote(call.at[down, r], call.at[down, r], cy_s.at[4 + i], cy_r.at[4 + i], dev_p(up)))
    remote(cent.at[bottom], call.at[up, bottom], cy_s.at[3], cy_r.at[3], dev_p(down)).wait_recv()
    for i, r in enumerate(bottoms):
        go(remote(call.at[up, r], call.at[up, r], cy_s.at[6 + i], cy_r.at[6 + i], dev_p(down)))
    go(remote(call.at[down, top], call.at[down, top], cc_s.at[1], cc_r.at[1], dev_p(mate)))
    go(remote(call.at[up, bottom], call.at[up, bottom], cc_s.at[2], cc_r.at[2], dev_p(mate)))
    members_on(2)

    for d in range(1, NX):
        src = at_x(NX - d)
        remote(pall.at[x], pall.at[src], px_s.at[d - 1], px_r.at[d - 1], dev_x(d)).wait_recv()
    base = (dp * (NP * CENT)).astype(F32)
    posb[...] = jnp.broadcast_to(columns_of(pall[...].reshape(NX * NZ, 1, 128)) - base, (QS, 128))

    def positives(chunk):
        here = posb[:, 0:1] - (chunk * CENT).astype(F32)
        hot = lax.broadcasted_iota(jnp.int32, (QS, CENT), 1).astype(F32) == here
        psum[...] += jnp.dot(hot.astype(BF16), call[chunk], preferred_element_type=F32).reshape(psum.shape)

    def scores(chunk):
        def rows(i, carry):
            r = pl.ds(i * 2, 2)
            q = qall[r].reshape(2 * NZ * ROWS, WIDTH)
            score[chunk, pl.ds(i * 256, 256), :] = lax.dot_general(
                q, call[chunk], (((1,), (1,)), ((), ())), preferred_element_type=F32
            )
            return carry

        lax.fori_loop(0, 2, rows, 0)

    own[0].wait()
    positives(p)
    remote(cent, call.at[mate], cc_s.at[0], cc_r.at[0], dev_p(mate)).wait_recv()
    positives(mate)
    for d in range(1, NX):
        src = at_x(NX - d)
        remote(qall.at[x], qall.at[src], qx_s.at[d - 1], qx_r.at[d - 1], dev_x(d)).wait_recv()
    scores(p)
    scores(mate)
    remote(cent.at[bottom], call.at[down, bottom], cy_s.at[1], cy_r.at[1], dev_p(up)).wait_recv()
    go(remote(call.at[down, bottom], call.at[down, bottom], cc_s.at[3], cc_r.at[3], dev_p(mate)))
    remote(cent.at[top], call.at[up, top], cy_s.at[2], cy_r.at[2], dev_p(down)).wait_recv()
    go(remote(call.at[up, top], call.at[up, top], cc_s.at[4], cc_r.at[4], dev_p(mate)))
    flip = 1 - 2 * c
    scores(down)
    scores(up)
    remote(call.at[down, top], call.at[down + flip, top], cc_s.at[1], cc_r.at[1], dev_p(mate)).wait_recv()
    remote(call.at[down, bottom], call.at[down + flip, bottom], cc_s.at[3], cc_r.at[3], dev_p(mate)).wait_recv()
    scores(down + flip)
    remote(call.at[up, bottom], call.at[up + flip, bottom], cc_s.at[2], cc_r.at[2], dev_p(mate)).wait_recv()
    remote(call.at[up, top], call.at[up + flip, top], cc_s.at[4], cc_r.at[4], dev_p(mate)).wait_recv()
    scores(up + flip)

    own[2].wait()
    for e in range(1, NZ):
        src = at_z(NZ - e)
        for d in range(NX):
            remote(mem.at[z, x, p], mall.at[src, d], mz_s.at[d, e - 1], mz_r.at[d, e - 1], dev_z(e)).wait_recv()
            remote(slot.at[z, x], sall.at[src, d], sz_s.at[d, e - 1], sz_r.at[d, e - 1], dev_z(e)).wait_recv()
    which = columns_of(sall[...].reshape(NX * NZ, 1, 128))
    cluster = lax.broadcasted_iota(jnp.int32, (QS, CENT), 1).astype(F32)
    hot = which == cluster
    picked = jnp.dot(hot.astype(BF16), call[p], preferred_element_type=F32)
    gap = mall[...].reshape(QS, WIDTH).astype(F32) - picked
    dist = jnp.sqrt(jnp.sum(gap * gap, axis=1, keepdims=True) + 1e-06)
    total = jnp.sum(jnp.where(hot, dist, 0.0), axis=0, keepdims=True)
    count = jnp.sum(hot.astype(F32), axis=0, keepdims=True)
    conc = (total + 1.0) / ((count + 1.0) * jnp.log(count + 10.0))
    conc_o[...] = conc
    invall[p] = 1.0 / conc
    for d in (4, 3, 5, 2, 6, 1, 7):
        go(remote(invall.at[p], invall.at[p], iv_s.at[d - 1], iv_r.at[d - 1], dev_p(at_p(d))))

    positives(down)
    positives(up)
    positives(down + flip)
    positives(up + flip)
    for i in range(2):
        r = tops[i]
        remote(call.at[down, r], call.at[far, r], cy_s.at[4 + i], cy_r.at[4 + i], dev_p(up)).wait_recv()
        go(remote(call.at[far, r], call.at[far, r], cc_s.at[5 + i], cc_r.at[5 + i], dev_p(mate)))
        r = bottoms[i]
        remote(call.at[up, r], call.at[far, r], cy_s.at[6 + i], cy_r.at[6 + i], dev_p(down)).wait_recv()
        go(remote(call.at[far, r], call.at[far, r], cc_s.at[7 + i], cc_r.at[7 + i], dev_p(mate)))
    scores(far)
    positives(far)
    for d in range(1, NP):
        src = at_p(NP - d)
        remote(invall.at[p], invall.at[src], iv_s.at[d - 1], iv_r.at[d - 1], dev_p(src)).wait_recv()

    step = 16

    def fold(v, op):
        return op(op(v[:, 0:128], v[:, 128:256]), op(v[:, 256:384], v[:, 384:512]))

    def soften(chunks, peak, sums):
        def largest(i, carry):
            r = pl.ds(pl.multiple_of(i * step, step), step)
            best = None
            for k in chunks:
                zed = score[k, r, :] * (invall[k] * LOG2E)
                best = zed if best is None else jnp.maximum(best, zed)
            peak[r, :] = fold(best, jnp.maximum)
            return carry

        lax.fori_loop(0, QS // step, largest, 0)
        peak[...] = jnp.broadcast_to(jnp.max(peak[...], axis=1, keepdims=True), (QS, 128))

        def soft(i, carry):
            r = pl.ds(pl.multiple_of(i * step, step), step)
            most = jnp.concatenate([peak[r, :]] * 4, axis=1)
            added = None
            for k in chunks:
                e = jnp.exp2(score[k, r, :] * (invall[k] * LOG2E) - most)
                wgt[k, r, :] = (e * invall[k]).astype(BF16)
                added = e if added is None else added + e
            sums[r, :] = fold(added, jnp.add)
            return carry

        lax.fori_loop(0, QS // step, soft, 0)

    early = (p, mate, down, up, down + flip, up + flip, far)
    last = far + flip
    soften(early, peak, sums)
    for i in range(4):
        r = (tops + bottoms)[i]
        remote(call.at[far, r], call.at[far + flip, r], cc_s.at[5 + i], cc_r.at[5 + i], dev_p(mate)).wait_recv()
    scores(last)
    soften((last,), peakb, sumsb)

    lane = lax.broadcasted_iota(jnp.int32, (QS, 128), 1)
    most = jnp.maximum(peak[...], peakb[...])
    peak[...] = jnp.exp2(peak[...] - most)
    peakb[...] = jnp.exp2(peakb[...] - most)
    summed = jnp.sum(sums[...] * peak[...] + sumsb[...] * peakb[...], axis=1, keepdims=True)
    mine = jnp.where(lane == 0, most, summed).T
    tile[x, z] = jnp.concatenate([mine[i : i + 1, b * 128 : (b + 1) * 128] for i in range(2) for b in range(NX)], axis=0)
    for d, e in both:
        go(remote(tile.at[x, z], tile.at[x, z], st_s.at[d * NZ + e], st_r.at[d * NZ + e], dev_xz(d, e)))

    def weigh(i, carry):
        r = pl.ds(pl.multiple_of(i * 256, 256), 256)
        out = None
        for k in early:
            term = jnp.dot(wgt[k, r, :], call[k], preferred_element_type=F32)
            out = term if out is None else out + term
        late = jnp.dot(wgt[last, r, :], call[last], preferred_element_type=F32)
        out = out * peak[r, 0:1] + late * peakb[r, 0:1]
        gsum[pl.ds(i * 2, 2)] = out.reshape(2, NZ, ROWS, WIDTH)
        return carry

    lax.fori_loop(0, 2, weigh, 0)

    def hits(i, carry):
        r = pl.ds(pl.multiple_of(i * step, step), step)
        here = jnp.concatenate([posb[r, :]] * 4, axis=1)
        col = lax.broadcasted_iota(jnp.int32, (step, CENT), 1).astype(F32)
        weight, logit = None, None
        for k in range(NP):
            hit = col + float(k * CENT) == here
            a = jnp.where(hit, jnp.broadcast_to(invall[k], (step, CENT)), 0.0)
            b = jnp.where(hit, score[k, r, :], 0.0)
            weight = a if weight is None else weight + a
            logit = b if logit is None else logit + b
        sums[r, :] = fold(weight, jnp.add)
        peak[r, :] = fold(logit, jnp.add)
        return carry

    lax.fori_loop(0, QS // step, hits, 0)
    scale = jnp.sum(sums[...], axis=1, keepdims=True)
    target = jnp.sum(peak[...], axis=1, keepdims=True) * scale
    posw[...] = jnp.broadcast_to(scale, (QS, 128)).reshape(posw.shape)
    turned = jnp.broadcast_to(target, (QS, 128)).T[0:8, :]
    for b in range(NX):
        tsend[b] = turned[:, b * 128 : (b + 1) * 128]
    positives(last)

    for d, e in both:
        src = (at_x(NX - d), at_z(NZ - e))
        remote(tile.at[x, z], tile.at[src], st_s.at[d * NZ + e], st_r.at[d * NZ + e], dev_xz(d, e)).wait_recv()
    tiles = tile[...].reshape(NX * NZ, 8, 128)
    best = jnp.max(tiles[:, 0:NX], axis=0)
    added = jnp.sum(tiles[:, NX:8] * jnp.exp2(tiles[:, 0:NX] - best[None]), axis=0)

    def flat(v):
        return jnp.concatenate([v[b : b + 1, :] for b in range(NX)], axis=1)

    share = flat(jnp.exp2(tile[x, z][0:NX] - best) / added)
    total_log = flat(best * LN2 + jnp.log(added))
    colr[...] = jnp.concatenate([share, total_log, jnp.zeros((126, QS), F32)], axis=0).T.reshape(colr.shape)

    ca, cb = pl.ds(0, CA), pl.ds(CA, CB)

    def part(at, cols):
        return gsum[at + (slice(None), cols)] * colr[at][..., 0:1] - psum[at + (slice(None), cols)] * posw[at][..., 0:1]

    def part_x(b):
        return part((b, slice(None)), ca)

    def part_z(b):
        return part((slice(None), b), cb)

    ga[1] = part_x(at_x(2)).astype(BF16)
    go(remote(ga.at[1], gra.at[1], gx_s.at[1], gx_r.at[1], dev_x(2)))
    for d in z_order[:3]:
        gb[d - 1] = part_z(at_z(d)).astype(BF16)
        go(remote(gb.at[d - 1], grb.at[d - 1], bz_s.at[d - 1], bz_r.at[d - 1], dev_z(d)))
    for d in (1, 3):
        ga[d - 1] = part_x(at_x(d)).astype(BF16)
        go(remote(ga.at[d - 1], gra.at[d - 1], gx_s.at[d - 1], gx_r.at[d - 1], dev_x(d)))
    for d in z_order[3:]:
        gb[d - 1] = part_z(at_z(d)).astype(BF16)
        go(remote(gb.at[d - 1], grb.at[d - 1], bz_s.at[d - 1], bz_r.at[d - 1], dev_z(d)))
    for d in (2, 1, 3):
        go(remote(tsend.at[at_x(d)], trx.at[d - 1], ux_s.at[d - 1], ux_r.at[d - 1], dev_x(d)))
    acca[...] = part_x(x)
    accb[...] = part_z(z)
    told = tsend[x]
    for d in (1, 3, 2):
        remote(ga.at[d - 1], gra.at[d - 1], gx_s.at[d - 1], gx_r.at[d - 1], dev_x(d)).wait_recv()
        acca[...] += gra[d - 1].astype(F32)
    ha[...] = acca[...].astype(BF16)
    for d in z_order:
        go(remote(ha.at[at_z(d)], hza.at[d - 1], gz_s.at[d - 1], gz_r.at[d - 1], dev_z(d)))
    for d in range(1, NZ):
        remote(gb.at[d - 1], grb.at[d - 1], bz_s.at[d - 1], bz_r.at[d - 1], dev_z(d)).wait_recv()
        accb[...] += grb[d - 1].astype(F32)
    hb[...] = accb[...].astype(BF16)
    for d in (2, 1, 3):
        go(remote(hb.at[at_x(d)], hxb.at[d - 1], bx_s.at[d - 1], bx_r.at[d - 1], dev_x(d)))
    for d in (1, 3, 2):
        remote(tsend.at[x], trx.at[d - 1], ux_s.at[d - 1], ux_r.at[d - 1], dev_x(d)).wait_recv()
        told = told + trx[d - 1]
    tsum[...] = told
    for d in z_order:
        go(remote(tsum, thz.at[d - 1], uz_s.at[d - 1], uz_r.at[d - 1], dev_z(d)))
    grad_b = accb[x]
    for d in (1, 3, 2):
        remote(hb.at[x], hxb.at[d - 1], bx_s.at[d - 1], bx_r.at[d - 1], dev_x(d)).wait_recv()
        grad_b = grad_b + hxb[d - 1].astype(F32)
    grad_a = acca[z]
    for d in range(1, NZ):
        remote(ha.at[z], hza.at[d - 1], gz_s.at[d - 1], gz_r.at[d - 1], dev_z(d)).wait_recv()
        grad_a = grad_a + hza[d - 1].astype(F32)

    fin[p, :, ca] = grad_a.astype(BF16)
    fin[p, :, cb] = grad_b.astype(BF16)
    for d in (4, 3, 5, 2, 6, 1, 7):
        go(remote(fin.at[p], fin.at[p], fn_s.at[d - 1], fn_r.at[d - 1], dev_p(at_p(d))))
    for d in range(1, NZ):
        remote(tsum, thz.at[d - 1], uz_s.at[d - 1], uz_r.at[d - 1], dev_z(d)).wait_recv()
        told = told + thz[d - 1]
    peak[0:128, :] = jnp.concatenate([told, jnp.zeros((120, 128), F32)], axis=0).T
    z_rows = pl.ds(pl.multiple_of(z * ROWS, ROWS), ROWS)
    lfin[p] = jnp.broadcast_to(colr[x, z][:, 1:2] - peak[z_rows, 0:1], (ROWS, 128))
    for d in (4, 3, 5, 2, 6, 1, 7):
        go(remote(lfin.at[p], lfin.at[p], ln_s.at[d - 1], ln_r.at[d - 1], dev_p(at_p(d))))
    for d in range(1, NP):
        src = at_p(NP - d)
        remote(lfin.at[p], lfin.at[src], ln_s.at[d - 1], ln_r.at[d - 1], dev_p(src)).wait_recv()
        remote(fin.at[p], fin.at[src], fn_s.at[d - 1], fn_r.at[d - 1], dev_p(src)).wait_recv()
    for copy in sends:
        copy.wait_send()


def finish(conc, lfin, fin, conc_o, loss_o, grad_o):
    conc_o[...] = conc[...]
    loss_o[...] = lfin[...].reshape(NP * ROWS, 128).T[0:1, :]
    grad_o[...] = fin[...].reshape(NP * ROWS, WIDTH)


def on_device(centroids, queries, positive, members, member_slot, block_count):
    vmem = pltpu.VMEM
    dma = pltpu.SemaphoreType.DMA
    sems = []
    for shape in (
        (NX - 1,), (NX - 1,), (NX, NZ - 1), (NX, NZ - 1), (NZ - 1,), (NX - 1,), (NZ - 1,), (NX - 1,),
        (8,), (9,), (NP - 1,), (NX * NZ,), (NX - 1,), (NZ - 1,), (NP - 1,), (NP - 1,),
        (NX - 1,), (NZ - 1,), (NZ - 1,), (NX - 1,),
    ):
        sems += [dma(shape), dma(shape)]
    whole = pl.BlockSpec(memory_space=vmem)
    conc, lfin, fin = pl.pallas_call(
        kernel,
        out_shape=(
            jax.ShapeDtypeStruct((1, CENT), F32),
            jax.ShapeDtypeStruct((NP, ROWS, 128), F32),
            jax.ShapeDtypeStruct((NP, ROWS, WIDTH), BF16),
        ),
        in_specs=[pl.BlockSpec(memory_space=pl.ANY)] * 3 + [whole] * 3,
        out_specs=(whole,) * 3,
        scratch_shapes=[
            vmem((NP, CENT, WIDTH), BF16),
            vmem((NX, NZ, ROWS, WIDTH), BF16),
            vmem((NX, NZ, 1, 128), F32),
            vmem((NX - 1, NZ, ROWS, WIDTH), BF16),
            vmem((NZ, NX, ROWS, WIDTH), BF16),
            vmem((NX - 1, NZ, 1, 128), F32),
            vmem((NZ, NX, 1, 128), F32),
            vmem((NP, 1, CENT), F32),
            vmem((NP, QS, CENT), F32),
            vmem((NP, QS, CENT), BF16),
            vmem((QS, 128), F32),
            vmem((QS, 128), F32),
            vmem((QS, 128), F32),
            vmem((QS, 128), F32),
            vmem((NX, NZ, 8, 128), F32),
            vmem((NX, NZ, ROWS, 128), F32),
            vmem((QS, 128), F32),
            vmem((NX, NZ, ROWS, 128), F32),
            vmem((NX, NZ, ROWS, WIDTH), F32),
            vmem((NX, NZ, ROWS, WIDTH), F32),
            vmem((NZ, NX, 1, 128), F32),
            vmem((1, 128), F32),
            vmem((NX, 8, 128), F32),
            vmem((NX - 1, 8, 128), F32),
            vmem((NZ - 1, 8, 128), F32),
            vmem((8, 128), F32),
            vmem((NX - 1, NZ, ROWS, CA), BF16),
            vmem((NX - 1, NZ, ROWS, CA), BF16),
            vmem((NZ, ROWS, CA), BF16),
            vmem((NZ - 1, ROWS, CA), BF16),
            vmem((NZ, ROWS, CA), F32),
            vmem((NZ - 1, NX, ROWS, CB), BF16),
            vmem((NZ - 1, NX, ROWS, CB), BF16),
            vmem((NX, ROWS, CB), BF16),
            vmem((NX - 1, ROWS, CB), BF16),
            vmem((NX, ROWS, CB), F32),
            dma((3,)),
            *sems,
        ],
        compiler_params=pltpu.CompilerParams(
            collective_id=0, has_side_effects=True, vmem_limit_bytes=56 * 1024 * 1024
        ),
        name="protonce",
    )(
        centroids,
        queries.reshape(NP, ROWS, WIDTH),
        members.reshape(NZ, NX, NP, ROWS, WIDTH),
        member_slot.transpose(0, 2, 3, 1).reshape(NP, ROWS, NX * NZ),
        block_count.transpose(0, 2, 1).reshape(NP, NX * NZ),
        positive.reshape(1, NP * ROWS),
    )
    conc, loss, grad = pl.pallas_call(
        finish,
        out_shape=(
            jax.ShapeDtypeStruct((1, CENT), F32),
            jax.ShapeDtypeStruct((1, NP * ROWS), F32),
            jax.ShapeDtypeStruct((NP * ROWS, WIDTH), BF16),
        ),
        in_specs=[whole] * 3,
        out_specs=(whole,) * 3,
        name="finish",
    )(conc, lfin, fin)
    return conc.reshape(CENT), loss.reshape(NP * ROWS), grad


def solution(mesh):
    placed = (
        P(("dp", "proto"), None),
        P("dp", None),
        P("dp"),
        P("dp", None, None, None, None),
        P("dp", None, None, None),
        P("dp", None, None),
    )
    return jax.shard_map(
        on_device,
        mesh=mesh,
        in_specs=placed,
        out_specs=(P(("dp", "proto")), P("dp"), P("dp", None)),
        check_vma=False,
    )
```

```python
import jax
import jax.numpy as jnp
from jax import lax
from jax.experimental import pallas as pl
from jax.experimental.pallas import tpu as pltpu
from jax.sharding import PartitionSpec as P

MESH = pl.DeviceIdType.MESH
NX, NZ, NP = 4, 8, 8
ROWS, WIDTH, CENT = 16, 768, 512
QS = NX * NZ * ROWS
CA = 512
CB = WIDTH - CA
F32, BF16 = jnp.float32, jnp.bfloat16
LOG2E, LN2 = 1.4426950408889634, 0.6931471805599453


def remote(src, dst, send, recv, device):
    return pltpu.make_async_remote_copy(
        src_ref=src, dst_ref=dst, send_sem=send, recv_sem=recv, device_id=device, device_id_type=MESH
    )


def columns_of(rows):
    n = rows.shape[0]
    wide = jnp.broadcast_to(rows, (n, ROWS, 128))
    lane = lax.broadcasted_iota(jnp.int32, (n, ROWS, 128), 2)
    sub = lax.broadcasted_iota(jnp.int32, (n, ROWS, 128), 1)
    return jnp.sum(jnp.where(lane == sub, wide, 0.0), axis=2, keepdims=True).reshape(n * ROWS, 1)


def kernel(
    cent, qry, mem, slot_in, count_in, pos_in, conc_o, lfin, fin,
    call, qall, pall, mx, mall, slx, sall, invall, score, wgt, peak, sums, peakb, sumsb, hitw, hitz, tile, colr, posb, posw,
    gsum, psum, slot, pos, tsend, trx, thz, tsum, ga, gra, ha, hza, acca, gb, grb, hb, hxb, accb,
    local, mx_s, mx_r, sx_s, sx_r, mz_s, mz_r, sz_s, sz_r, qz_s, qz_r, qx_s, qx_r, pz_s, pz_r, px_s, px_r,
    cy_s, cy_r, cc_s, cc_r, iv_s, iv_r, st_s, st_r, gx_s, gx_r, gz_s, gz_r, fn_s, fn_r, ln_s, ln_r,
    ux_s, ux_r, uz_s, uz_r, bz_s, bz_r, bx_s, bx_r,
):
    dp = lax.axis_index("dp")
    p = lax.axis_index("proto")
    z, x = dp // NX, dp % NX
    y, c = p // 2, p % 2

    def at_x(d):
        return (x + d) % NX

    def at_z(d):
        return (z + d) % NZ

    def at_p(d):
        return (p + d) % NP

    def dev_x(d):
        return {"dp": z * NX + at_x(d), "proto": p}

    def dev_z(d):
        return {"dp": at_z(d) * NX + x, "proto": p}

    def dev_xz(d, e):
        return {"dp": at_z(e) * NX + at_x(d), "proto": p}

    def dev_p(q):
        return {"dp": dp, "proto": q}

    barrier = pltpu.get_barrier_semaphore()
    both = sorted(
        ((d, e) for d in range(NX) for e in range(NZ) if d + e), key=lambda v: -min(v[0], NX - v[0]) - min(v[1], NZ - v[1])
    )
    up = ((y + 1) % 4) * 2 + c
    down = ((y + 3) % 4) * 2 + c
    far = ((y + 2) % 4) * 2 + c
    mate = y * 2 + (1 - c)
    for d in (4, 3, 5, 2, 6, 1, 7):
        pl.semaphore_signal(barrier, inc=1, device_id=dev_z(d), device_id_type=MESH)
    for d in (2, 1, 3):
        pl.semaphore_signal(barrier, inc=1, device_id=dev_x(d), device_id_type=MESH)
    for q in (up, down, mate):
        pl.semaphore_signal(barrier, inc=1, device_id=dev_p(q), device_id_type=MESH)

    used = lax.broadcasted_iota(jnp.int32, (ROWS, NX * NZ), 0) < count_in[pl.ds(p, 1), :]
    ids = jnp.where(used, slot_in[p], -1).astype(F32)
    ids = jnp.concatenate([ids, jnp.zeros((ROWS, 128 - NX * NZ), F32)], axis=1)
    ids = jnp.concatenate([ids, jnp.zeros((128 - ROWS, 128), F32)], axis=0).T
    for i in range(NX * NZ):
        slot[i // NX, i % NX] = ids[i : i + 1, :]
    wide = jnp.broadcast_to(pos_in[...].astype(F32), (8, 128))
    pos[...] = pltpu.roll(wide, (128 - p * ROWS) % 128, 1)[0:1, :]

    pl.semaphore_wait(barrier, NX + NZ + 1)

    sends = []

    def go(copy):
        copy.start()
        sends.append(copy)

    z_order = (4, 3, 5, 2, 6, 1, 7)
    half = CENT // 2
    top, bottom = pl.ds(0, half), pl.ds(half, half)
    cut = 176
    tops = (pl.ds(0, cut), pl.ds(cut, half - cut))
    bottoms = (pl.ds(half, cut), pl.ds(half + cut, half - cut))

    for d in z_order:
        go(remote(pos, pall.at[x, z], pz_s.at[d - 1], pz_r.at[d - 1], dev_z(d)))
    for d in z_order:
        go(remote(qry.at[p], qall.at[x, z], qz_s.at[d - 1], qz_r.at[d - 1], dev_z(d)))
    go(remote(cent.at[top], call.at[p, top], cy_s.at[0], cy_r.at[0], dev_p(up)))
    go(remote(cent.at[bottom], call.at[p, bottom], cy_s.at[3], cy_r.at[3], dev_p(down)))
    go(remote(cent.at[bottom], call.at[p, bottom], cy_s.at[1], cy_r.at[1], dev_p(up)))
    go(remote(cent.at[top], call.at[p, top], cy_s.at[2], cy_r.at[2], dev_p(down)))
    go(remote(cent, call.at[p], cc_s.at[0], cc_r.at[0], dev_p(mate)))
    for d in (1, 3, 2):
        go(remote(mem.at[:, at_x(d), p], mx.at[d - 1], mx_s.at[d - 1], mx_r.at[d - 1], dev_x(d)))
        go(remote(slot.at[:, at_x(d)], slx.at[d - 1], sx_s.at[d - 1], sx_r.at[d - 1], dev_x(d)))
    for d in z_order:
        go(remote(mem.at[at_z(d), x, p], mall.at[z, 0], mz_s.at[0, d - 1], mz_r.at[0, d - 1], dev_z(d)))
        go(remote(slot.at[at_z(d), x], sall.at[z, 0], sz_s.at[0, d - 1], sz_r.at[0, d - 1], dev_z(d)))
    own = (
        pltpu.make_async_copy(cent, call.at[p], local.at[0]),
        pltpu.make_async_copy(qry.at[p], qall.at[x, z], local.at[1]),
        pltpu.make_async_copy(mem.at[z, x, p], mall.at[z, 0], local.at[2]),
    )
    for copy in own:
        copy.start()
    pall[x, z] = pos[...]
    sall[z, 0] = slot[z, x]
    psum[...] = jnp.zeros_like(psum)

    for d in range(1, NZ):
        src = at_z(NZ - d)
        remote(pos, pall.at[x, src], pz_s.at[d - 1], pz_r.at[d - 1], dev_z(d)).wait_recv()
    for d in (2, 1, 3):
        go(remote(pall.at[x], pall.at[x], px_s.at[d - 1], px_r.at[d - 1], dev_x(d)))
    own[1].wait()
    for d in range(1, NZ):
        src = at_z(NZ - d)
        remote(qry.at[p], qall.at[x, src], qz_s.at[d - 1], qz_r.at[d - 1], dev_z(d)).wait_recv()
    for d in (2, 1, 3):
        go(remote(qall.at[x], qall.at[x], qx_s.at[d - 1], qx_r.at[d - 1], dev_x(d)))

    def members_on(d):
        remote(mem.at[:, x, p], mx.at[d - 1], mx_s.at[d - 1], mx_r.at[d - 1], dev_x(d)).wait_recv()
        remote(slot.at[:, x], slx.at[d - 1], sx_s.at[d - 1], sx_r.at[d - 1], dev_x(d)).wait_recv()
        for e in z_order:
            go(remote(mx.at[d - 1, at_z(e)], mall.at[z, d], mz_s.at[d, e - 1], mz_r.at[d, e - 1], dev_z(e)))
            go(remote(slx.at[d - 1, at_z(e)], sall.at[z, d], sz_s.at[d, e - 1], sz_r.at[d, e - 1], dev_z(e)))
        mall[z, d] = mx[d - 1, z]
        sall[z, d] = slx[d - 1, z]

    members_on(1)
    members_on(3)
    remote(cent.at[top], call.at[down, top], cy_s.at[0], cy_r.at[0], dev_p(up)).wait_recv()
    for i, r in enumerate(tops):
        go(remote(call.at[down, r], call.at[down, r], cy_s.at[4 + i], cy_r.at[4 + i], dev_p(up)))
    remote(cent.at[bottom], call.at[up, bottom], cy_s.at[3], cy_r.at[3], dev_p(down)).wait_recv()
    for i, r in enumerate(bottoms):
        go(remote(call.at[up, r], call.at[up, r], cy_s.at[6 + i], cy_r.at[6 + i], dev_p(down)))
    go(remote(call.at[down, top], call.at[down, top], cc_s.at[1], cc_r.at[1], dev_p(mate)))
    go(remote(call.at[up, bottom], call.at[up, bottom], cc_s.at[2], cc_r.at[2], dev_p(mate)))
    members_on(2)

    for d in range(1, NX):
        src = at_x(NX - d)
        remote(pall.at[x], pall.at[src], px_s.at[d - 1], px_r.at[d - 1], dev_x(d)).wait_recv()
    base = (dp * (NP * CENT)).astype(F32)
    posb[...] = jnp.broadcast_to(columns_of(pall[...].reshape(NX * NZ, 1, 128)) - base, (QS, 128))

    def positives(chunk):
        here = posb[:, 0:1] - (chunk * CENT).astype(F32)
        hot = lax.broadcasted_iota(jnp.int32, (QS, CENT), 1).astype(F32) == here
        psum[...] += jnp.dot(hot.astype(BF16), call[chunk], preferred_element_type=F32).reshape(psum.shape)

    def scores(chunk):
        def rows(i, carry):
            r = pl.ds(i * 2, 2)
            q = qall[r].reshape(2 * NZ * ROWS, WIDTH)
            score[chunk, pl.ds(i * 256, 256), :] = lax.dot_general(
                q, call[chunk], (((1,), (1,)), ((), ())), preferred_element_type=F32
            )
            return carry

        lax.fori_loop(0, 2, rows, 0)

    own[0].wait()
    positives(p)
    remote(cent, call.at[mate], cc_s.at[0], cc_r.at[0], dev_p(mate)).wait_recv()
    positives(mate)
    for d in range(1, NX):
        src = at_x(NX - d)
        remote(qall.at[x], qall.at[src], qx_s.at[d - 1], qx_r.at[d - 1], dev_x(d)).wait_recv()
    scores(p)
    scores(mate)
    remote(cent.at[bottom], call.at[down, bottom], cy_s.at[1], cy_r.at[1], dev_p(up)).wait_recv()
    go(remote(call.at[down, bottom], call.at[down, bottom], cc_s.at[3], cc_r.at[3], dev_p(mate)))
    remote(cent.at[top], call.at[up, top], cy_s.at[2], cy_r.at[2], dev_p(down)).wait_recv()
    go(remote(call.at[up, top], call.at[up, top], cc_s.at[4], cc_r.at[4], dev_p(mate)))
    flip = 1 - 2 * c
    scores(down)
    scores(up)
    remote(call.at[down, top], call.at[down + flip, top], cc_s.at[1], cc_r.at[1], dev_p(mate)).wait_recv()
    remote(call.at[down, bottom], call.at[down + flip, bottom], cc_s.at[3], cc_r.at[3], dev_p(mate)).wait_recv()
    scores(down + flip)
    remote(call.at[up, bottom], call.at[up + flip, bottom], cc_s.at[2], cc_r.at[2], dev_p(mate)).wait_recv()
    remote(call.at[up, top], call.at[up + flip, top], cc_s.at[4], cc_r.at[4], dev_p(mate)).wait_recv()
    scores(up + flip)

    own[2].wait()
    for e in range(1, NZ):
        src = at_z(NZ - e)
        for d in range(NX):
            remote(mem.at[z, x, p], mall.at[src, d], mz_s.at[d, e - 1], mz_r.at[d, e - 1], dev_z(e)).wait_recv()
            remote(slot.at[z, x], sall.at[src, d], sz_s.at[d, e - 1], sz_r.at[d, e - 1], dev_z(e)).wait_recv()
    which = columns_of(sall[...].reshape(NX * NZ, 1, 128))
    cluster = lax.broadcasted_iota(jnp.int32, (QS, CENT), 1).astype(F32)
    hot = which == cluster
    picked = jnp.dot(hot.astype(BF16), call[p], preferred_element_type=F32)
    gap = mall[...].reshape(QS, WIDTH).astype(F32) - picked
    dist = jnp.sqrt(jnp.sum(gap * gap, axis=1, keepdims=True) + 1e-06)
    total = jnp.sum(jnp.where(hot, dist, 0.0), axis=0, keepdims=True)
    count = jnp.sum(hot.astype(F32), axis=0, keepdims=True)
    conc = (total + 1.0) / ((count + 1.0) * jnp.log(count + 10.0))
    conc_o[...] = conc
    invall[p] = 1.0 / conc
    for d in (4, 3, 5, 2, 6, 1, 7):
        go(remote(invall.at[p], invall.at[p], iv_s.at[d - 1], iv_r.at[d - 1], dev_p(at_p(d))))

    positives(down)
    positives(up)
    positives(down + flip)
    positives(up + flip)
    for i in range(2):
        r = tops[i]
        remote(call.at[down, r], call.at[far, r], cy_s.at[4 + i], cy_r.at[4 + i], dev_p(up)).wait_recv()
        go(remote(call.at[far, r], call.at[far, r], cc_s.at[5 + i], cc_r.at[5 + i], dev_p(mate)))
        r = bottoms[i]
        remote(call.at[up, r], call.at[far, r], cy_s.at[6 + i], cy_r.at[6 + i], dev_p(down)).wait_recv()
        go(remote(call.at[far, r], call.at[far, r], cc_s.at[7 + i], cc_r.at[7 + i], dev_p(mate)))
    scores(far)
    for d in range(1, NP):
        src = at_p(NP - d)
        remote(invall.at[p], invall.at[src], iv_s.at[d - 1], iv_r.at[d - 1], dev_p(src)).wait_recv()

    step = 16

    def fold(v, op):
        return op(op(v[:, 0:128], v[:, 128:256]), op(v[:, 256:384], v[:, 384:512]))

    def soften(chunks, peak, sums):
        def largest(i, carry):
            r = pl.ds(pl.multiple_of(i * step, step), step)
            best = None
            for k in chunks:
                zed = score[k, r, :] * (invall[k] * LOG2E)
                best = zed if best is None else jnp.maximum(best, zed)
            peak[r, :] = fold(best, jnp.maximum)
            return carry

        lax.fori_loop(0, QS // step, largest, 0)
        peak[...] = jnp.broadcast_to(jnp.max(peak[...], axis=1, keepdims=True), (QS, 128))

        def soft(i, carry):
            r = pl.ds(pl.multiple_of(i * step, step), step)
            most = jnp.concatenate([peak[r, :]] * 4, axis=1)
            added = None
            for k in chunks:
                e = jnp.exp2(score[k, r, :] * (invall[k] * LOG2E) - most)
                wgt[k, r, :] = (e * invall[k]).astype(BF16)
                added = e if added is None else added + e
            sums[r, :] = fold(added, jnp.add)
            return carry

        lax.fori_loop(0, QS // step, soft, 0)

    early = (p, mate, down, up, down + flip, up + flip, far)
    last = far + flip
    soften(early, peak, sums)
    for i in range(4):
        r = (tops + bottoms)[i]
        remote(call.at[far, r], call.at[far + flip, r], cc_s.at[5 + i], cc_r.at[5 + i], dev_p(mate)).wait_recv()
    scores(last)
    soften((last,), peakb, sumsb)

    lane = lax.broadcasted_iota(jnp.int32, (QS, 128), 1)
    most = jnp.maximum(peak[...], peakb[...])
    peak[...] = jnp.exp2(peak[...] - most)
    peakb[...] = jnp.exp2(peakb[...] - most)
    summed = jnp.sum(sums[...] * peak[...] + sumsb[...] * peakb[...], axis=1, keepdims=True)
    mine = jnp.where(lane == 0, most, summed).T
    tile[x, z] = jnp.concatenate([mine[i : i + 1, b * 128 : (b + 1) * 128] for i in range(2) for b in range(NX)], axis=0)
    for d, e in both:
        go(remote(tile.at[x, z], tile.at[x, z], st_s.at[d * NZ + e], st_r.at[d * NZ + e], dev_xz(d, e)))

    def weigh(i, carry):
        r = pl.ds(pl.multiple_of(i * 256, 256), 256)
        out = None
        for k in early:
            term = jnp.dot(wgt[k, r, :], call[k], preferred_element_type=F32)
            out = term if out is None else out + term
        late = jnp.dot(wgt[last, r, :], call[last], preferred_element_type=F32)
        for s in range(0, 256, step):
            q = pl.ds(pl.multiple_of(i * 256 + s, step), step)
            here = jnp.concatenate([posb[q, :]] * 4, axis=1)
            col = lax.broadcasted_iota(jnp.int32, (step, CENT), 1).astype(F32)
            weight, logit = None, None
            for k in range(NP):
                hit = col == here - float(k * CENT)
                a = jnp.where(hit, jnp.broadcast_to(invall[k], (step, CENT)), 0.0)
                b = jnp.where(hit, score[k, q, :], 0.0)
                weight = a if weight is None else weight + a
                logit = b if logit is None else logit + b
            hitw[q, :] = fold(weight, jnp.add)
            hitz[q, :] = fold(logit, jnp.add)
        out = out * peak[r, 0:1] + late * peakb[r, 0:1]
        gsum[pl.ds(i * 2, 2)] = out.reshape(2, NZ, ROWS, WIDTH)
        return carry

    lax.fori_loop(0, 2, weigh, 0)
    scale = jnp.sum(hitw[...], axis=1, keepdims=True)
    target = jnp.sum(hitz[...], axis=1, keepdims=True) * scale
    posw[...] = jnp.broadcast_to(scale, (QS, 128)).reshape(posw.shape)
    turned = jnp.broadcast_to(target, (QS, 128)).T[0:8, :]
    for b in range(NX):
        tsend[b] = turned[:, b * 128 : (b + 1) * 128]
    for d in (2, 1, 3):
        go(remote(tsend.at[at_x(d)], trx.at[d - 1], ux_s.at[d - 1], ux_r.at[d - 1], dev_x(d)))
    positives(far)
    positives(last)

    for d, e in both:
        src = (at_x(NX - d), at_z(NZ - e))
        remote(tile.at[x, z], tile.at[src], st_s.at[d * NZ + e], st_r.at[d * NZ + e], dev_xz(d, e)).wait_recv()
    tiles = tile[...].reshape(NX * NZ, 8, 128)
    best = jnp.max(tiles[:, 0:NX], axis=0)
    added = jnp.sum(tiles[:, NX:8] * jnp.exp2(tiles[:, 0:NX] - best[None]), axis=0)

    def flat(v):
        return jnp.concatenate([v[b : b + 1, :] for b in range(NX)], axis=1)

    share = flat(jnp.exp2(tile[x, z][0:NX] - best) / added)
    total_log = flat(best * LN2 + jnp.log(added))
    colr[...] = jnp.concatenate([share, total_log, jnp.zeros((126, QS), F32)], axis=0).T.reshape(colr.shape)

    ca, cb = pl.ds(0, CA), pl.ds(CA, CB)

    def part(at, cols):
        return gsum[at + (slice(None), cols)] * colr[at][..., 0:1] - psum[at + (slice(None), cols)] * posw[at][..., 0:1]

    def part_x(b):
        return part((b, slice(None)), ca)

    def part_z(b):
        return part((slice(None), b), cb)

    ga[1] = part_x(at_x(2)).astype(BF16)
    go(remote(ga.at[1], gra.at[1], gx_s.at[1], gx_r.at[1], dev_x(2)))
    for d in z_order[:3]:
        gb[d - 1] = part_z(at_z(d)).astype(BF16)
        go(remote(gb.at[d - 1], grb.at[d - 1], bz_s.at[d - 1], bz_r.at[d - 1], dev_z(d)))
    for d in (1, 3):
        ga[d - 1] = part_x(at_x(d)).astype(BF16)
        go(remote(ga.at[d - 1], gra.at[d - 1], gx_s.at[d - 1], gx_r.at[d - 1], dev_x(d)))
    for d in z_order[3:]:
        gb[d - 1] = part_z(at_z(d)).astype(BF16)
        go(remote(gb.at[d - 1], grb.at[d - 1], bz_s.at[d - 1], bz_r.at[d - 1], dev_z(d)))
    told = tsend[x]
    for d in (1, 3, 2):
        remote(tsend.at[x], trx.at[d - 1], ux_s.at[d - 1], ux_r.at[d - 1], dev_x(d)).wait_recv()
        told = told + trx[d - 1]
    tsum[...] = told
    for d in z_order:
        go(remote(tsum, thz.at[d - 1], uz_s.at[d - 1], uz_r.at[d - 1], dev_z(d)))
    acca[...] = part_x(x)
    accb[...] = part_z(z)
    for d in (1, 3, 2):
        remote(ga.at[d - 1], gra.at[d - 1], gx_s.at[d - 1], gx_r.at[d - 1], dev_x(d)).wait_recv()
        acca[...] += gra[d - 1].astype(F32)
    ha[...] = acca[...].astype(BF16)
    for d in z_order:
        go(remote(ha.at[at_z(d)], hza.at[d - 1], gz_s.at[d - 1], gz_r.at[d - 1], dev_z(d)))
    for d in range(1, NZ):
        remote(gb.at[d - 1], grb.at[d - 1], bz_s.at[d - 1], bz_r.at[d - 1], dev_z(d)).wait_recv()
        accb[...] += grb[d - 1].astype(F32)
    hb[...] = accb[...].astype(BF16)
    for d in (2, 1, 3):
        go(remote(hb.at[at_x(d)], hxb.at[d - 1], bx_s.at[d - 1], bx_r.at[d - 1], dev_x(d)))
    for d in range(1, NZ):
        remote(tsum, thz.at[d - 1], uz_s.at[d - 1], uz_r.at[d - 1], dev_z(d)).wait_recv()
        told = told + thz[d - 1]
    peak[0:128, :] = jnp.concatenate([told, jnp.zeros((120, 128), F32)], axis=0).T
    z_rows = pl.ds(pl.multiple_of(z * ROWS, ROWS), ROWS)
    lfin[p] = jnp.broadcast_to(colr[x, z][:, 1:2] - peak[z_rows, 0:1], (ROWS, 128))
    for d in (4, 3, 5, 2, 6, 1, 7):
        go(remote(lfin.at[p], lfin.at[p], ln_s.at[d - 1], ln_r.at[d - 1], dev_p(at_p(d))))
    grad_b = accb[x]
    for d in (1, 3, 2):
        remote(hb.at[x], hxb.at[d - 1], bx_s.at[d - 1], bx_r.at[d - 1], dev_x(d)).wait_recv()
        grad_b = grad_b + hxb[d - 1].astype(F32)
    grad_a = acca[z]
    for d in range(1, NZ):
        remote(ha.at[z], hza.at[d - 1], gz_s.at[d - 1], gz_r.at[d - 1], dev_z(d)).wait_recv()
        grad_a = grad_a + hza[d - 1].astype(F32)

    fin[p, :, ca] = grad_a.astype(BF16)
    fin[p, :, cb] = grad_b.astype(BF16)
    for d in (4, 3, 5, 2, 6, 1, 7):
        go(remote(fin.at[p], fin.at[p], fn_s.at[d - 1], fn_r.at[d - 1], dev_p(at_p(d))))
    for d in range(1, NP):
        src = at_p(NP - d)
        remote(lfin.at[p], lfin.at[src], ln_s.at[d - 1], ln_r.at[d - 1], dev_p(src)).wait_recv()
        remote(fin.at[p], fin.at[src], fn_s.at[d - 1], fn_r.at[d - 1], dev_p(src)).wait_recv()
    for copy in sends:
        copy.wait_send()


def finish(conc, lfin, fin, conc_o, loss_o, grad_o):
    conc_o[...] = conc[...]
    loss_o[...] = lfin[...].reshape(NP * ROWS, 128).T[0:1, :]
    grad_o[...] = fin[...].reshape(NP * ROWS, WIDTH)


def on_device(centroids, queries, positive, members, member_slot, block_count):
    vmem = pltpu.VMEM
    dma = pltpu.SemaphoreType.DMA
    sems = []
    for shape in (
        (NX - 1,), (NX - 1,), (NX, NZ - 1), (NX, NZ - 1), (NZ - 1,), (NX - 1,), (NZ - 1,), (NX - 1,),
        (8,), (9,), (NP - 1,), (NX * NZ,), (NX - 1,), (NZ - 1,), (NP - 1,), (NP - 1,),
        (NX - 1,), (NZ - 1,), (NZ - 1,), (NX - 1,),
    ):
        sems += [dma(shape), dma(shape)]
    whole = pl.BlockSpec(memory_space=vmem)
    conc, lfin, fin = pl.pallas_call(
        kernel,
        out_shape=(
            jax.ShapeDtypeStruct((1, CENT), F32),
            jax.ShapeDtypeStruct((NP, ROWS, 128), F32),
            jax.ShapeDtypeStruct((NP, ROWS, WIDTH), BF16),
        ),
        in_specs=[pl.BlockSpec(memory_space=pl.ANY)] * 3 + [whole] * 3,
        out_specs=(whole,) * 3,
        scratch_shapes=[
            vmem((NP, CENT, WIDTH), BF16),
            vmem((NX, NZ, ROWS, WIDTH), BF16),
            vmem((NX, NZ, 1, 128), F32),
            vmem((NX - 1, NZ, ROWS, WIDTH), BF16),
            vmem((NZ, NX, ROWS, WIDTH), BF16),
            vmem((NX - 1, NZ, 1, 128), F32),
            vmem((NZ, NX, 1, 128), F32),
            vmem((NP, 1, CENT), F32),
            vmem((NP, QS, CENT), F32),
            vmem((NP, QS, CENT), BF16),
            vmem((QS, 128), F32),
            vmem((QS, 128), F32),
            vmem((QS, 128), F32),
            vmem((QS, 128), F32),
            vmem((QS, 128), F32),
            vmem((QS, 128), F32),
            vmem((NX, NZ, 8, 128), F32),
            vmem((NX, NZ, ROWS, 128), F32),
            vmem((QS, 128), F32),
            vmem((NX, NZ, ROWS, 128), F32),
            vmem((NX, NZ, ROWS, WIDTH), F32),
            vmem((NX, NZ, ROWS, WIDTH), F32),
            vmem((NZ, NX, 1, 128), F32),
            vmem((1, 128), F32),
            vmem((NX, 8, 128), F32),
            vmem((NX - 1, 8, 128), F32),
            vmem((NZ - 1, 8, 128), F32),
            vmem((8, 128), F32),
            vmem((NX - 1, NZ, ROWS, CA), BF16),
            vmem((NX - 1, NZ, ROWS, CA), BF16),
            vmem((NZ, ROWS, CA), BF16),
            vmem((NZ - 1, ROWS, CA), BF16),
            vmem((NZ, ROWS, CA), F32),
            vmem((NZ - 1, NX, ROWS, CB), BF16),
            vmem((NZ - 1, NX, ROWS, CB), BF16),
            vmem((NX, ROWS, CB), BF16),
            vmem((NX - 1, ROWS, CB), BF16),
            vmem((NX, ROWS, CB), F32),
            dma((3,)),
            *sems,
        ],
        compiler_params=pltpu.CompilerParams(
            collective_id=0, has_side_effects=True, vmem_limit_bytes=56 * 1024 * 1024
        ),
        name="protonce",
    )(
        centroids,
        queries.reshape(NP, ROWS, WIDTH),
        members.reshape(NZ, NX, NP, ROWS, WIDTH),
        member_slot.transpose(0, 2, 3, 1).reshape(NP, ROWS, NX * NZ),
        block_count.transpose(0, 2, 1).reshape(NP, NX * NZ),
        positive.reshape(1, NP * ROWS),
    )
    conc, loss, grad = pl.pallas_call(
        finish,
        out_shape=(
            jax.ShapeDtypeStruct((1, CENT), F32),
            jax.ShapeDtypeStruct((1, NP * ROWS), F32),
            jax.ShapeDtypeStruct((NP * ROWS, WIDTH), BF16),
        ),
        in_specs=[whole] * 3,
        out_specs=(whole,) * 3,
        name="finish",
    )(conc, lfin, fin)
    return conc.reshape(CENT), loss.reshape(NP * ROWS), grad


def solution(mesh):
    placed = (
        P(("dp", "proto"), None),
        P("dp", None),
        P("dp"),
        P("dp", None, None, None, None),
        P("dp", None, None, None),
        P("dp", None, None),
    )
    return jax.shard_map(
        on_device,
        mesh=mesh,
        in_specs=placed,
        out_specs=(P(("dp", "proto")), P("dp"), P("dp", None)),
        check_vma=False,
    )
```

```python
import jax
import jax.numpy as jnp
from jax import lax
from jax.experimental import pallas as pl
from jax.experimental.pallas import tpu as pltpu
from jax.sharding import PartitionSpec as P

MESH = pl.DeviceIdType.MESH
NX, NZ, NP = 4, 8, 8
ROWS, WIDTH, CENT = 16, 768, 512
QS = NX * NZ * ROWS
CA = 512
CB = WIDTH - CA
F32, BF16 = jnp.float32, jnp.bfloat16
LOG2E, LN2 = 1.4426950408889634, 0.6931471805599453


def remote(src, dst, send, recv, device):
    return pltpu.make_async_remote_copy(
        src_ref=src, dst_ref=dst, send_sem=send, recv_sem=recv, device_id=device, device_id_type=MESH
    )


def columns_of(rows):
    n = rows.shape[0]
    wide = jnp.broadcast_to(rows, (n, ROWS, 128))
    lane = lax.broadcasted_iota(jnp.int32, (n, ROWS, 128), 2)
    sub = lax.broadcasted_iota(jnp.int32, (n, ROWS, 128), 1)
    return jnp.sum(jnp.where(lane == sub, wide, 0.0), axis=2, keepdims=True).reshape(n * ROWS, 1)


def kernel(
    cent, qry, mem, slot_hbm, count_hbm, pos_hbm, conc_o, lfin, fin,
    slot_in, count_in, pos_in, call, qall, pall, mx, mall, slx, sall, invall, score, wgt, peak, sums, peakb, sumsb, hitw, hitz, tile, colr, posb, posw,
    gsum, psum, slot, pos, tsend, trx, thz, tsum, ga, gra, ha, hza, acca, gb, grb, hb, hxb, accb,
    local, mx_s, mx_r, sx_s, sx_r, mz_s, mz_r, sz_s, sz_r, qz_s, qz_r, qx_s, qx_r, pz_s, pz_r, px_s, px_r,
    cy_s, cy_r, cc_s, cc_r, iv_s, iv_r, st_s, st_r, gx_s, gx_r, gz_s, gz_r, fn_s, fn_r, ln_s, ln_r,
    ux_s, ux_r, uz_s, uz_r, bz_s, bz_r, bx_s, bx_r,
):
    dp = lax.axis_index("dp")
    p = lax.axis_index("proto")
    z, x = dp // NX, dp % NX
    y, c = p // 2, p % 2

    def at_x(d):
        return (x + d) % NX

    def at_z(d):
        return (z + d) % NZ

    def at_p(d):
        return (p + d) % NP

    def dev_x(d):
        return {"dp": z * NX + at_x(d), "proto": p}

    def dev_z(d):
        return {"dp": at_z(d) * NX + x, "proto": p}

    def dev_xz(d, e):
        return {"dp": at_z(e) * NX + at_x(d), "proto": p}

    def dev_p(q):
        return {"dp": dp, "proto": q}

    barrier = pltpu.get_barrier_semaphore()
    both = sorted(
        ((d, e) for d in range(NX) for e in range(NZ) if d + e), key=lambda v: -min(v[0], NX - v[0]) - min(v[1], NZ - v[1])
    )
    up = ((y + 1) % 4) * 2 + c
    down = ((y + 3) % 4) * 2 + c
    far = ((y + 2) % 4) * 2 + c
    mate = y * 2 + (1 - c)
    for d in (4, 3, 5, 2, 6, 1, 7):
        pl.semaphore_signal(barrier, inc=1, device_id=dev_z(d), device_id_type=MESH)
    for d in (2, 1, 3):
        pl.semaphore_signal(barrier, inc=1, device_id=dev_x(d), device_id_type=MESH)
    for q in (up, down, mate):
        pl.semaphore_signal(barrier, inc=1, device_id=dev_p(q), device_id_type=MESH)

    loads = (
        pltpu.make_async_copy(slot_hbm.at[p], slot_in, local.at[3]),
        pltpu.make_async_copy(count_hbm, count_in, local.at[4]),
        pltpu.make_async_copy(pos_hbm, pos_in, local.at[5]),
    )
    for copy in loads:
        copy.start()
    for copy in loads:
        copy.wait()
    used = lax.broadcasted_iota(jnp.int32, (ROWS, NX * NZ), 0) < count_in[pl.ds(p, 1), :]
    ids = jnp.where(used, slot_in[...], -1).astype(F32)
    ids = jnp.concatenate([ids, jnp.zeros((ROWS, 128 - NX * NZ), F32)], axis=1)
    ids = jnp.concatenate([ids, jnp.zeros((128 - ROWS, 128), F32)], axis=0).T
    for i in range(NX * NZ):
        slot[i // NX, i % NX] = ids[i : i + 1, :]
    wide = jnp.broadcast_to(pos_in[...].astype(F32), (8, 128))
    pos[...] = pltpu.roll(wide, (128 - p * ROWS) % 128, 1)[0:1, :]

    pl.semaphore_wait(barrier, NX + NZ + 1)

    sends = []

    def go(copy):
        copy.start()
        sends.append(copy)

    z_order = (4, 3, 5, 2, 6, 1, 7)
    half = CENT // 2
    top, bottom = pl.ds(0, half), pl.ds(half, half)
    cut = 176
    tops = (pl.ds(0, cut), pl.ds(cut, half - cut))
    bottoms = (pl.ds(half, cut), pl.ds(half + cut, half - cut))

    for d in z_order:
        go(remote(pos, pall.at[x, z], pz_s.at[d - 1], pz_r.at[d - 1], dev_z(d)))
    for d in z_order:
        go(remote(qry.at[p], qall.at[x, z], qz_s.at[d - 1], qz_r.at[d - 1], dev_z(d)))
    go(remote(cent.at[top], call.at[p, top], cy_s.at[0], cy_r.at[0], dev_p(up)))
    go(remote(cent.at[bottom], call.at[p, bottom], cy_s.at[3], cy_r.at[3], dev_p(down)))
    go(remote(cent.at[bottom], call.at[p, bottom], cy_s.at[1], cy_r.at[1], dev_p(up)))
    go(remote(cent.at[top], call.at[p, top], cy_s.at[2], cy_r.at[2], dev_p(down)))
    go(remote(cent, call.at[p], cc_s.at[0], cc_r.at[0], dev_p(mate)))
    for d in (1, 3, 2):
        go(remote(mem.at[:, at_x(d), p], mx.at[d - 1], mx_s.at[d - 1], mx_r.at[d - 1], dev_x(d)))
        go(remote(slot.at[:, at_x(d)], slx.at[d - 1], sx_s.at[d - 1], sx_r.at[d - 1], dev_x(d)))
    for d in z_order:
        go(remote(mem.at[at_z(d), x, p], mall.at[z, 0], mz_s.at[0, d - 1], mz_r.at[0, d - 1], dev_z(d)))
        go(remote(slot.at[at_z(d), x], sall.at[z, 0], sz_s.at[0, d - 1], sz_r.at[0, d - 1], dev_z(d)))
    own = (
        pltpu.make_async_copy(cent, call.at[p], local.at[0]),
        pltpu.make_async_copy(qry.at[p], qall.at[x, z], local.at[1]),
        pltpu.make_async_copy(mem.at[z, x, p], mall.at[z, 0], local.at[2]),
    )
    for copy in own:
        copy.start()
    pall[x, z] = pos[...]
    sall[z, 0] = slot[z, x]
    psum[...] = jnp.zeros_like(psum)

    for d in range(1, NZ):
        src = at_z(NZ - d)
        remote(pos, pall.at[x, src], pz_s.at[d - 1], pz_r.at[d - 1], dev_z(d)).wait_recv()
    for d in (2, 1, 3):
        go(remote(pall.at[x], pall.at[x], px_s.at[d - 1], px_r.at[d - 1], dev_x(d)))
    own[1].wait()
    for d in range(1, NZ):
        src = at_z(NZ - d)
        remote(qry.at[p], qall.at[x, src], qz_s.at[d - 1], qz_r.at[d - 1], dev_z(d)).wait_recv()
    for d in (2, 1, 3):
        go(remote(qall.at[x], qall.at[x], qx_s.at[d - 1], qx_r.at[d - 1], dev_x(d)))

    def members_on(d):
        remote(mem.at[:, x, p], mx.at[d - 1], mx_s.at[d - 1], mx_r.at[d - 1], dev_x(d)).wait_recv()
        remote(slot.at[:, x], slx.at[d - 1], sx_s.at[d - 1], sx_r.at[d - 1], dev_x(d)).wait_recv()
        for e in z_order:
            go(remote(mx.at[d - 1, at_z(e)], mall.at[z, d], mz_s.at[d, e - 1], mz_r.at[d, e - 1], dev_z(e)))
            go(remote(slx.at[d - 1, at_z(e)], sall.at[z, d], sz_s.at[d, e - 1], sz_r.at[d, e - 1], dev_z(e)))
        mall[z, d] = mx[d - 1, z]
        sall[z, d] = slx[d - 1, z]

    members_on(1)
    members_on(3)
    remote(cent.at[top], call.at[down, top], cy_s.at[0], cy_r.at[0], dev_p(up)).wait_recv()
    for i, r in enumerate(tops):
        go(remote(call.at[down, r], call.at[down, r], cy_s.at[4 + i], cy_r.at[4 + i], dev_p(up)))
    remote(cent.at[bottom], call.at[up, bottom], cy_s.at[3], cy_r.at[3], dev_p(down)).wait_recv()
    for i, r in enumerate(bottoms):
        go(remote(call.at[up, r], call.at[up, r], cy_s.at[6 + i], cy_r.at[6 + i], dev_p(down)))
    go(remote(call.at[down, top], call.at[down, top], cc_s.at[1], cc_r.at[1], dev_p(mate)))
    go(remote(call.at[up, bottom], call.at[up, bottom], cc_s.at[2], cc_r.at[2], dev_p(mate)))
    members_on(2)

    for d in range(1, NX):
        src = at_x(NX - d)
        remote(pall.at[x], pall.at[src], px_s.at[d - 1], px_r.at[d - 1], dev_x(d)).wait_recv()
    base = (dp * (NP * CENT)).astype(F32)
    posb[...] = jnp.broadcast_to(columns_of(pall[...].reshape(NX * NZ, 1, 128)) - base, (QS, 128))

    def positives(chunk):
        here = posb[:, 0:1] - (chunk * CENT).astype(F32)
        hot = lax.broadcasted_iota(jnp.int32, (QS, CENT), 1).astype(F32) == here
        psum[...] += jnp.dot(hot.astype(BF16), call[chunk], preferred_element_type=F32).reshape(psum.shape)

    def scores(chunk):
        def rows(i, carry):
            r = pl.ds(i * 2, 2)
            q = qall[r].reshape(2 * NZ * ROWS, WIDTH)
            score[chunk, pl.ds(i * 256, 256), :] = lax.dot_general(
                q, call[chunk], (((1,), (1,)), ((), ())), preferred_element_type=F32
            )
            return carry

        lax.fori_loop(0, 2, rows, 0)

    own[0].wait()
    positives(p)
    remote(cent, call.at[mate], cc_s.at[0], cc_r.at[0], dev_p(mate)).wait_recv()
    positives(mate)
    for d in range(1, NX):
        src = at_x(NX - d)
        remote(qall.at[x], qall.at[src], qx_s.at[d - 1], qx_r.at[d - 1], dev_x(d)).wait_recv()
    scores(p)
    scores(mate)
    remote(cent.at[bottom], call.at[down, bottom], cy_s.at[1], cy_r.at[1], dev_p(up)).wait_recv()
    go(remote(call.at[down, bottom], call.at[down, bottom], cc_s.at[3], cc_r.at[3], dev_p(mate)))
    remote(cent.at[top], call.at[up, top], cy_s.at[2], cy_r.at[2], dev_p(down)).wait_recv()
    go(remote(call.at[up, top], call.at[up, top], cc_s.at[4], cc_r.at[4], dev_p(mate)))
    flip = 1 - 2 * c
    scores(down)
    scores(up)
    remote(call.at[down, top], call.at[down + flip, top], cc_s.at[1], cc_r.at[1], dev_p(mate)).wait_recv()
    remote(call.at[down, bottom], call.at[down + flip, bottom], cc_s.at[3], cc_r.at[3], dev_p(mate)).wait_recv()
    scores(down + flip)
    remote(call.at[up, bottom], call.at[up + flip, bottom], cc_s.at[2], cc_r.at[2], dev_p(mate)).wait_recv()
    remote(call.at[up, top], call.at[up + flip, top], cc_s.at[4], cc_r.at[4], dev_p(mate)).wait_recv()
    scores(up + flip)

    own[2].wait()
    for e in range(1, NZ):
        src = at_z(NZ - e)
        for d in range(NX):
            remote(mem.at[z, x, p], mall.at[src, d], mz_s.at[d, e - 1], mz_r.at[d, e - 1], dev_z(e)).wait_recv()
            remote(slot.at[z, x], sall.at[src, d], sz_s.at[d, e - 1], sz_r.at[d, e - 1], dev_z(e)).wait_recv()
    which = columns_of(sall[...].reshape(NX * NZ, 1, 128))
    cluster = lax.broadcasted_iota(jnp.int32, (QS, CENT), 1).astype(F32)
    hot = which == cluster
    picked = jnp.dot(hot.astype(BF16), call[p], preferred_element_type=F32)
    gap = mall[...].reshape(QS, WIDTH).astype(F32) - picked
    dist = jnp.sqrt(jnp.sum(gap * gap, axis=1, keepdims=True) + 1e-06)
    total = jnp.sum(jnp.where(hot, dist, 0.0), axis=0, keepdims=True)
    count = jnp.sum(hot.astype(F32), axis=0, keepdims=True)
    conc = (total + 1.0) / ((count + 1.0) * jnp.log(count + 10.0))
    conc_o[...] = conc
    invall[p] = 1.0 / conc
    for d in (4, 3, 5, 2, 6, 1, 7):
        go(remote(invall.at[p], invall.at[p], iv_s.at[d - 1], iv_r.at[d - 1], dev_p(at_p(d))))

    positives(down)
    positives(up)
    positives(down + flip)
    positives(up + flip)
    for i in range(2):
        r = tops[i]
        remote(call.at[down, r], call.at[far, r], cy_s.at[4 + i], cy_r.at[4 + i], dev_p(up)).wait_recv()
        go(remote(call.at[far, r], call.at[far, r], cc_s.at[5 + i], cc_r.at[5 + i], dev_p(mate)))
        r = bottoms[i]
        remote(call.at[up, r], call.at[far, r], cy_s.at[6 + i], cy_r.at[6 + i], dev_p(down)).wait_recv()
        go(remote(call.at[far, r], call.at[far, r], cc_s.at[7 + i], cc_r.at[7 + i], dev_p(mate)))
    scores(far)
    for d in range(1, NP):
        src = at_p(NP - d)
        remote(invall.at[p], invall.at[src], iv_s.at[d - 1], iv_r.at[d - 1], dev_p(src)).wait_recv()

    step = 16

    def fold(v, op):
        return op(op(v[:, 0:128], v[:, 128:256]), op(v[:, 256:384], v[:, 384:512]))

    def soften(chunks, peak, sums):
        def largest(i, carry):
            r = pl.ds(pl.multiple_of(i * step, step), step)
            best = None
            for k in chunks:
                zed = score[k, r, :] * (invall[k] * LOG2E)
                best = zed if best is None else jnp.maximum(best, zed)
            peak[r, :] = fold(best, jnp.maximum)
            return carry

        lax.fori_loop(0, QS // step, largest, 0)
        peak[...] = jnp.broadcast_to(jnp.max(peak[...], axis=1, keepdims=True), (QS, 128))

        def soft(i, carry):
            r = pl.ds(pl.multiple_of(i * step, step), step)
            most = jnp.concatenate([peak[r, :]] * 4, axis=1)
            added = None
            for k in chunks:
                e = jnp.exp2(score[k, r, :] * (invall[k] * LOG2E) - most)
                wgt[k, r, :] = (e * invall[k]).astype(BF16)
                added = e if added is None else added + e
            sums[r, :] = fold(added, jnp.add)
            return carry

        lax.fori_loop(0, QS // step, soft, 0)

    early = (p, mate, down, up, down + flip, up + flip, far)
    last = far + flip
    soften(early, peak, sums)
    for i in range(4):
        r = (tops + bottoms)[i]
        remote(call.at[far, r], call.at[far + flip, r], cc_s.at[5 + i], cc_r.at[5 + i], dev_p(mate)).wait_recv()
    scores(last)
    soften((last,), peakb, sumsb)

    lane = lax.broadcasted_iota(jnp.int32, (QS, 128), 1)
    most = jnp.maximum(peak[...], peakb[...])
    peak[...] = jnp.exp2(peak[...] - most)
    peakb[...] = jnp.exp2(peakb[...] - most)
    summed = jnp.sum(sums[...] * peak[...] + sumsb[...] * peakb[...], axis=1, keepdims=True)
    mine = jnp.where(lane == 0, most, summed).T
    tile[x, z] = jnp.concatenate([mine[i : i + 1, b * 128 : (b + 1) * 128] for i in range(2) for b in range(NX)], axis=0)
    for d, e in both:
        go(remote(tile.at[x, z], tile.at[x, z], st_s.at[d * NZ + e], st_r.at[d * NZ + e], dev_xz(d, e)))

    def weigh(i, carry):
        r = pl.ds(pl.multiple_of(i * 256, 256), 256)
        out = None
        for k in early:
            term = jnp.dot(wgt[k, r, :], call[k], preferred_element_type=F32)
            out = term if out is None else out + term
        late = jnp.dot(wgt[last, r, :], call[last], preferred_element_type=F32)
        for s in range(0, 256, step):
            q = pl.ds(pl.multiple_of(i * 256 + s, step), step)
            here = jnp.concatenate([posb[q, :]] * 4, axis=1)
            col = lax.broadcasted_iota(jnp.int32, (step, CENT), 1).astype(F32)
            weight, logit = None, None
            for k in range(NP):
                hit = col == here - float(k * CENT)
                a = jnp.where(hit, jnp.broadcast_to(invall[k], (step, CENT)), 0.0)
                b = jnp.where(hit, score[k, q, :], 0.0)
                weight = a if weight is None else weight + a
                logit = b if logit is None else logit + b
            hitw[q, :] = fold(weight, jnp.add)
            hitz[q, :] = fold(logit, jnp.add)
        out = out * peak[r, 0:1] + late * peakb[r, 0:1]
        gsum[pl.ds(i * 2, 2)] = out.reshape(2, NZ, ROWS, WIDTH)
        return carry

    lax.fori_loop(0, 2, weigh, 0)
    scale = jnp.sum(hitw[...], axis=1, keepdims=True)
    target = jnp.sum(hitz[...], axis=1, keepdims=True) * scale
    posw[...] = jnp.broadcast_to(scale, (QS, 128)).reshape(posw.shape)
    turned = jnp.broadcast_to(target, (QS, 128)).T[0:8, :]
    for b in range(NX):
        tsend[b] = turned[:, b * 128 : (b + 1) * 128]
    for d in (2, 1, 3):
        go(remote(tsend.at[at_x(d)], trx.at[d - 1], ux_s.at[d - 1], ux_r.at[d - 1], dev_x(d)))
    positives(far)
    positives(last)

    for d, e in both:
        src = (at_x(NX - d), at_z(NZ - e))
        remote(tile.at[x, z], tile.at[src], st_s.at[d * NZ + e], st_r.at[d * NZ + e], dev_xz(d, e)).wait_recv()
    tiles = tile[...].reshape(NX * NZ, 8, 128)
    best = jnp.max(tiles[:, 0:NX], axis=0)
    added = jnp.sum(tiles[:, NX:8] * jnp.exp2(tiles[:, 0:NX] - best[None]), axis=0)

    def flat(v):
        return jnp.concatenate([v[b : b + 1, :] for b in range(NX)], axis=1)

    share = flat(jnp.exp2(tile[x, z][0:NX] - best) / added)
    total_log = flat(best * LN2 + jnp.log(added))
    colr[...] = jnp.concatenate([share, total_log, jnp.zeros((126, QS), F32)], axis=0).T.reshape(colr.shape)

    ca, cb = pl.ds(0, CA), pl.ds(CA, CB)

    def part(at, cols):
        return gsum[at + (slice(None), cols)] * colr[at][..., 0:1] - psum[at + (slice(None), cols)] * posw[at][..., 0:1]

    def part_x(b):
        return part((b, slice(None)), ca)

    def part_z(b):
        return part((slice(None), b), cb)

    ga[1] = part_x(at_x(2)).astype(BF16)
    go(remote(ga.at[1], gra.at[1], gx_s.at[1], gx_r.at[1], dev_x(2)))
    for d in z_order[:3]:
        gb[d - 1] = part_z(at_z(d)).astype(BF16)
        go(remote(gb.at[d - 1], grb.at[d - 1], bz_s.at[d - 1], bz_r.at[d - 1], dev_z(d)))
    for d in (1, 3):
        ga[d - 1] = part_x(at_x(d)).astype(BF16)
        go(remote(ga.at[d - 1], gra.at[d - 1], gx_s.at[d - 1], gx_r.at[d - 1], dev_x(d)))
    for d in z_order[3:]:
        gb[d - 1] = part_z(at_z(d)).astype(BF16)
        go(remote(gb.at[d - 1], grb.at[d - 1], bz_s.at[d - 1], bz_r.at[d - 1], dev_z(d)))
    told = tsend[x]
    for d in (1, 3, 2):
        remote(tsend.at[x], trx.at[d - 1], ux_s.at[d - 1], ux_r.at[d - 1], dev_x(d)).wait_recv()
        told = told + trx[d - 1]
    tsum[...] = told
    for d in z_order:
        go(remote(tsum, thz.at[d - 1], uz_s.at[d - 1], uz_r.at[d - 1], dev_z(d)))
    acca[...] = part_x(x)
    accb[...] = part_z(z)
    for d in (1, 3, 2):
        remote(ga.at[d - 1], gra.at[d - 1], gx_s.at[d - 1], gx_r.at[d - 1], dev_x(d)).wait_recv()
        acca[...] += gra[d - 1].astype(F32)
    ha[...] = acca[...].astype(BF16)
    for d in z_order:
        go(remote(ha.at[at_z(d)], hza.at[d - 1], gz_s.at[d - 1], gz_r.at[d - 1], dev_z(d)))
    for d in range(1, NZ):
        remote(gb.at[d - 1], grb.at[d - 1], bz_s.at[d - 1], bz_r.at[d - 1], dev_z(d)).wait_recv()
        accb[...] += grb[d - 1].astype(F32)
    hb[...] = accb[...].astype(BF16)
    for d in (2, 1, 3):
        go(remote(hb.at[at_x(d)], hxb.at[d - 1], bx_s.at[d - 1], bx_r.at[d - 1], dev_x(d)))
    for d in range(1, NZ):
        remote(tsum, thz.at[d - 1], uz_s.at[d - 1], uz_r.at[d - 1], dev_z(d)).wait_recv()
        told = told + thz[d - 1]
    peak[0:128, :] = jnp.concatenate([told, jnp.zeros((120, 128), F32)], axis=0).T
    z_rows = pl.ds(pl.multiple_of(z * ROWS, ROWS), ROWS)
    lfin[p] = jnp.broadcast_to(colr[x, z][:, 1:2] - peak[z_rows, 0:1], (ROWS, 128))
    for d in (4, 3, 5, 2, 6, 1, 7):
        go(remote(lfin.at[p], lfin.at[p], ln_s.at[d - 1], ln_r.at[d - 1], dev_p(at_p(d))))
    grad_b = accb[x]
    for d in (1, 3, 2):
        remote(hb.at[x], hxb.at[d - 1], bx_s.at[d - 1], bx_r.at[d - 1], dev_x(d)).wait_recv()
        grad_b = grad_b + hxb[d - 1].astype(F32)
    grad_a = acca[z]
    for d in range(1, NZ):
        remote(ha.at[z], hza.at[d - 1], gz_s.at[d - 1], gz_r.at[d - 1], dev_z(d)).wait_recv()
        grad_a = grad_a + hza[d - 1].astype(F32)

    fin[p, :, ca] = grad_a.astype(BF16)
    fin[p, :, cb] = grad_b.astype(BF16)
    for d in (4, 3, 5, 2, 6, 1, 7):
        go(remote(fin.at[p], fin.at[p], fn_s.at[d - 1], fn_r.at[d - 1], dev_p(at_p(d))))
    for d in range(1, NP):
        src = at_p(NP - d)
        remote(lfin.at[p], lfin.at[src], ln_s.at[d - 1], ln_r.at[d - 1], dev_p(src)).wait_recv()
        remote(fin.at[p], fin.at[src], fn_s.at[d - 1], fn_r.at[d - 1], dev_p(src)).wait_recv()
    for copy in sends:
        copy.wait_send()


def finish(conc, lfin, fin, conc_o, loss_o, grad_o):
    conc_o[...] = conc[...]
    loss_o[...] = lfin[...].reshape(NP * ROWS, 128).T[0:1, :]
    grad_o[...] = fin[...].reshape(NP * ROWS, WIDTH)


def on_device(centroids, queries, positive, members, member_slot, block_count):
    vmem = pltpu.VMEM
    dma = pltpu.SemaphoreType.DMA
    sems = []
    for shape in (
        (NX - 1,), (NX - 1,), (NX, NZ - 1), (NX, NZ - 1), (NZ - 1,), (NX - 1,), (NZ - 1,), (NX - 1,),
        (8,), (9,), (NP - 1,), (NX * NZ,), (NX - 1,), (NZ - 1,), (NP - 1,), (NP - 1,),
        (NX - 1,), (NZ - 1,), (NZ - 1,), (NX - 1,),
    ):
        sems += [dma(shape), dma(shape)]
    whole = pl.BlockSpec(memory_space=vmem)
    conc, lfin, fin = pl.pallas_call(
        kernel,
        out_shape=(
            vmem((1, CENT), F32),
            vmem((NP, ROWS, 128), F32),
            vmem((NP, ROWS, WIDTH), BF16),
        ),
        in_specs=[pl.BlockSpec(memory_space=pl.ANY)] * 6,
        out_specs=(whole,) * 3,
        scratch_shapes=[
            vmem((ROWS, NX * NZ), jnp.int32),
            vmem((NP, NX * NZ), jnp.int32),
            vmem((1, NP * ROWS), jnp.int32),
            vmem((NP, CENT, WIDTH), BF16),
            vmem((NX, NZ, ROWS, WIDTH), BF16),
            vmem((NX, NZ, 1, 128), F32),
            vmem((NX - 1, NZ, ROWS, WIDTH), BF16),
            vmem((NZ, NX, ROWS, WIDTH), BF16),
            vmem((NX - 1, NZ, 1, 128), F32),
            vmem((NZ, NX, 1, 128), F32),
            vmem((NP, 1, CENT), F32),
            vmem((NP, QS, CENT), F32),
            vmem((NP, QS, CENT), BF16),
            vmem((QS, 128), F32),
            vmem((QS, 128), F32),
            vmem((QS, 128), F32),
            vmem((QS, 128), F32),
            vmem((QS, 128), F32),
            vmem((QS, 128), F32),
            vmem((NX, NZ, 8, 128), F32),
            vmem((NX, NZ, ROWS, 128), F32),
            vmem((QS, 128), F32),
            vmem((NX, NZ, ROWS, 128), F32),
            vmem((NX, NZ, ROWS, WIDTH), F32),
            vmem((NX, NZ, ROWS, WIDTH), F32),
            vmem((NZ, NX, 1, 128), F32),
            vmem((1, 128), F32),
            vmem((NX, 8, 128), F32),
            vmem((NX - 1, 8, 128), F32),
            vmem((NZ - 1, 8, 128), F32),
            vmem((8, 128), F32),
            vmem((NX - 1, NZ, ROWS, CA), BF16),
            vmem((NX - 1, NZ, ROWS, CA), BF16),
            vmem((NZ, ROWS, CA), BF16),
            vmem((NZ - 1, ROWS, CA), BF16),
            vmem((NZ, ROWS, CA), F32),
            vmem((NZ - 1, NX, ROWS, CB), BF16),
            vmem((NZ - 1, NX, ROWS, CB), BF16),
            vmem((NX, ROWS, CB), BF16),
            vmem((NX - 1, ROWS, CB), BF16),
            vmem((NX, ROWS, CB), F32),
            dma((6,)),
            *sems,
        ],
        compiler_params=pltpu.CompilerParams(
            collective_id=0, has_side_effects=True, vmem_limit_bytes=56 * 1024 * 1024
        ),
        name="protonce",
    )(
        centroids,
        queries.reshape(NP, ROWS, WIDTH),
        members.reshape(NZ, NX, NP, ROWS, WIDTH),
        member_slot.transpose(0, 2, 3, 1).reshape(NP, ROWS, NX * NZ),
        block_count.transpose(0, 2, 1).reshape(NP, NX * NZ),
        positive.reshape(1, NP * ROWS),
    )
    conc, loss, grad = pl.pallas_call(
        finish,
        out_shape=(
            jax.ShapeDtypeStruct((1, CENT), F32),
            jax.ShapeDtypeStruct((1, NP * ROWS), F32),
            jax.ShapeDtypeStruct((NP * ROWS, WIDTH), BF16),
        ),
        in_specs=[whole] * 3,
        out_specs=(whole,) * 3,
        name="finish",
    )(*(pltpu.with_memory_space_constraint(v, vmem) for v in (conc, lfin, fin)))
    return conc.reshape(CENT), loss.reshape(NP * ROWS), grad


def solution(mesh):
    placed = (
        P(("dp", "proto"), None),
        P("dp", None),
        P("dp"),
        P("dp", None, None, None, None),
        P("dp", None, None, None),
        P("dp", None, None),
    )
    return jax.shard_map(
        on_device,
        mesh=mesh,
        in_specs=placed,
        out_specs=(P(("dp", "proto")), P("dp"), P("dp", None)),
        check_vma=False,
    )
```

```python
import jax
import jax.numpy as jnp
from jax import lax
from jax.experimental import pallas as pl
from jax.experimental.pallas import tpu as pltpu
from jax.sharding import PartitionSpec as P

MESH = pl.DeviceIdType.MESH
NX, NZ, NP = 4, 8, 8
ROWS, WIDTH, CENT = 16, 768, 512
QS = NX * NZ * ROWS
CA = 512
CB = WIDTH - CA
F32, BF16 = jnp.float32, jnp.bfloat16
LOG2E, LN2 = 1.4426950408889634, 0.6931471805599453


def remote(src, dst, send, recv, device):
    return pltpu.make_async_remote_copy(
        src_ref=src, dst_ref=dst, send_sem=send, recv_sem=recv, device_id=device, device_id_type=MESH
    )


def columns_of(rows):
    n = rows.shape[0]
    wide = jnp.broadcast_to(rows, (n, ROWS, 128))
    lane = lax.broadcasted_iota(jnp.int32, (n, ROWS, 128), 2)
    sub = lax.broadcasted_iota(jnp.int32, (n, ROWS, 128), 1)
    return jnp.sum(jnp.where(lane == sub, wide, 0.0), axis=2, keepdims=True).reshape(n * ROWS, 1)


def kernel(
    cent, qry, mem, slot_hbm, count_hbm, pos_hbm, conc_o, lfin, fin,
    slot_in, count_in, pos_in, call, qall, pall, mx, mall, slx, sall, invall, score, wgt, peak, sums, peakb, sumsb, hitw, hitz, tile, colr, posb, posw,
    gsum, psum, slot, pos, tsend, trx, thz, tsum, ga, gra, ha, hza, acca, gb, grb, hb, hxb, accb,
    local, mx_s, mx_r, sx_s, sx_r, mz_s, mz_r, sz_s, sz_r, qz_s, qz_r, qx_s, qx_r, pz_s, pz_r, px_s, px_r,
    cy_s, cy_r, cc_s, cc_r, iv_s, iv_r, st_s, st_r, gx_s, gx_r, gz_s, gz_r, fn_s, fn_r, ln_s, ln_r,
    ux_s, ux_r, uz_s, uz_r, bz_s, bz_r, bx_s, bx_r,
):
    dp = lax.axis_index("dp")
    p = lax.axis_index("proto")
    z, x = dp // NX, dp % NX
    y, c = p // 2, p % 2

    def at_x(d):
        return (x + d) % NX

    def at_z(d):
        return (z + d) % NZ

    def at_p(d):
        return (p + d) % NP

    def dev_x(d):
        return {"dp": z * NX + at_x(d), "proto": p}

    def dev_z(d):
        return {"dp": at_z(d) * NX + x, "proto": p}

    def dev_xz(d, e):
        return {"dp": at_z(e) * NX + at_x(d), "proto": p}

    def dev_p(q):
        return {"dp": dp, "proto": q}

    barrier = pltpu.get_barrier_semaphore()
    both = sorted(
        ((d, e) for d in range(NX) for e in range(NZ) if d + e), key=lambda v: -min(v[0], NX - v[0]) - min(v[1], NZ - v[1])
    )
    up = ((y + 1) % 4) * 2 + c
    down = ((y + 3) % 4) * 2 + c
    far = ((y + 2) % 4) * 2 + c
    mate = y * 2 + (1 - c)
    for d in (4, 3, 5, 2, 6, 1, 7):
        pl.semaphore_signal(barrier, inc=1, device_id=dev_z(d), device_id_type=MESH)
    for d in (2, 1, 3):
        pl.semaphore_signal(barrier, inc=1, device_id=dev_x(d), device_id_type=MESH)
    for q in (up, down, mate):
        pl.semaphore_signal(barrier, inc=1, device_id=dev_p(q), device_id_type=MESH)

    loads = (
        pltpu.make_async_copy(slot_hbm.at[p], slot_in, local.at[3]),
        pltpu.make_async_copy(count_hbm, count_in, local.at[4]),
        pltpu.make_async_copy(pos_hbm, pos_in, local.at[5]),
    )
    for copy in loads:
        copy.start()
    for copy in loads:
        copy.wait()
    used = lax.broadcasted_iota(jnp.int32, (ROWS, NX * NZ), 0) < count_in[pl.ds(p, 1), :]
    ids = jnp.where(used, slot_in[...], -1).astype(F32)
    ids = jnp.concatenate([ids, jnp.zeros((ROWS, 128 - NX * NZ), F32)], axis=1)
    ids = jnp.concatenate([ids, jnp.zeros((128 - ROWS, 128), F32)], axis=0).T
    for i in range(NX * NZ):
        slot[i // NX, i % NX] = ids[i : i + 1, :]
    wide = jnp.broadcast_to(pos_in[...].astype(F32), (8, 128))
    pos[...] = pltpu.roll(wide, (128 - p * ROWS) % 128, 1)[0:1, :]

    pl.semaphore_wait(barrier, NX + NZ + 1)

    sends = []

    def go(copy):
        copy.start()
        sends.append(copy)

    z_order = (4, 3, 5, 2, 6, 1, 7)
    half = CENT // 2
    top, bottom = pl.ds(0, half), pl.ds(half, half)
    cut = 176
    tops = (pl.ds(0, cut), pl.ds(cut, half - cut))
    bottoms = (pl.ds(half, cut), pl.ds(half + cut, half - cut))

    for d in z_order:
        go(remote(pos, pall.at[x, z], pz_s.at[d - 1], pz_r.at[d - 1], dev_z(d)))
    for d in z_order:
        go(remote(qry.at[p], qall.at[x, z], qz_s.at[d - 1], qz_r.at[d - 1], dev_z(d)))
    go(remote(cent.at[top], call.at[p, top], cy_s.at[0], cy_r.at[0], dev_p(up)))
    go(remote(cent.at[bottom], call.at[p, bottom], cy_s.at[3], cy_r.at[3], dev_p(down)))
    go(remote(cent.at[bottom], call.at[p, bottom], cy_s.at[1], cy_r.at[1], dev_p(up)))
    go(remote(cent.at[top], call.at[p, top], cy_s.at[2], cy_r.at[2], dev_p(down)))
    go(remote(cent, call.at[p], cc_s.at[0], cc_r.at[0], dev_p(mate)))
    for d in (1, 3, 2):
        go(remote(mem.at[:, at_x(d), p], mx.at[d - 1], mx_s.at[d - 1], mx_r.at[d - 1], dev_x(d)))
        go(remote(slot.at[:, at_x(d)], slx.at[d - 1], sx_s.at[d - 1], sx_r.at[d - 1], dev_x(d)))
    for d in z_order:
        go(remote(mem.at[at_z(d), x, p], mall.at[z, 0], mz_s.at[0, d - 1], mz_r.at[0, d - 1], dev_z(d)))
        go(remote(slot.at[at_z(d), x], sall.at[z, 0], sz_s.at[0, d - 1], sz_r.at[0, d - 1], dev_z(d)))
    own = (
        pltpu.make_async_copy(cent, call.at[p], local.at[0]),
        pltpu.make_async_copy(qry.at[p], qall.at[x, z], local.at[1]),
        pltpu.make_async_copy(mem.at[z, x, p], mall.at[z, 0], local.at[2]),
    )
    for copy in own:
        copy.start()
    pall[x, z] = pos[...]
    sall[z, 0] = slot[z, x]
    psum[...] = jnp.zeros_like(psum)

    for d in range(1, NZ):
        src = at_z(NZ - d)
        remote(pos, pall.at[x, src], pz_s.at[d - 1], pz_r.at[d - 1], dev_z(d)).wait_recv()
    for d in (2, 1, 3):
        go(remote(pall.at[x], pall.at[x], px_s.at[d - 1], px_r.at[d - 1], dev_x(d)))
    own[1].wait()
    for d in range(1, NZ):
        src = at_z(NZ - d)
        remote(qry.at[p], qall.at[x, src], qz_s.at[d - 1], qz_r.at[d - 1], dev_z(d)).wait_recv()
    for d in (2, 1, 3):
        go(remote(qall.at[x], qall.at[x], qx_s.at[d - 1], qx_r.at[d - 1], dev_x(d)))

    def members_on(d):
        remote(mem.at[:, x, p], mx.at[d - 1], mx_s.at[d - 1], mx_r.at[d - 1], dev_x(d)).wait_recv()
        remote(slot.at[:, x], slx.at[d - 1], sx_s.at[d - 1], sx_r.at[d - 1], dev_x(d)).wait_recv()
        for e in z_order:
            go(remote(mx.at[d - 1, at_z(e)], mall.at[z, d], mz_s.at[d, e - 1], mz_r.at[d, e - 1], dev_z(e)))
            go(remote(slx.at[d - 1, at_z(e)], sall.at[z, d], sz_s.at[d, e - 1], sz_r.at[d, e - 1], dev_z(e)))
        mall[z, d] = mx[d - 1, z]
        sall[z, d] = slx[d - 1, z]

    members_on(1)
    members_on(3)
    remote(cent.at[top], call.at[down, top], cy_s.at[0], cy_r.at[0], dev_p(up)).wait_recv()
    for i, r in enumerate(tops):
        go(remote(call.at[down, r], call.at[down, r], cy_s.at[4 + i], cy_r.at[4 + i], dev_p(up)))
    remote(cent.at[bottom], call.at[up, bottom], cy_s.at[3], cy_r.at[3], dev_p(down)).wait_recv()
    for i, r in enumerate(bottoms):
        go(remote(call.at[up, r], call.at[up, r], cy_s.at[6 + i], cy_r.at[6 + i], dev_p(down)))
    go(remote(call.at[down, top], call.at[down, top], cc_s.at[1], cc_r.at[1], dev_p(mate)))
    go(remote(call.at[up, bottom], call.at[up, bottom], cc_s.at[2], cc_r.at[2], dev_p(mate)))
    members_on(2)

    for d in range(1, NX):
        src = at_x(NX - d)
        remote(pall.at[x], pall.at[src], px_s.at[d - 1], px_r.at[d - 1], dev_x(d)).wait_recv()
    base = (dp * (NP * CENT)).astype(F32)
    posb[...] = jnp.broadcast_to(columns_of(pall[...].reshape(NX * NZ, 1, 128)) - base, (QS, 128))

    def positives(chunk):
        here = posb[:, 0:1] - (chunk * CENT).astype(F32)
        hot = lax.broadcasted_iota(jnp.int32, (QS, CENT), 1).astype(F32) == here
        psum[...] += jnp.dot(hot.astype(BF16), call[chunk], preferred_element_type=F32).reshape(psum.shape)

    def scores(chunk):
        def rows(i, carry):
            r = pl.ds(i * 2, 2)
            q = qall[r].reshape(2 * NZ * ROWS, WIDTH)
            score[chunk, pl.ds(i * 256, 256), :] = lax.dot_general(
                q, call[chunk], (((1,), (1,)), ((), ())), preferred_element_type=F32
            )
            return carry

        lax.fori_loop(0, 2, rows, 0)

    own[0].wait()
    positives(p)
    remote(cent, call.at[mate], cc_s.at[0], cc_r.at[0], dev_p(mate)).wait_recv()
    positives(mate)
    for d in range(1, NX):
        src = at_x(NX - d)
        remote(qall.at[x], qall.at[src], qx_s.at[d - 1], qx_r.at[d - 1], dev_x(d)).wait_recv()
    scores(p)
    scores(mate)
    remote(cent.at[bottom], call.at[down, bottom], cy_s.at[1], cy_r.at[1], dev_p(up)).wait_recv()
    go(remote(call.at[down, bottom], call.at[down, bottom], cc_s.at[3], cc_r.at[3], dev_p(mate)))
    remote(cent.at[top], call.at[up, top], cy_s.at[2], cy_r.at[2], dev_p(down)).wait_recv()
    go(remote(call.at[up, top], call.at[up, top], cc_s.at[4], cc_r.at[4], dev_p(mate)))
    flip = 1 - 2 * c
    scores(down)
    scores(up)
    remote(call.at[down, top], call.at[down + flip, top], cc_s.at[1], cc_r.at[1], dev_p(mate)).wait_recv()
    remote(call.at[down, bottom], call.at[down + flip, bottom], cc_s.at[3], cc_r.at[3], dev_p(mate)).wait_recv()
    scores(down + flip)
    remote(call.at[up, bottom], call.at[up + flip, bottom], cc_s.at[2], cc_r.at[2], dev_p(mate)).wait_recv()
    remote(call.at[up, top], call.at[up + flip, top], cc_s.at[4], cc_r.at[4], dev_p(mate)).wait_recv()
    scores(up + flip)

    own[2].wait()
    for e in range(1, NZ):
        src = at_z(NZ - e)
        for d in range(NX):
            remote(mem.at[z, x, p], mall.at[src, d], mz_s.at[d, e - 1], mz_r.at[d, e - 1], dev_z(e)).wait_recv()
            remote(slot.at[z, x], sall.at[src, d], sz_s.at[d, e - 1], sz_r.at[d, e - 1], dev_z(e)).wait_recv()
    which = columns_of(sall[...].reshape(NX * NZ, 1, 128))
    cluster = lax.broadcasted_iota(jnp.int32, (QS, CENT), 1).astype(F32)
    hot = which == cluster
    picked = jnp.dot(hot.astype(BF16), call[p], preferred_element_type=F32)
    gap = mall[...].reshape(QS, WIDTH).astype(F32) - picked
    dist = jnp.sqrt(jnp.sum(gap * gap, axis=1, keepdims=True) + 1e-06)
    total = jnp.sum(jnp.where(hot, dist, 0.0), axis=0, keepdims=True)
    count = jnp.sum(hot.astype(F32), axis=0, keepdims=True)
    conc = (total + 1.0) / ((count + 1.0) * jnp.log(count + 10.0))
    conc_o[...] = conc
    invall[p] = 1.0 / conc
    for d in (4, 3, 5, 2, 6, 1, 7):
        go(remote(invall.at[p], invall.at[p], iv_s.at[d - 1], iv_r.at[d - 1], dev_p(at_p(d))))

    positives(down)
    positives(up)
    positives(down + flip)
    positives(up + flip)
    for i in range(2):
        r = tops[i]
        remote(call.at[down, r], call.at[far, r], cy_s.at[4 + i], cy_r.at[4 + i], dev_p(up)).wait_recv()
        go(remote(call.at[far, r], call.at[far, r], cc_s.at[5 + i], cc_r.at[5 + i], dev_p(mate)))
        r = bottoms[i]
        remote(call.at[up, r], call.at[far, r], cy_s.at[6 + i], cy_r.at[6 + i], dev_p(down)).wait_recv()
        go(remote(call.at[far, r], call.at[far, r], cc_s.at[7 + i], cc_r.at[7 + i], dev_p(mate)))
    scores(far)
    for d in range(1, NP):
        src = at_p(NP - d)
        remote(invall.at[p], invall.at[src], iv_s.at[d - 1], iv_r.at[d - 1], dev_p(src)).wait_recv()

    step = 16

    def fold(v, op):
        return op(op(v[:, 0:128], v[:, 128:256]), op(v[:, 256:384], v[:, 384:512]))

    def soften(chunks, peak, sums):
        def largest(i, carry):
            r = pl.ds(pl.multiple_of(i * step, step), step)
            best = None
            for k in chunks:
                zed = score[k, r, :] * (invall[k] * LOG2E)
                best = zed if best is None else jnp.maximum(best, zed)
            peak[r, :] = fold(best, jnp.maximum)
            return carry

        lax.fori_loop(0, QS // step, largest, 0, unroll=4)
        peak[...] = jnp.broadcast_to(jnp.max(peak[...], axis=1, keepdims=True), (QS, 128))

        def soft(i, carry):
            r = pl.ds(pl.multiple_of(i * step, step), step)
            most = jnp.concatenate([peak[r, :]] * 4, axis=1)
            added = None
            for k in chunks:
                e = jnp.exp2(score[k, r, :] * (invall[k] * LOG2E) - most)
                wgt[k, r, :] = (e * invall[k]).astype(BF16)
                added = e if added is None else added + e
            sums[r, :] = fold(added, jnp.add)
            return carry

        lax.fori_loop(0, QS // step, soft, 0, unroll=4)

    early = (p, mate, down, up, down + flip, up + flip, far)
    last = far + flip
    soften(early, peak, sums)
    for i in range(4):
        r = (tops + bottoms)[i]
        remote(call.at[far, r], call.at[far + flip, r], cc_s.at[5 + i], cc_r.at[5 + i], dev_p(mate)).wait_recv()
    scores(last)
    soften((last,), peakb, sumsb)

    lane = lax.broadcasted_iota(jnp.int32, (QS, 128), 1)
    most = jnp.maximum(peak[...], peakb[...])
    peak[...] = jnp.exp2(peak[...] - most)
    peakb[...] = jnp.exp2(peakb[...] - most)
    summed = jnp.sum(sums[...] * peak[...] + sumsb[...] * peakb[...], axis=1, keepdims=True)
    mine = jnp.where(lane == 0, most, summed).T
    tile[x, z] = jnp.concatenate([mine[i : i + 1, b * 128 : (b + 1) * 128] for i in range(2) for b in range(NX)], axis=0)
    for d, e in both:
        go(remote(tile.at[x, z], tile.at[x, z], st_s.at[d * NZ + e], st_r.at[d * NZ + e], dev_xz(d, e)))

    def weigh(i, carry):
        r = pl.ds(pl.multiple_of(i * 256, 256), 256)
        out = None
        for k in early:
            term = jnp.dot(wgt[k, r, :], call[k], preferred_element_type=F32)
            out = term if out is None else out + term
        late = jnp.dot(wgt[last, r, :], call[last], preferred_element_type=F32)
        for s in range(0, 256, step):
            q = pl.ds(pl.multiple_of(i * 256 + s, step), step)
            here = jnp.concatenate([posb[q, :]] * 4, axis=1)
            col = lax.broadcasted_iota(jnp.int32, (step, CENT), 1).astype(F32)
            weight, logit = None, None
            for k in range(NP):
                hit = col == here - float(k * CENT)
                a = jnp.where(hit, jnp.broadcast_to(invall[k], (step, CENT)), 0.0)
                b = jnp.where(hit, score[k, q, :], 0.0)
                weight = a if weight is None else weight + a
                logit = b if logit is None else logit + b
            hitw[q, :] = fold(weight, jnp.add)
            hitz[q, :] = fold(logit, jnp.add)
        out = out * peak[r, 0:1] + late * peakb[r, 0:1]
        gsum[pl.ds(i * 2, 2)] = out.reshape(2, NZ, ROWS, WIDTH)
        return carry

    lax.fori_loop(0, 2, weigh, 0)
    scale = jnp.sum(hitw[...], axis=1, keepdims=True)
    target = jnp.sum(hitz[...], axis=1, keepdims=True) * scale
    posw[...] = jnp.broadcast_to(scale, (QS, 128)).reshape(posw.shape)
    turned = jnp.broadcast_to(target, (QS, 128)).T[0:8, :]
    for b in range(NX):
        tsend[b] = turned[:, b * 128 : (b + 1) * 128]
    for d in (2, 1, 3):
        go(remote(tsend.at[at_x(d)], trx.at[d - 1], ux_s.at[d - 1], ux_r.at[d - 1], dev_x(d)))
    positives(far)
    positives(last)

    for d, e in both:
        src = (at_x(NX - d), at_z(NZ - e))
        remote(tile.at[x, z], tile.at[src], st_s.at[d * NZ + e], st_r.at[d * NZ + e], dev_xz(d, e)).wait_recv()
    tiles = tile[...].reshape(NX * NZ, 8, 128)
    best = jnp.max(tiles[:, 0:NX], axis=0)
    added = jnp.sum(tiles[:, NX:8] * jnp.exp2(tiles[:, 0:NX] - best[None]), axis=0)

    def flat(v):
        return jnp.concatenate([v[b : b + 1, :] for b in range(NX)], axis=1)

    share = flat(jnp.exp2(tile[x, z][0:NX] - best) / added)
    total_log = flat(best * LN2 + jnp.log(added))
    colr[...] = jnp.concatenate([share, total_log, jnp.zeros((126, QS), F32)], axis=0).T.reshape(colr.shape)

    ca, cb = pl.ds(0, CA), pl.ds(CA, CB)

    def part(at, cols):
        return gsum[at + (slice(None), cols)] * colr[at][..., 0:1] - psum[at + (slice(None), cols)] * posw[at][..., 0:1]

    def part_x(b):
        return part((b, slice(None)), ca)

    def part_z(b):
        return part((slice(None), b), cb)

    ga[1] = part_x(at_x(2)).astype(BF16)
    go(remote(ga.at[1], gra.at[1], gx_s.at[1], gx_r.at[1], dev_x(2)))
    for d in z_order[:3]:
        gb[d - 1] = part_z(at_z(d)).astype(BF16)
        go(remote(gb.at[d - 1], grb.at[d - 1], bz_s.at[d - 1], bz_r.at[d - 1], dev_z(d)))
    for d in (1, 3):
        ga[d - 1] = part_x(at_x(d)).astype(BF16)
        go(remote(ga.at[d - 1], gra.at[d - 1], gx_s.at[d - 1], gx_r.at[d - 1], dev_x(d)))
    for d in z_order[3:]:
        gb[d - 1] = part_z(at_z(d)).astype(BF16)
        go(remote(gb.at[d - 1], grb.at[d - 1], bz_s.at[d - 1], bz_r.at[d - 1], dev_z(d)))
    told = tsend[x]
    for d in (1, 3, 2):
        remote(tsend.at[x], trx.at[d - 1], ux_s.at[d - 1], ux_r.at[d - 1], dev_x(d)).wait_recv()
        told = told + trx[d - 1]
    tsum[...] = told
    for d in z_order:
        go(remote(tsum, thz.at[d - 1], uz_s.at[d - 1], uz_r.at[d - 1], dev_z(d)))
    acca[...] = part_x(x)
    accb[...] = part_z(z)
    for d in (1, 3, 2):
        remote(ga.at[d - 1], gra.at[d - 1], gx_s.at[d - 1], gx_r.at[d - 1], dev_x(d)).wait_recv()
        acca[...] += gra[d - 1].astype(F32)
    ha[...] = acca[...].astype(BF16)
    for d in z_order:
        go(remote(ha.at[at_z(d)], hza.at[d - 1], gz_s.at[d - 1], gz_r.at[d - 1], dev_z(d)))
    for d in range(1, NZ):
        remote(gb.at[d - 1], grb.at[d - 1], bz_s.at[d - 1], bz_r.at[d - 1], dev_z(d)).wait_recv()
        accb[...] += grb[d - 1].astype(F32)
    hb[...] = accb[...].astype(BF16)
    for d in (2, 1, 3):
        go(remote(hb.at[at_x(d)], hxb.at[d - 1], bx_s.at[d - 1], bx_r.at[d - 1], dev_x(d)))
    for d in range(1, NZ):
        remote(tsum, thz.at[d - 1], uz_s.at[d - 1], uz_r.at[d - 1], dev_z(d)).wait_recv()
        told = told + thz[d - 1]
    peak[0:128, :] = jnp.concatenate([told, jnp.zeros((120, 128), F32)], axis=0).T
    z_rows = pl.ds(pl.multiple_of(z * ROWS, ROWS), ROWS)
    lfin[p] = jnp.broadcast_to(colr[x, z][:, 1:2] - peak[z_rows, 0:1], (ROWS, 128))
    for d in (4, 3, 5, 2, 6, 1, 7):
        go(remote(lfin.at[p], lfin.at[p], ln_s.at[d - 1], ln_r.at[d - 1], dev_p(at_p(d))))
    grad_b = accb[x]
    for d in (1, 3, 2):
        remote(hb.at[x], hxb.at[d - 1], bx_s.at[d - 1], bx_r.at[d - 1], dev_x(d)).wait_recv()
        grad_b = grad_b + hxb[d - 1].astype(F32)
    grad_a = acca[z]
    for d in range(1, NZ):
        remote(ha.at[z], hza.at[d - 1], gz_s.at[d - 1], gz_r.at[d - 1], dev_z(d)).wait_recv()
        grad_a = grad_a + hza[d - 1].astype(F32)

    earlier = tuple(sends)
    sends.clear()
    fin[p, :, ca] = grad_a.astype(BF16)
    fin[p, :, cb] = grad_b.astype(BF16)
    for d in (4, 3, 5, 2, 6, 1, 7):
        go(remote(fin.at[p], fin.at[p], fn_s.at[d - 1], fn_r.at[d - 1], dev_p(at_p(d))))
    for copy in earlier:
        copy.wait_send()
    for d in range(1, NP):
        src = at_p(NP - d)
        remote(lfin.at[p], lfin.at[src], ln_s.at[d - 1], ln_r.at[d - 1], dev_p(src)).wait_recv()
        remote(fin.at[p], fin.at[src], fn_s.at[d - 1], fn_r.at[d - 1], dev_p(src)).wait_recv()
    for copy in sends:
        copy.wait_send()


def finish(conc, lfin, fin, conc_o, loss_o, grad_o):
    conc_o[...] = conc[...]
    loss_o[...] = lfin[...].reshape(NP * ROWS, 128).T[0:1, :]
    grad_o[...] = fin[...].reshape(NP * ROWS, WIDTH)


def on_device(centroids, queries, positive, members, member_slot, block_count):
    vmem = pltpu.VMEM
    dma = pltpu.SemaphoreType.DMA
    sems = []
    for shape in (
        (NX - 1,), (NX - 1,), (NX, NZ - 1), (NX, NZ - 1), (NZ - 1,), (NX - 1,), (NZ - 1,), (NX - 1,),
        (8,), (9,), (NP - 1,), (NX * NZ,), (NX - 1,), (NZ - 1,), (NP - 1,), (NP - 1,),
        (NX - 1,), (NZ - 1,), (NZ - 1,), (NX - 1,),
    ):
        sems += [dma(shape), dma(shape)]
    whole = pl.BlockSpec(memory_space=vmem)
    conc, lfin, fin = pl.pallas_call(
        kernel,
        out_shape=(
            vmem((1, CENT), F32),
            vmem((NP, ROWS, 128), F32),
            vmem((NP, ROWS, WIDTH), BF16),
        ),
        in_specs=[pl.BlockSpec(memory_space=pl.ANY)] * 6,
        out_specs=(whole,) * 3,
        scratch_shapes=[
            vmem((ROWS, NX * NZ), jnp.int32),
            vmem((NP, NX * NZ), jnp.int32),
            vmem((1, NP * ROWS), jnp.int32),
            vmem((NP, CENT, WIDTH), BF16),
            vmem((NX, NZ, ROWS, WIDTH), BF16),
            vmem((NX, NZ, 1, 128), F32),
            vmem((NX - 1, NZ, ROWS, WIDTH), BF16),
            vmem((NZ, NX, ROWS, WIDTH), BF16),
            vmem((NX - 1, NZ, 1, 128), F32),
            vmem((NZ, NX, 1, 128), F32),
            vmem((NP, 1, CENT), F32),
            vmem((NP, QS, CENT), F32),
            vmem((NP, QS, CENT), BF16),
            vmem((QS, 128), F32),
            vmem((QS, 128), F32),
            vmem((QS, 128), F32),
            vmem((QS, 128), F32),
            vmem((QS, 128), F32),
            vmem((QS, 128), F32),
            vmem((NX, NZ, 8, 128), F32),
            vmem((NX, NZ, ROWS, 128), F32),
            vmem((QS, 128), F32),
            vmem((NX, NZ, ROWS, 128), F32),
            vmem((NX, NZ, ROWS, WIDTH), F32),
            vmem((NX, NZ, ROWS, WIDTH), F32),
            vmem((NZ, NX, 1, 128), F32),
            vmem((1, 128), F32),
            vmem((NX, 8, 128), F32),
            vmem((NX - 1, 8, 128), F32),
            vmem((NZ - 1, 8, 128), F32),
            vmem((8, 128), F32),
            vmem((NX - 1, NZ, ROWS, CA), BF16),
            vmem((NX - 1, NZ, ROWS, CA), BF16),
            vmem((NZ, ROWS, CA), BF16),
            vmem((NZ - 1, ROWS, CA), BF16),
            vmem((NZ, ROWS, CA), F32),
            vmem((NZ - 1, NX, ROWS, CB), BF16),
            vmem((NZ - 1, NX, ROWS, CB), BF16),
            vmem((NX, ROWS, CB), BF16),
            vmem((NX - 1, ROWS, CB), BF16),
            vmem((NX, ROWS, CB), F32),
            dma((6,)),
            *sems,
        ],
        compiler_params=pltpu.CompilerParams(
            collective_id=0, has_side_effects=True, vmem_limit_bytes=56 * 1024 * 1024
        ),
        name="protonce",
    )(
        centroids,
        queries.reshape(NP, ROWS, WIDTH),
        members.reshape(NZ, NX, NP, ROWS, WIDTH),
        member_slot.transpose(0, 2, 3, 1).reshape(NP, ROWS, NX * NZ),
        block_count.transpose(0, 2, 1).reshape(NP, NX * NZ),
        positive.reshape(1, NP * ROWS),
    )
    conc, loss, grad = pl.pallas_call(
        finish,
        out_shape=(
            jax.ShapeDtypeStruct((1, CENT), F32),
            jax.ShapeDtypeStruct((1, NP * ROWS), F32),
            jax.ShapeDtypeStruct((NP * ROWS, WIDTH), BF16),
        ),
        in_specs=[whole] * 3,
        out_specs=(whole,) * 3,
        name="finish",
    )(*(pltpu.with_memory_space_constraint(v, vmem) for v in (conc, lfin, fin)))
    return conc.reshape(CENT), loss.reshape(NP * ROWS), grad


def solution(mesh):
    placed = (
        P(("dp", "proto"), None),
        P("dp", None),
        P("dp"),
        P("dp", None, None, None, None),
        P("dp", None, None, None),
        P("dp", None, None),
    )
    return jax.shard_map(
        on_device,
        mesh=mesh,
        in_specs=placed,
        out_specs=(P(("dp", "proto")), P("dp"), P("dp", None)),
        check_vma=False,
    )
```

```python
import jax
import jax.numpy as jnp
from jax import lax
from jax.experimental import pallas as pl
from jax.experimental.pallas import tpu as pltpu
from jax.sharding import PartitionSpec as P

MESH = pl.DeviceIdType.MESH
NX, NZ, NP = 4, 8, 8
ROWS, WIDTH, CENT = 16, 768, 512
QS = NX * NZ * ROWS
CA = 512
CB = WIDTH - CA
F32, BF16 = jnp.float32, jnp.bfloat16
LOG2E, LN2 = 1.4426950408889634, 0.6931471805599453


def remote(src, dst, send, recv, device):
    return pltpu.make_async_remote_copy(
        src_ref=src, dst_ref=dst, send_sem=send, recv_sem=recv, device_id=device, device_id_type=MESH
    )


def columns_of(rows):
    n = rows.shape[0]
    wide = jnp.broadcast_to(rows, (n, ROWS, 128))
    lane = lax.broadcasted_iota(jnp.int32, (n, ROWS, 128), 2)
    sub = lax.broadcasted_iota(jnp.int32, (n, ROWS, 128), 1)
    return jnp.sum(jnp.where(lane == sub, wide, 0.0), axis=2, keepdims=True).reshape(n * ROWS, 1)


def kernel(
    cent, qry, mem, slot_hbm, count_hbm, pos_hbm, conc_o, lfin, fin,
    slot_in, count_in, pos_in, call, qall, pall, mx, mall, slx, sall, invall, score, wgt, peak, sums, peakb, sumsb, hitw, hitz, tile, colr, posb, posw,
    gsum, psum, slot, pos, tsend, trx, thz, tsum, ga, gra, ha, hza, acca, gb, grb, hb, hxb, accb,
    local, mx_s, mx_r, sx_s, sx_r, mz_s, mz_r, sz_s, sz_r, qz_s, qz_r, qx_s, qx_r, pz_s, pz_r, px_s, px_r,
    cy_s, cy_r, cc_s, cc_r, iv_s, iv_r, st_s, st_r, gx_s, gx_r, gz_s, gz_r, fn_s, fn_r, ln_s, ln_r,
    ux_s, ux_r, uz_s, uz_r, bz_s, bz_r, bx_s, bx_r,
):
    dp = lax.axis_index("dp")
    p = lax.axis_index("proto")
    z, x = dp // NX, dp % NX
    y, c = p // 2, p % 2

    def at_x(d):
        return (x + d) % NX

    def at_z(d):
        return (z + d) % NZ

    def at_p(d):
        return (p + d) % NP

    def dev_x(d):
        return {"dp": z * NX + at_x(d), "proto": p}

    def dev_z(d):
        return {"dp": at_z(d) * NX + x, "proto": p}

    def dev_xz(d, e):
        return {"dp": at_z(e) * NX + at_x(d), "proto": p}

    def dev_p(q):
        return {"dp": dp, "proto": q}

    barrier = pltpu.get_barrier_semaphore()
    both = sorted(
        ((d, e) for d in range(NX) for e in range(NZ) if d + e), key=lambda v: -min(v[0], NX - v[0]) - min(v[1], NZ - v[1])
    )
    up = ((y + 1) % 4) * 2 + c
    down = ((y + 3) % 4) * 2 + c
    far = ((y + 2) % 4) * 2 + c
    mate = y * 2 + (1 - c)
    for d in (4, 3, 5, 2, 6, 1, 7):
        pl.semaphore_signal(barrier, inc=1, device_id=dev_z(d), device_id_type=MESH)
    for d in (2, 1, 3):
        pl.semaphore_signal(barrier, inc=1, device_id=dev_x(d), device_id_type=MESH)
    for q in (up, down, mate):
        pl.semaphore_signal(barrier, inc=1, device_id=dev_p(q), device_id_type=MESH)

    loads = (
        pltpu.make_async_copy(slot_hbm.at[p], slot_in, local.at[3]),
        pltpu.make_async_copy(count_hbm, count_in, local.at[4]),
        pltpu.make_async_copy(pos_hbm, pos_in, local.at[5]),
    )
    for copy in loads:
        copy.start()
    for copy in loads:
        copy.wait()
    used = lax.broadcasted_iota(jnp.int32, (ROWS, NX * NZ), 0) < count_in[pl.ds(p, 1), :]
    ids = jnp.where(used, slot_in[...], -1).astype(F32)
    ids = jnp.concatenate([ids, jnp.zeros((ROWS, 128 - NX * NZ), F32)], axis=1)
    ids = jnp.concatenate([ids, jnp.zeros((128 - ROWS, 128), F32)], axis=0).T
    for i in range(NX * NZ):
        slot[i // NX, i % NX] = ids[i : i + 1, :]
    wide = jnp.broadcast_to(pos_in[...].astype(F32), (8, 128))
    pos[...] = pltpu.roll(wide, (128 - p * ROWS) % 128, 1)[0:1, :]

    pl.semaphore_wait(barrier, NX + NZ + 1)

    sends = []

    def go(copy):
        copy.start()
        sends.append(copy)

    z_order = (4, 3, 5, 2, 6, 1, 7)
    half = CENT // 2
    top, bottom = pl.ds(0, half), pl.ds(half, half)
    cut = 176
    tops = (pl.ds(0, cut), pl.ds(cut, half - cut))
    bottoms = (pl.ds(half, cut), pl.ds(half + cut, half - cut))

    for d in z_order:
        go(remote(pos, pall.at[x, z], pz_s.at[d - 1], pz_r.at[d - 1], dev_z(d)))
    for d in z_order:
        go(remote(qry.at[p], qall.at[x, z], qz_s.at[d - 1], qz_r.at[d - 1], dev_z(d)))
    go(remote(cent.at[top], call.at[p, top], cy_s.at[0], cy_r.at[0], dev_p(up)))
    go(remote(cent.at[bottom], call.at[p, bottom], cy_s.at[3], cy_r.at[3], dev_p(down)))
    go(remote(cent.at[bottom], call.at[p, bottom], cy_s.at[1], cy_r.at[1], dev_p(up)))
    go(remote(cent.at[top], call.at[p, top], cy_s.at[2], cy_r.at[2], dev_p(down)))
    go(remote(cent, call.at[p], cc_s.at[0], cc_r.at[0], dev_p(mate)))
    for d in (1, 3, 2):
        go(remote(mem.at[:, at_x(d), p], mx.at[d - 1], mx_s.at[d - 1], mx_r.at[d - 1], dev_x(d)))
        go(remote(slot.at[:, at_x(d)], slx.at[d - 1], sx_s.at[d - 1], sx_r.at[d - 1], dev_x(d)))
    for d in z_order:
        go(remote(mem.at[at_z(d), x, p], mall.at[z, 0], mz_s.at[0, d - 1], mz_r.at[0, d - 1], dev_z(d)))
        go(remote(slot.at[at_z(d), x], sall.at[z, 0], sz_s.at[0, d - 1], sz_r.at[0, d - 1], dev_z(d)))
    own = (
        pltpu.make_async_copy(cent, call.at[p], local.at[0]),
        pltpu.make_async_copy(qry.at[p], qall.at[x, z], local.at[1]),
        pltpu.make_async_copy(mem.at[z, x, p], mall.at[z, 0], local.at[2]),
    )
    for copy in own:
        copy.start()
    pall[x, z] = pos[...]
    sall[z, 0] = slot[z, x]
    psum[...] = jnp.zeros_like(psum)

    for d in range(1, NZ):
        src = at_z(NZ - d)
        remote(pos, pall.at[x, src], pz_s.at[d - 1], pz_r.at[d - 1], dev_z(d)).wait_recv()
    for d in (2, 1, 3):
        go(remote(pall.at[x], pall.at[x], px_s.at[d - 1], px_r.at[d - 1], dev_x(d)))
    own[1].wait()
    for d in range(1, NZ):
        src = at_z(NZ - d)
        remote(qry.at[p], qall.at[x, src], qz_s.at[d - 1], qz_r.at[d - 1], dev_z(d)).wait_recv()
    for d in (2, 1, 3):
        go(remote(qall.at[x], qall.at[x], qx_s.at[d - 1], qx_r.at[d - 1], dev_x(d)))

    def members_on(d):
        remote(mem.at[:, x, p], mx.at[d - 1], mx_s.at[d - 1], mx_r.at[d - 1], dev_x(d)).wait_recv()
        remote(slot.at[:, x], slx.at[d - 1], sx_s.at[d - 1], sx_r.at[d - 1], dev_x(d)).wait_recv()
        for e in z_order:
            go(remote(mx.at[d - 1, at_z(e)], mall.at[z, d], mz_s.at[d, e - 1], mz_r.at[d, e - 1], dev_z(e)))
            go(remote(slx.at[d - 1, at_z(e)], sall.at[z, d], sz_s.at[d, e - 1], sz_r.at[d, e - 1], dev_z(e)))
        mall[z, d] = mx[d - 1, z]
        sall[z, d] = slx[d - 1, z]

    members_on(1)
    members_on(3)
    remote(cent.at[top], call.at[down, top], cy_s.at[0], cy_r.at[0], dev_p(up)).wait_recv()
    for i, r in enumerate(tops):
        go(remote(call.at[down, r], call.at[down, r], cy_s.at[4 + i], cy_r.at[4 + i], dev_p(up)))
    remote(cent.at[bottom], call.at[up, bottom], cy_s.at[3], cy_r.at[3], dev_p(down)).wait_recv()
    for i, r in enumerate(bottoms):
        go(remote(call.at[up, r], call.at[up, r], cy_s.at[6 + i], cy_r.at[6 + i], dev_p(down)))
    go(remote(call.at[down, top], call.at[down, top], cc_s.at[1], cc_r.at[1], dev_p(mate)))
    go(remote(call.at[up, bottom], call.at[up, bottom], cc_s.at[2], cc_r.at[2], dev_p(mate)))
    members_on(2)

    for d in range(1, NX):
        src = at_x(NX - d)
        remote(pall.at[x], pall.at[src], px_s.at[d - 1], px_r.at[d - 1], dev_x(d)).wait_recv()
    base = (dp * (NP * CENT)).astype(F32)
    posb[...] = jnp.broadcast_to(columns_of(pall[...].reshape(NX * NZ, 1, 128)) - base, (QS, 128))

    def positives(chunk):
        here = posb[:, 0:1] - (chunk * CENT).astype(F32)
        hot = lax.broadcasted_iota(jnp.int32, (QS, CENT), 1).astype(F32) == here
        psum[...] += jnp.dot(hot.astype(BF16), call[chunk], preferred_element_type=F32).reshape(psum.shape)

    def scores(chunk):
        def rows(i, carry):
            r = pl.ds(i * 2, 2)
            q = qall[r].reshape(2 * NZ * ROWS, WIDTH)
            score[chunk, pl.ds(i * 256, 256), :] = lax.dot_general(
                q, call[chunk], (((1,), (1,)), ((), ())), preferred_element_type=F32
            )
            return carry

        lax.fori_loop(0, 2, rows, 0)

    own[0].wait()
    positives(p)
    remote(cent, call.at[mate], cc_s.at[0], cc_r.at[0], dev_p(mate)).wait_recv()
    positives(mate)
    for d in range(1, NX):
        src = at_x(NX - d)
        remote(qall.at[x], qall.at[src], qx_s.at[d - 1], qx_r.at[d - 1], dev_x(d)).wait_recv()
    scores(p)
    scores(mate)
    remote(cent.at[bottom], call.at[down, bottom], cy_s.at[1], cy_r.at[1], dev_p(up)).wait_recv()
    go(remote(call.at[down, bottom], call.at[down, bottom], cc_s.at[3], cc_r.at[3], dev_p(mate)))
    remote(cent.at[top], call.at[up, top], cy_s.at[2], cy_r.at[2], dev_p(down)).wait_recv()
    go(remote(call.at[up, top], call.at[up, top], cc_s.at[4], cc_r.at[4], dev_p(mate)))
    flip = 1 - 2 * c
    scores(down)
    scores(up)
    remote(call.at[down, top], call.at[down + flip, top], cc_s.at[1], cc_r.at[1], dev_p(mate)).wait_recv()
    remote(call.at[down, bottom], call.at[down + flip, bottom], cc_s.at[3], cc_r.at[3], dev_p(mate)).wait_recv()
    remote(call.at[up, bottom], call.at[up + flip, bottom], cc_s.at[2], cc_r.at[2], dev_p(mate)).wait_recv()
    remote(call.at[up, top], call.at[up + flip, top], cc_s.at[4], cc_r.at[4], dev_p(mate)).wait_recv()

    own[2].wait()
    for e in range(1, NZ):
        src = at_z(NZ - e)
        for d in range(NX):
            remote(mem.at[z, x, p], mall.at[src, d], mz_s.at[d, e - 1], mz_r.at[d, e - 1], dev_z(e)).wait_recv()
            remote(slot.at[z, x], sall.at[src, d], sz_s.at[d, e - 1], sz_r.at[d, e - 1], dev_z(e)).wait_recv()
    which = columns_of(sall[...].reshape(NX * NZ, 1, 128))
    cluster = lax.broadcasted_iota(jnp.int32, (QS, CENT), 1).astype(F32)
    hot = which == cluster
    picked = jnp.dot(hot.astype(BF16), call[p], preferred_element_type=F32)
    gap = mall[...].reshape(QS, WIDTH).astype(F32) - picked
    dist = jnp.sqrt(jnp.sum(gap * gap, axis=1, keepdims=True) + 1e-06)
    total = jnp.sum(jnp.where(hot, dist, 0.0), axis=0, keepdims=True)
    count = jnp.sum(hot.astype(F32), axis=0, keepdims=True)
    conc = (total + 1.0) / ((count + 1.0) * jnp.log(count + 10.0))
    conc_o[...] = conc
    invall[p] = 1.0 / conc
    for d in (4, 3, 5, 2, 6, 1, 7):
        go(remote(invall.at[p], invall.at[p], iv_s.at[d - 1], iv_r.at[d - 1], dev_p(at_p(d))))

    scores(down + flip)
    scores(up + flip)
    positives(down)
    positives(up)
    positives(down + flip)
    positives(up + flip)
    for i in range(2):
        r = tops[i]
        remote(call.at[down, r], call.at[far, r], cy_s.at[4 + i], cy_r.at[4 + i], dev_p(up)).wait_recv()
        go(remote(call.at[far, r], call.at[far, r], cc_s.at[5 + i], cc_r.at[5 + i], dev_p(mate)))
        r = bottoms[i]
        remote(call.at[up, r], call.at[far, r], cy_s.at[6 + i], cy_r.at[6 + i], dev_p(down)).wait_recv()
        go(remote(call.at[far, r], call.at[far, r], cc_s.at[7 + i], cc_r.at[7 + i], dev_p(mate)))
    scores(far)
    for d in range(1, NP):
        src = at_p(NP - d)
        remote(invall.at[p], invall.at[src], iv_s.at[d - 1], iv_r.at[d - 1], dev_p(src)).wait_recv()

    step = 16

    def fold(v, op):
        return op(op(v[:, 0:128], v[:, 128:256]), op(v[:, 256:384], v[:, 384:512]))

    def soften(chunks, peak, sums):
        def largest(i, carry):
            r = pl.ds(pl.multiple_of(i * step, step), step)
            best = None
            for k in chunks:
                zed = score[k, r, :] * (invall[k] * LOG2E)
                best = zed if best is None else jnp.maximum(best, zed)
            peak[r, :] = fold(best, jnp.maximum)
            return carry

        lax.fori_loop(0, QS // step, largest, 0, unroll=4)
        peak[...] = jnp.broadcast_to(jnp.max(peak[...], axis=1, keepdims=True), (QS, 128))

        def soft(i, carry):
            r = pl.ds(pl.multiple_of(i * step, step), step)
            most = jnp.concatenate([peak[r, :]] * 4, axis=1)
            added = None
            for k in chunks:
                e = jnp.exp2(score[k, r, :] * (invall[k] * LOG2E) - most)
                wgt[k, r, :] = (e * invall[k]).astype(BF16)
                added = e if added is None else added + e
            sums[r, :] = fold(added, jnp.add)
            return carry

        lax.fori_loop(0, QS // step, soft, 0, unroll=4)

    early = (p, mate, down, up, down + flip, up + flip, far)
    last = far + flip
    soften(early, peak, sums)
    for i in range(4):
        r = (tops + bottoms)[i]
        remote(call.at[far, r], call.at[far + flip, r], cc_s.at[5 + i], cc_r.at[5 + i], dev_p(mate)).wait_recv()
    scores(last)
    soften((last,), peakb, sumsb)

    lane = lax.broadcasted_iota(jnp.int32, (QS, 128), 1)
    most = jnp.maximum(peak[...], peakb[...])
    peak[...] = jnp.exp2(peak[...] - most)
    peakb[...] = jnp.exp2(peakb[...] - most)
    summed = jnp.sum(sums[...] * peak[...] + sumsb[...] * peakb[...], axis=1, keepdims=True)
    mine = jnp.where(lane == 0, most, summed).T
    tile[x, z] = jnp.concatenate([mine[i : i + 1, b * 128 : (b + 1) * 128] for i in range(2) for b in range(NX)], axis=0)
    for d, e in both:
        go(remote(tile.at[x, z], tile.at[x, z], st_s.at[d * NZ + e], st_r.at[d * NZ + e], dev_xz(d, e)))

    def weigh(i, carry):
        r = pl.ds(pl.multiple_of(i * 256, 256), 256)
        out = None
        for k in early:
            term = jnp.dot(wgt[k, r, :], call[k], preferred_element_type=F32)
            out = term if out is None else out + term
        late = jnp.dot(wgt[last, r, :], call[last], preferred_element_type=F32)
        for s in range(0, 256, step):
            q = pl.ds(pl.multiple_of(i * 256 + s, step), step)
            here = jnp.concatenate([posb[q, :]] * 4, axis=1)
            col = lax.broadcasted_iota(jnp.int32, (step, CENT), 1).astype(F32)
            weight, logit = None, None
            for k in range(NP):
                hit = col == here - float(k * CENT)
                a = jnp.where(hit, jnp.broadcast_to(invall[k], (step, CENT)), 0.0)
                b = jnp.where(hit, score[k, q, :], 0.0)
                weight = a if weight is None else weight + a
                logit = b if logit is None else logit + b
            hitw[q, :] = fold(weight, jnp.add)
            hitz[q, :] = fold(logit, jnp.add)
        out = out * peak[r, 0:1] + late * peakb[r, 0:1]
        gsum[pl.ds(i * 2, 2)] = out.reshape(2, NZ, ROWS, WIDTH)
        return carry

    lax.fori_loop(0, 2, weigh, 0)
    scale = jnp.sum(hitw[...], axis=1, keepdims=True)
    target = jnp.sum(hitz[...], axis=1, keepdims=True) * scale
    posw[...] = jnp.broadcast_to(scale, (QS, 128)).reshape(posw.shape)
    turned = jnp.broadcast_to(target, (QS, 128)).T[0:8, :]
    for b in range(NX):
        tsend[b] = turned[:, b * 128 : (b + 1) * 128]
    for d in (2, 1, 3):
        go(remote(tsend.at[at_x(d)], trx.at[d - 1], ux_s.at[d - 1], ux_r.at[d - 1], dev_x(d)))
    positives(far)
    positives(last)

    for d, e in both:
        src = (at_x(NX - d), at_z(NZ - e))
        remote(tile.at[x, z], tile.at[src], st_s.at[d * NZ + e], st_r.at[d * NZ + e], dev_xz(d, e)).wait_recv()
    tiles = tile[...].reshape(NX * NZ, 8, 128)
    best = jnp.max(tiles[:, 0:NX], axis=0)
    added = jnp.sum(tiles[:, NX:8] * jnp.exp2(tiles[:, 0:NX] - best[None]), axis=0)

    def flat(v):
        return jnp.concatenate([v[b : b + 1, :] for b in range(NX)], axis=1)

    share = flat(jnp.exp2(tile[x, z][0:NX] - best) / added)
    total_log = flat(best * LN2 + jnp.log(added))
    colr[...] = jnp.concatenate([share, total_log, jnp.zeros((126, QS), F32)], axis=0).T.reshape(colr.shape)

    ca, cb = pl.ds(0, CA), pl.ds(CA, CB)

    def part(at, cols):
        return gsum[at + (slice(None), cols)] * colr[at][..., 0:1] - psum[at + (slice(None), cols)] * posw[at][..., 0:1]

    def part_x(b):
        return part((b, slice(None)), ca)

    def part_z(b):
        return part((slice(None), b), cb)

    ga[1] = part_x(at_x(2)).astype(BF16)
    go(remote(ga.at[1], gra.at[1], gx_s.at[1], gx_r.at[1], dev_x(2)))
    for d in z_order[:3]:
        gb[d - 1] = part_z(at_z(d)).astype(BF16)
        go(remote(gb.at[d - 1], grb.at[d - 1], bz_s.at[d - 1], bz_r.at[d - 1], dev_z(d)))
    for d in (1, 3):
        ga[d - 1] = part_x(at_x(d)).astype(BF16)
        go(remote(ga.at[d - 1], gra.at[d - 1], gx_s.at[d - 1], gx_r.at[d - 1], dev_x(d)))
    for d in z_order[3:]:
        gb[d - 1] = part_z(at_z(d)).astype(BF16)
        go(remote(gb.at[d - 1], grb.at[d - 1], bz_s.at[d - 1], bz_r.at[d - 1], dev_z(d)))
    told = tsend[x]
    for d in (1, 3, 2):
        remote(tsend.at[x], trx.at[d - 1], ux_s.at[d - 1], ux_r.at[d - 1], dev_x(d)).wait_recv()
        told = told + trx[d - 1]
    tsum[...] = told
    for d in z_order:
        go(remote(tsum, thz.at[d - 1], uz_s.at[d - 1], uz_r.at[d - 1], dev_z(d)))
    acca[...] = part_x(x)
    accb[...] = part_z(z)
    for d in (1, 3, 2):
        remote(ga.at[d - 1], gra.at[d - 1], gx_s.at[d - 1], gx_r.at[d - 1], dev_x(d)).wait_recv()
        acca[...] += gra[d - 1].astype(F32)
    ha[...] = acca[...].astype(BF16)
    for d in z_order:
        go(remote(ha.at[at_z(d)], hza.at[d - 1], gz_s.at[d - 1], gz_r.at[d - 1], dev_z(d)))
    for d in range(1, NZ):
        remote(gb.at[d - 1], grb.at[d - 1], bz_s.at[d - 1], bz_r.at[d - 1], dev_z(d)).wait_recv()
        accb[...] += grb[d - 1].astype(F32)
    hb[...] = accb[...].astype(BF16)
    for d in (2, 1, 3):
        go(remote(hb.at[at_x(d)], hxb.at[d - 1], bx_s.at[d - 1], bx_r.at[d - 1], dev_x(d)))
    for d in range(1, NZ):
        remote(tsum, thz.at[d - 1], uz_s.at[d - 1], uz_r.at[d - 1], dev_z(d)).wait_recv()
        told = told + thz[d - 1]
    peak[0:128, :] = jnp.concatenate([told, jnp.zeros((120, 128), F32)], axis=0).T
    z_rows = pl.ds(pl.multiple_of(z * ROWS, ROWS), ROWS)
    lfin[p] = jnp.broadcast_to(colr[x, z][:, 1:2] - peak[z_rows, 0:1], (ROWS, 128))
    for d in (4, 3, 5, 2, 6, 1, 7):
        go(remote(lfin.at[p], lfin.at[p], ln_s.at[d - 1], ln_r.at[d - 1], dev_p(at_p(d))))
    grad_b = accb[x]
    for d in (1, 3, 2):
        remote(hb.at[x], hxb.at[d - 1], bx_s.at[d - 1], bx_r.at[d - 1], dev_x(d)).wait_recv()
        grad_b = grad_b + hxb[d - 1].astype(F32)
    grad_a = acca[z]
    for d in range(1, NZ):
        remote(ha.at[z], hza.at[d - 1], gz_s.at[d - 1], gz_r.at[d - 1], dev_z(d)).wait_recv()
        grad_a = grad_a + hza[d - 1].astype(F32)

    earlier = tuple(sends)
    sends.clear()
    fin[p, :, ca] = grad_a.astype(BF16)
    fin[p, :, cb] = grad_b.astype(BF16)
    for d in (4, 3, 5, 2, 6, 1, 7):
        go(remote(fin.at[p], fin.at[p], fn_s.at[d - 1], fn_r.at[d - 1], dev_p(at_p(d))))
    for copy in earlier:
        copy.wait_send()
    for d in range(1, NP):
        src = at_p(NP - d)
        remote(lfin.at[p], lfin.at[src], ln_s.at[d - 1], ln_r.at[d - 1], dev_p(src)).wait_recv()
        remote(fin.at[p], fin.at[src], fn_s.at[d - 1], fn_r.at[d - 1], dev_p(src)).wait_recv()
    for copy in sends:
        copy.wait_send()


def finish(conc, lfin, fin, conc_o, loss_o, grad_o):
    conc_o[...] = conc[...]
    loss_o[...] = lfin[...].reshape(NP * ROWS, 128).T[0:1, :]
    grad_o[...] = fin[...].reshape(NP * ROWS, WIDTH)


def on_device(centroids, queries, positive, members, member_slot, block_count):
    vmem = pltpu.VMEM
    dma = pltpu.SemaphoreType.DMA
    sems = []
    for shape in (
        (NX - 1,), (NX - 1,), (NX, NZ - 1), (NX, NZ - 1), (NZ - 1,), (NX - 1,), (NZ - 1,), (NX - 1,),
        (8,), (9,), (NP - 1,), (NX * NZ,), (NX - 1,), (NZ - 1,), (NP - 1,), (NP - 1,),
        (NX - 1,), (NZ - 1,), (NZ - 1,), (NX - 1,),
    ):
        sems += [dma(shape), dma(shape)]
    whole = pl.BlockSpec(memory_space=vmem)
    conc, lfin, fin = pl.pallas_call(
        kernel,
        out_shape=(
            vmem((1, CENT), F32),
            vmem((NP, ROWS, 128), F32),
            vmem((NP, ROWS, WIDTH), BF16),
        ),
        in_specs=[pl.BlockSpec(memory_space=pl.ANY)] * 6,
        out_specs=(whole,) * 3,
        scratch_shapes=[
            vmem((ROWS, NX * NZ), jnp.int32),
            vmem((NP, NX * NZ), jnp.int32),
            vmem((1, NP * ROWS), jnp.int32),
            vmem((NP, CENT, WIDTH), BF16),
            vmem((NX, NZ, ROWS, WIDTH), BF16),
            vmem((NX, NZ, 1, 128), F32),
            vmem((NX - 1, NZ, ROWS, WIDTH), BF16),
            vmem((NZ, NX, ROWS, WIDTH), BF16),
            vmem((NX - 1, NZ, 1, 128), F32),
            vmem((NZ, NX, 1, 128), F32),
            vmem((NP, 1, CENT), F32),
            vmem((NP, QS, CENT), F32),
            vmem((NP, QS, CENT), BF16),
            vmem((QS, 128), F32),
            vmem((QS, 128), F32),
            vmem((QS, 128), F32),
            vmem((QS, 128), F32),
            vmem((QS, 128), F32),
            vmem((QS, 128), F32),
            vmem((NX, NZ, 8, 128), F32),
            vmem((NX, NZ, ROWS, 128), F32),
            vmem((QS, 128), F32),
            vmem((NX, NZ, ROWS, 128), F32),
            vmem((NX, NZ, ROWS, WIDTH), F32),
            vmem((NX, NZ, ROWS, WIDTH), F32),
            vmem((NZ, NX, 1, 128), F32),
            vmem((1, 128), F32),
            vmem((NX, 8, 128), F32),
            vmem((NX - 1, 8, 128), F32),
            vmem((NZ - 1, 8, 128), F32),
            vmem((8, 128), F32),
            vmem((NX - 1, NZ, ROWS, CA), BF16),
            vmem((NX - 1, NZ, ROWS, CA), BF16),
            vmem((NZ, ROWS, CA), BF16),
            vmem((NZ - 1, ROWS, CA), BF16),
            vmem((NZ, ROWS, CA), F32),
            vmem((NZ - 1, NX, ROWS, CB), BF16),
            vmem((NZ - 1, NX, ROWS, CB), BF16),
            vmem((NX, ROWS, CB), BF16),
            vmem((NX - 1, ROWS, CB), BF16),
            vmem((NX, ROWS, CB), F32),
            dma((6,)),
            *sems,
        ],
        compiler_params=pltpu.CompilerParams(
            collective_id=0, has_side_effects=True, vmem_limit_bytes=56 * 1024 * 1024
        ),
        name="protonce",
    )(
        centroids,
        queries.reshape(NP, ROWS, WIDTH),
        members.reshape(NZ, NX, NP, ROWS, WIDTH),
        member_slot.transpose(0, 2, 3, 1).reshape(NP, ROWS, NX * NZ),
        block_count.transpose(0, 2, 1).reshape(NP, NX * NZ),
        positive.reshape(1, NP * ROWS),
    )
    conc, loss, grad = pl.pallas_call(
        finish,
        out_shape=(
            jax.ShapeDtypeStruct((1, CENT), F32),
            jax.ShapeDtypeStruct((1, NP * ROWS), F32),
            jax.ShapeDtypeStruct((NP * ROWS, WIDTH), BF16),
        ),
        in_specs=[whole] * 3,
        out_specs=(whole,) * 3,
        name="finish",
    )(*(pltpu.with_memory_space_constraint(v, vmem) for v in (conc, lfin, fin)))
    return conc.reshape(CENT), loss.reshape(NP * ROWS), grad


def solution(mesh):
    placed = (
        P(("dp", "proto"), None),
        P("dp", None),
        P("dp"),
        P("dp", None, None, None, None),
        P("dp", None, None, None),
        P("dp", None, None),
    )
    return jax.shard_map(
        on_device,
        mesh=mesh,
        in_specs=placed,
        out_specs=(P(("dp", "proto")), P("dp"), P("dp", None)),
        check_vma=False,
    )
```
